32 devices in a mesh: wide: 8 (over z, y), narrow: 4 (over x, core).
Axes of the slice: x: 2, y: 2, z: 4, core: 2. Of those that a mesh axis runs over, the one named last changes fastest.
Arguments:
- patches: bfloat16 [16384, 768], P('wide'), may hold values from -6 to 6
- norm_gain_attn: float32 [768], replicated, may hold values from 0.5 to 1.5
- norm_gain_mlp: float32 [768], replicated, may hold values from 0.5 to 1.5
- w_query: bfloat16 [768, 768], P('wide', 'narrow'), may hold values from -0.109375 to 0.109375
- w_key: bfloat16 [768, 768], P('wide', 'narrow'), may hold values from -0.109375 to 0.109375
- w_value: bfloat16 [768, 768], P('wide', 'narrow'), may hold values from -0.21875 to 0.21875
- w_out: bfloat16 [768, 768], P('narrow', 'wide'), may hold values from -0.625 to 0.625
- w_gate: bfloat16 [768, 2048], P('wide', 'narrow'), may hold values from -0.21875 to 0.21875
- w_up: bfloat16 [768, 2048], P('wide', 'narrow'), may hold values from -0.21875 to 0.21875
- w_down: bfloat16 [2048, 768], P('narrow', 'wide'), may hold values from -0.125 to 0.125
- cotangent: bfloat16 [16384, 768], P('wide'), may hold values from -6 to 6
- item_slots: int32 [32], P('wide'), may hold values from 512 to 2048, as said below
- valid_counts: int32 [32], P('wide'), may hold values from 1 to 2048, as said below
Outputs:
- output: bfloat16 [16384, 768], P('wide', 'narrow')
- grad_patches: float32 [16384, 768], P('wide', 'narrow')
- grad_gain_attn: float32 [768], replicated
- grad_gain_mlp: float32 [768], replicated
- grad_w_query: float32 [768, 768], P('wide', 'narrow')
- grad_w_key: float32 [768, 768], P('wide', 'narrow')
- grad_w_value: float32 [768, 768], P('wide', 'narrow')
- grad_w_out: float32 [768, 768], P('narrow', 'wide')
- grad_w_gate: float32 [768, 2048], P('wide', 'narrow')
- grad_w_up: float32 [768, 2048], P('wide', 'narrow')
- grad_w_down: float32 [2048, 768], P('narrow', 'wide')
- rms_values: float32 [3], replicated
The draws below stay inside these ranges and needn't reach their ends.
Inputs may be any that keep to these rules, and one draw needn't show every extreme that they name: `item_slots`: each block of 512 slots carries the number of slots of its item: 512, 1024 or 2048. An item of b slots occupies b slots starting at a multiple of b, so no item crosses a multiple of 2048. `valid_counts`: each block carries the valid patch count of its item, the same on all the item's blocks and at most the item's slots; the first that many slots of the item are patches, the rest padding.
All inputs are finite; a program needn't handle non-finite values.
Results may differ from the reference program's by a relative error of at most 0.015.
Values may be sent and summed in bfloat16 or wider, within the bound.
No kernel may reach another device: no remote copies, remote signals or barrier semaphores. Data moves between devices by JAX's collectives and lax.ppermute only.
A program may use at most 128 MiB of HBM per device.

```python
import jax
import jax.numpy as jnp
from jax import lax

D = 768
HEADS = 12
HEAD_DIM = 64
FF = 2048
TOK_DEV = 2048
UNIT = 512
WINDOW = 2048
TOKENS = 16384
N_WIDE = 8


def item_layout(key):
    blocks_dev = TOK_DEV // UNIT
    block_count = N_WIDE * blocks_dev
    window_count = block_count // 4
    patterns = jnp.array([[4, 4, 4, 4], [2, 2, 2, 2], [2, 2, 1, 1], [1, 1, 2, 2], [1, 1, 1, 1]], jnp.int32)
    picked = jax.random.randint(jax.random.fold_in(key, 7), (window_count,), 0, 5)
    picked = picked.at[window_count - 1].set(0)
    unit_counts = patterns[picked].reshape(block_count)
    slot_blocks = unit_counts * UNIT
    block_index = jnp.arange(block_count, dtype=jnp.int32)
    device = block_index // blocks_dev
    percent = 20 + 60 * device // max(N_WIDE - 1, 1)
    low_end = jnp.maximum(1, slot_blocks * percent // 100)
    high_end = slot_blocks * (percent + 20) // 100 + 1
    raw_counts = jax.random.randint(jax.random.fold_in(key, 13), (block_count,), low_end, high_end)
    first_block = block_index // unit_counts * unit_counts
    count_blocks = raw_counts[first_block]
    count_blocks = jnp.where(block_index >= block_count - 4, 4 * UNIT, count_blocks)
    return (slot_blocks, count_blocks)


def draw_item_slots(key, part):
    return item_layout(key)[0]


def draw_valid_counts(key, part):
    return item_layout(key)[1]


def steps_of(rng, dims, shards, least, top_value):
    factor_of, own = 1.0, jax.random.fold_in(rng, 6)
    for axis_at, blocks in shards:
        steps = jnp.exp(jax.random.uniform(jax.random.fold_in(own, axis_at), (blocks,), jnp.float32, least / len(shards), top_value / len(shards)))
        factor_of = factor_of * jnp.repeat(steps, dims[axis_at] // blocks).reshape([-1 if axis == axis_at else 1 for axis in range(len(dims))])
    return factor_of


def centred(key, extent, deviation, most, shards=(), kind=jnp.bfloat16):
    result = jax.random.normal(key, extent, jnp.float32) * deviation
    if len(shards) > 0:
        result = steps_of(key, extent, shards, -0.22, 0.18) * result
    return jnp.clip(result, min=-most, max=most).astype(kind)


def setup_inputs(seed: int = 0) -> dict:
    keys = jax.random.split(jax.random.key(seed), 14)
    patches = centred(keys[0], (TOKENS, D), 1.0, 6.0, ((0, 8),))
    norm_gain_attn = jnp.clip(1.0 + 0.1 * jax.random.normal(keys[1], (D,), jnp.float32), 0.5, 1.5)
    norm_gain_mlp = jnp.clip(1.0 + 0.1 * jax.random.normal(keys[2], (D,), jnp.float32), 0.5, 1.5)
    w_query = centred(keys[3], (D, D), (4 * D) ** -0.5, 0.109375, ((0, 8), (1, 4)))
    w_key = centred(keys[4], (D, D), (4 * D) ** -0.5, 0.109375, ((0, 8), (1, 4)))
    w_value = centred(keys[5], (D, D), D ** -0.5, 0.21875, ((0, 8), (1, 4)))
    w_out = centred(keys[6], (D, D), (D // 8) ** -0.5, 0.625, ((0, 4), (1, 8)))
    w_gate = centred(keys[7], (D, FF), D ** -0.5, 0.21875, ((0, 8), (1, 4)))
    w_up = centred(keys[8], (D, FF), D ** -0.5, 0.21875, ((0, 8), (1, 4)))
    w_down = centred(keys[9], (FF, D), FF ** -0.5, 0.125, ((0, 4), (1, 8)))
    cotangent = centred(keys[10], (TOKENS, D), 1.0, 6.0, ((0, 8),))
    item_slots = draw_item_slots(jax.random.fold_in(keys[13], 71), 0)
    valid_counts = draw_valid_counts(jax.random.fold_in(keys[13], 71), 0)
    return dict(patches=patches, norm_gain_attn=norm_gain_attn, norm_gain_mlp=norm_gain_mlp, w_query=w_query, w_key=w_key, w_value=w_value, w_out=w_out, w_gate=w_gate, w_up=w_up, w_down=w_down, cotangent=cotangent, item_slots=item_slots, valid_counts=valid_counts)


epsilon = 1e-06
masked_score = -1e+30

@jax.custom_vjp
def low(v):
    return lax.optimization_barrier(v.astype(jnp.bfloat16)).astype(jnp.float32)

@jax.custom_vjp
def low_back(v):
    return v

def low_keep(v):
    return (low(v), None)

def low_pass(kept, grad):
    return (grad,)

def back_keep(v):
    return (v, None)

def back_low(kept, grad):
    return (low(grad),)
low.defvjp(low_keep, low_pass)
low_back.defvjp(back_keep, back_low)

def matmul(left, right):
    return jnp.dot(left, right, precision=lax.Precision.HIGHEST, preferred_element_type=jnp.float32)

def rms_norm(values, gain):
    scale = lax.rsqrt(lax.optimization_barrier(jnp.mean(values * values, axis=-1, keepdims=True)) + epsilon)
    return values * scale * gain

def spread_blocks(block_values, block_width):
    return (block_values[:, None] + jnp.zeros((1, block_width), jnp.int32)).reshape(-1)

def token_layout(slot_rows, valid_rows, slot_count):
    block_width = slot_count // slot_rows.shape[0]
    slot_tok = spread_blocks(slot_rows, block_width)
    valid_tok = spread_blocks(valid_rows, block_width)
    position = jnp.arange(slot_count, dtype=jnp.int32)
    item_start = position // slot_tok * slot_tok
    live_mask = position - item_start < valid_tok
    return (item_start, live_mask)

def window_attention(query_win, key_win, value_win, item_win, live_win):
    window_rows = query_win.shape[0]
    query_heads = query_win.reshape(window_rows, HEADS, HEAD_DIM)
    key_heads = key_win.reshape(window_rows, HEADS, HEAD_DIM)
    value_heads = value_win.reshape(window_rows, HEADS, HEAD_DIM)
    scores = jnp.einsum('qhe,khe->hqk', query_heads, key_heads, precision=lax.Precision.HIGHEST)
    scores = low_back(scores)
    allowed = (item_win[:, None] == item_win[None, :]) & live_win[None, :]
    scores = jnp.where(allowed[None, :, :], scores, masked_score)
    probabilities = low(jax.nn.softmax(scores, axis=-1))
    mixed_heads = jnp.einsum('hqk,khe->qhe', probabilities, value_heads, precision=lax.Precision.HIGHEST)
    return mixed_heads.reshape(window_rows, HEADS * HEAD_DIM)

def attend_window(window_items):
    return window_attention(window_items[0], window_items[1], window_items[2], window_items[3], window_items[4])

def block_forward(weights, inputs, item_start, live_mask, keep_mask):
    gain_attn, gain_mlp, query_w, key_w, value_w, out_w, gate_w, up_w, down_w = weights
    slot_count = inputs.shape[0]
    windows = slot_count // WINDOW
    normed = low(rms_norm(inputs, gain_attn))
    queries = low(low_back(matmul(normed, query_w)))
    key_rows = low(low_back(matmul(normed, key_w)))
    value_rows = low(low_back(matmul(normed, value_w)))
    attended = lax.map(jax.checkpoint(attend_window), (queries.reshape(windows, WINDOW, D), key_rows.reshape(windows, WINDOW, D), value_rows.reshape(windows, WINDOW, D), item_start.reshape(windows, WINDOW), live_mask.reshape(windows, WINDOW)))
    heads_out = low(low_back(attended.reshape(slot_count, D)))
    attn_out = low_back(matmul(heads_out, out_w))
    middle = inputs + attn_out
    normed_mid = low(rms_norm(middle, gain_mlp))
    gate_rows = low_back(matmul(normed_mid, gate_w))
    up_rows = low_back(matmul(normed_mid, up_w))
    hidden = low(jax.nn.gelu(gate_rows, approximate=True) * up_rows)
    mlp_out = low_back(matmul(hidden, down_w))
    layer_out = keep_mask[:, None] * (middle + mlp_out)
    return (layer_out, (attn_out, mlp_out))

def reference(patches, norm_gain_attn, norm_gain_mlp, w_query, w_key, w_value, w_out, w_gate, w_up, w_down, cotangent, item_slots, valid_counts):
    params = tuple((weight.astype(jnp.float32) for weight in (norm_gain_attn, norm_gain_mlp, w_query, w_key, w_value, w_out, w_gate, w_up, w_down)))
    input_groups = patches.astype(jnp.float32).reshape(N_WIDE, TOK_DEV, D)
    cot_groups = cotangent.astype(jnp.float32).reshape(N_WIDE, TOK_DEV, D)
    slot_groups = item_slots.reshape(N_WIDE, TOK_DEV // UNIT)
    valid_groups = valid_counts.reshape(N_WIDE, TOK_DEV // UNIT)

    def one_group(running, group_items):
        grad_sums, stat_sums = running
        input_block, cot_block, slot_block, valid_block = group_items
        item_start, live_mask = token_layout(slot_block, valid_block, TOK_DEV)
        keep_mask = live_mask.astype(jnp.float32)

        def forward(weights, inputs):
            return block_forward(weights, inputs, item_start, live_mask, keep_mask)
        layer_out, pullback, branches = jax.vjp(forward, params, input_block, has_aux=True)
        grad_params, grad_inputs = pullback(cot_block)
        attn_out, mlp_out = branches
        stat_terms = jnp.stack([jnp.sum(keep_mask[:, None] * attn_out * attn_out), jnp.sum(keep_mask[:, None] * mlp_out * mlp_out), jnp.sum(layer_out * layer_out), jnp.sum(keep_mask)])
        grad_sums = jax.tree.map(jnp.add, grad_sums, grad_params)
        return ((grad_sums, stat_sums + stat_terms), (layer_out.astype(jnp.bfloat16), grad_inputs))
    start_grads = jax.tree.map(jnp.zeros_like, params)
    (grad_sums, stat_sums), (outputs, grad_inputs) = lax.scan(one_group, (start_grads, jnp.zeros((4,), jnp.float32)), (input_groups, cot_groups, slot_groups, valid_groups))
    rms_values = jnp.sqrt(stat_sums[:3] / (stat_sums[3] * D))
    return (outputs.reshape(TOKENS, D), grad_inputs.reshape(TOKENS, D), grad_sums[0], grad_sums[1], grad_sums[2], grad_sums[3], grad_sums[4], grad_sums[5], grad_sums[6], grad_sums[7], grad_sums[8], rms_values)
```

```python
import functools

import jax
import jax.numpy as jnp
from jax import lax
from jax.experimental import pallas as pl
from jax.experimental.pallas import tpu as pltpu
from jax.sharding import PartitionSpec as P

f32 = jnp.float32
bf16 = jnp.bfloat16
HEAD_DIM = 64
UNIT = 512
WINDOW = 2048
LANES = 128
epsilon = 1e-06
BIG = 1e30
GELU_C = 0.7978845608028654
GELU_A = 0.044715
VMEM_LIMIT = 56 << 20

NT = (((1,), (1,)), ((), ()))
NN = (((1,), (0,)), ((), ()))


def mm(a, b, dims=NN):
    return lax.dot_general(a, b, dims, preferred_element_type=f32)


def split3(v):
    high = v.astype(bf16)
    rest = v - high.astype(f32)
    middle = rest.astype(bf16)
    low = (rest - middle.astype(f32)).astype(bf16)
    return high.astype(f32), middle.astype(f32), low.astype(f32)


def lane_halves():
    lane = lax.broadcasted_iota(jnp.int32, (1, LANES), 1)
    first = (lane < HEAD_DIM).astype(f32)
    return lane, first.astype(bf16), (1.0 - first).astype(bf16)


def load_blocks(table, sources, target, wide_index, rows, sem):
    copies = []
    for k, (src, lead, half, offset) in enumerate(table):
        start = pl.multiple_of((wide_index ^ offset) * rows, 8 if rows % 16 else 16)
        copies.append(
            pltpu.make_async_copy(
                sources[src].at[lead], target.at[half, pl.ds(start, rows), :], sem.at[k]
            )
        )
    for copy in copies:
        copy.start()
    for copy in copies:
        copy.wait()


def store_blocks(table, acc, targets, wide_index, rows):
    for src, lead, half, offset in table:
        start = pl.multiple_of((wide_index ^ offset) * rows, 8)
        targets[src][lead] = acc[half, pl.ds(start, rows), :].astype(bf16)


def lane_join(buf, first, width):
    return jnp.concatenate(
        [buf[0, :, first : first + width], buf[1, :, first : first + width]], axis=1
    )


def proj_kernel(table, n_src, rows, share, s_ref, x_ref, gain_ref, *refs):
    sources = refs[:n_src]
    q_ref, k_ref, v_ref, buf, wq, wk, wv, sem = refs[n_src:]
    i = pl.program_id(0)

    @pl.when(i == 0)
    def _():
        load_blocks(table, sources, buf, s_ref[1], rows, sem)
        wq[...] = lane_join(buf, 0, share)
        wk[...] = lane_join(buf, share, share)
        wv[...] = lane_join(buf, 2 * share, share)

    x = x_ref[...].astype(f32)
    scale = lax.rsqrt(jnp.mean(x * x, axis=1, keepdims=True) + epsilon)
    normed = (x * scale * gain_ref[...]).astype(bf16)
    k_ref[...] = mm(normed, wk[...]).astype(bf16)
    v_ref[...] = mm(normed, wv[...]).astype(bf16)
    half = pl.num_programs(0) // 2

    @pl.when(i // half == s_ref[0])
    def _():
        q_ref[...] = mm(normed, wq[...]).astype(bf16)


def own_tile(i, s, half):
    return jnp.clip(i - s[0] * half, 0, half - 1)


def project(scalars, patches, gain, table, sources, rows, share, tile=512):
    n, d = patches.shape
    width = sources[0].shape[-1]
    steps = n // tile
    half = steps // 2
    any_spec = pl.BlockSpec(memory_space=pl.ANY)
    return pl.pallas_call(
        functools.partial(proj_kernel, table, len(sources), rows, share),
        out_shape=(
            jax.ShapeDtypeStruct((n // 2, 2 * share), bf16),
            jax.ShapeDtypeStruct((n, 2 * share), bf16),
            jax.ShapeDtypeStruct((n, 2 * share), bf16),
        ),
        grid_spec=pltpu.PrefetchScalarGridSpec(
            num_scalar_prefetch=1,
            grid=(steps,),
            in_specs=[
                pl.BlockSpec((tile, d), lambda i, s: (i, 0)),
                pl.BlockSpec((1, d), lambda i, s: (0, 0)),
            ]
            + [any_spec] * len(sources),
            out_specs=[
                pl.BlockSpec((tile, 2 * share), lambda i, s: (own_tile(i, s, half), 0)),
                pl.BlockSpec((tile, 2 * share), lambda i, s: (i, 0)),
                pl.BlockSpec((tile, 2 * share), lambda i, s: (i, 0)),
            ],
            scratch_shapes=[pltpu.VMEM((2, d, width), bf16)]
            + [pltpu.VMEM((d, 2 * share), bf16)] * 3
            + [pltpu.SemaphoreType.DMA((len(table),))],
        ),
        compiler_params=pltpu.CompilerParams(vmem_limit_bytes=VMEM_LIMIT),
        cost_estimate=pl.CostEstimate(
            flops=2 * n * d * 5 * share, bytes_accessed=4 * n * d, transcendentals=0
        ),
        name="project",
    )(scalars, patches, gain, *sources)


def attend_kernel(table, n_src, rows, share, chunk, s_ref, q_ref, k_ref, v_ref, qf_ref, kf_ref, *refs):
    sources = refs[:n_src]
    o_ref, qfo_ref, part_ref, k_a, k_b, v_a, v_b, buf, wo, acc, sem = refs[n_src:]
    lane, first, second = lane_halves()
    pair, i = pl.program_id(0), pl.program_id(1)

    @pl.when((pair == 0) & (i == 0))
    def _():
        load_blocks(table, sources, buf, s_ref[1], rows, sem)
        joined = lane_join(buf, 3 * share, share)
        for p in range(wo.shape[0]):
            wo[p] = joined[:, p * LANES : (p + 1) * LANES]

    @pl.when(i == 0)
    def _():
        k, v, kf = k_ref[...], v_ref[...], kf_ref[...]
        k_a[...] = k * first + kf * second
        k_b[...] = k * second + kf * first
        v_a[...] = v * first + (lane == HEAD_DIM).astype(f32).astype(bf16)
        v_b[...] = v * second + (lane == 0).astype(f32).astype(bf16)

    q, qf = q_ref[...], qf_ref[...]
    keys = k_a.shape[0]
    results = []
    for kk, vv, own, other, column in ((k_a, v_a, first, second, HEAD_DIM), (k_b, v_b, second, first, 0)):
        query = q * own + qf * other
        scores = [mm(query, kk[c : c + chunk, :], NT) for c in range(0, keys, chunk)]
        top = functools.reduce(jnp.maximum, [jnp.max(s, axis=1, keepdims=True) for s in scores])
        mixed = None
        for at, s in enumerate(scores):
            part = mm(jnp.exp(s - top).astype(bf16), vv[at * chunk : (at + 1) * chunk, :])
            mixed = part if mixed is None else mixed + part
        total = mixed[:, column : column + 1]
        results.append((mixed / total, top + jnp.log(total)))
    (out_a, lse_a), (out_b, lse_b) = results
    out = jnp.where(lane < HEAD_DIM, out_a, out_b).astype(bf16)
    o_ref[...] = out
    features = qf.astype(f32)
    for at, value in zip((69, 70, 71, 5, 6, 7), split3(lse_a) + split3(lse_b)):
        features = jnp.where(lane == at, value, features)
    qfo_ref[...] = features.astype(bf16)
    part = mm(out, wo[pair], NT)
    tile = q.shape[0]
    here = pl.ds(pl.multiple_of(i * tile, tile), tile)

    @pl.when(pair == 0)
    def _():
        acc[here, :] = part

    @pl.when(pair > 0)
    def _():
        acc[here, :] += part

    part_ref[...] = acc[here, :].astype(bf16)


def attend(scalars, q, k, v, qf, kf, table, sources, rows, share, tile=256, chunk=512):
    n, width = q.shape
    keys = k.shape[0]
    pairs = width // LANES
    steps = n // tile
    d = rows * (len(table) // 2)
    any_spec = pl.BlockSpec(memory_space=pl.ANY)
    row_spec = pl.BlockSpec((tile, LANES), lambda p, i, s: (i, p))
    key_spec = pl.BlockSpec((keys, LANES), lambda p, i, s: (0, p))
    return pl.pallas_call(
        functools.partial(attend_kernel, table, len(sources), rows, share, chunk),
        out_shape=(
            jax.ShapeDtypeStruct((n, width), bf16),
            jax.ShapeDtypeStruct((n, width), bf16),
            jax.ShapeDtypeStruct((n, d), bf16),
        ),
        grid_spec=pltpu.PrefetchScalarGridSpec(
            num_scalar_prefetch=1,
            grid=(pairs, steps),
            in_specs=[
                row_spec,
                key_spec,
                key_spec,
                pl.BlockSpec((tile, LANES), lambda p, i, s: (s[0] * steps + i, 0)),
                pl.BlockSpec((keys, LANES), lambda p, i, s: (0, 0)),
            ]
            + [any_spec] * len(sources),
            out_specs=[
                row_spec,
                row_spec,
                pl.BlockSpec((tile, d), lambda p, i, s: (jnp.where(p == pairs - 1, i, 0), 0)),
            ],
            scratch_shapes=[pltpu.VMEM((keys, LANES), bf16)] * 4
            + [
                pltpu.VMEM((2, d, sources[0].shape[-1]), bf16),
                pltpu.VMEM((pairs, d, LANES), bf16),
                pltpu.VMEM((n, d), f32),
                pltpu.SemaphoreType.DMA((len(table),)),
            ],
        ),
        compiler_params=pltpu.CompilerParams(vmem_limit_bytes=VMEM_LIMIT),
        cost_estimate=pl.CostEstimate(
            flops=4 * n * keys * width * 4, bytes_accessed=8 * n * d, transcendentals=n * keys
        ),
        name="attend",
    )(scalars, q, k, v, qf, kf, *sources)


def mid_norm(x_ref, a_ref, b_ref):
    attn = a_ref[...].astype(f32) + b_ref[...].astype(f32)
    middle = x_ref[...].astype(f32) + attn
    scale = lax.rsqrt(jnp.mean(middle * middle, axis=1, keepdims=True) + epsilon)
    return attn, middle, scale


def feed_kernel(
    table, n_src, rows, out_table, n_out, ff, s_ref, x_ref, a_ref, b_ref, cot_ref, kf_ref, gain_ref, *refs
):
    sources = refs[:n_src]
    mlp_ref, mid_ref, gnm_ref, stat_ref = refs[n_src : n_src + 4]
    targets = refs[n_src + 4 : n_src + 4 + n_out]
    buf, acc, stat, sem = refs[n_src + 4 + n_out :]
    i = pl.program_id(0)
    d = x_ref.shape[1]
    quarter = d // 4

    @pl.when(i == 0)
    def _():
        load_blocks(table, sources, buf, s_ref[1], rows, sem)
        acc[...] = jnp.zeros_like(acc)
        stat[...] = jnp.zeros_like(stat)

    attn, middle, scale = mid_norm(x_ref, a_ref, b_ref)
    live = kf_ref[:, 4:5].astype(f32) >= 0.0
    stat[...] += jnp.sum(jnp.where(live, attn * attn, 0.0), axis=0, keepdims=True)
    normed = (middle * scale * gain_ref[...]).astype(bf16)
    grad = jnp.where(live, cot_ref[...].astype(f32), 0.0).astype(bf16)
    normed_t = normed.T
    grad_t = grad.T
    mid_t = middle.T
    back = None
    hiddens = []
    for half in range(2):
        w_gate = buf[half, :, 0:ff]
        w_up = buf[half, :, ff : 2 * ff]
        w_down = buf[half, :, 2 * ff : 3 * ff]
        gate = mm(normed, w_gate)
        up = mm(normed, w_up)
        back_hidden = mm(grad, w_down)
        square = gate * gate
        angle = jnp.tanh(GELU_C * gate * (1.0 + GELU_A * square))
        cdf = 0.5 * (1.0 + angle)
        act = gate * cdf
        slope = cdf + 0.5 * gate * (1.0 - angle * angle) * (GELU_C * (1.0 + 3.0 * GELU_A * square))
        hidden = (act * up).astype(bf16)
        grad_gate = (back_hidden * up * slope).astype(bf16)
        grad_up = (back_hidden * act).astype(bf16)
        acc[half, :, 0:ff] += mm(normed_t, grad_gate)
        acc[half, :, ff : 2 * ff] += mm(normed_t, grad_up)
        acc[half, :, 2 * ff : 3 * ff] += mm(grad_t, hidden)
        part = mm(grad_gate, w_gate, NT) + mm(grad_up, w_up, NT)
        back = part if back is None else back + part
        hiddens.append(hidden)
    gnm_ref[...] = back.astype(bf16)
    here = s_ref[2]
    for at, offset in enumerate((0, 2, 1, 3)):
        start = pl.ds(pl.multiple_of((here ^ offset) * quarter, 16), quarter)
        out = mm(buf[0, start, 2 * ff : 3 * ff], hiddens[0], NT) + mm(
            buf[1, start, 2 * ff : 3 * ff], hiddens[1], NT
        )
        mlp_ref[at * quarter : (at + 1) * quarter, :] = out.astype(bf16)
    mid_ref[...] = mid_t

    @pl.when(i == pl.num_programs(0) - 1)
    def _():
        stat_ref[...] = stat[...]
        store_blocks(out_table, acc, targets, s_ref[1], rows)


def feed_forward(scalars, patches, a, b, cot, kf, gain, table, sources, rows, out_table, out_leads, tile=256):
    n, d = a.shape
    width = sources[0].shape[-1]
    ff = width // 3
    steps = n // tile
    any_spec = pl.BlockSpec(memory_space=pl.ANY)
    own_spec = pl.BlockSpec((tile, d), lambda i, s: (s[0] * steps + i, 0))
    row_spec = pl.BlockSpec((tile, d), lambda i, s: (i, 0))
    return pl.pallas_call(
        functools.partial(feed_kernel, table, len(sources), rows, out_table, len(out_leads), ff),
        out_shape=(
            jax.ShapeDtypeStruct((d, n), bf16),
            jax.ShapeDtypeStruct((d, n), f32),
            jax.ShapeDtypeStruct((n, d), bf16),
            jax.ShapeDtypeStruct((1, d), f32),
        )
        + tuple(jax.ShapeDtypeStruct((lead, rows, width), bf16) for lead in out_leads),
        grid_spec=pltpu.PrefetchScalarGridSpec(
            num_scalar_prefetch=1,
            grid=(steps,),
            in_specs=[
                own_spec,
                row_spec,
                row_spec,
                own_spec,
                pl.BlockSpec((tile, LANES), lambda i, s: (s[0] * steps + i, 0)),
                pl.BlockSpec((1, d), lambda i, s: (0, 0)),
            ]
            + [any_spec] * len(sources),
            out_specs=[
                pl.BlockSpec((d, tile), lambda i, s: (0, i)),
                pl.BlockSpec((d, tile), lambda i, s: (0, i)),
                row_spec,
                pl.BlockSpec((1, d), lambda i, s: (0, 0)),
            ]
            + [
                pl.BlockSpec((lead, rows, width), lambda i, s: (0, 0, 0), pipeline_mode=pl.Buffered(1))
                for lead in out_leads
            ],
            scratch_shapes=[
                pltpu.VMEM((2, d, width), bf16),
                pltpu.VMEM((2, d, width), f32),
                pltpu.VMEM((1, d), f32),
                pltpu.SemaphoreType.DMA((len(table),)),
            ],
        ),
        compiler_params=pltpu.CompilerParams(vmem_limit_bytes=VMEM_LIMIT),
        cost_estimate=pl.CostEstimate(
            flops=2 * n * d * width * 6, bytes_accessed=10 * n * d, transcendentals=n * ff
        ),
        name="feed_forward",
    )(scalars, patches, a, b, cot, kf, gain, *sources)


def mid_kernel(
    table, n_src, rows, share, s_ref, x_ref, a_ref, b_ref, g_ref, h_ref, cot_ref, kf_ref, gain_ref, o_ref, *refs
):
    sources = refs[:n_src]
    gm_ref, do_ref, dwo_ref, gain_out, buf, wo, acc, total, sem = refs[n_src:]
    i = pl.program_id(0)

    @pl.when(i == 0)
    def _():
        load_blocks(table, sources, buf, s_ref[1], rows, sem)
        wo[...] = lane_join(buf, 3 * share, share)
        acc[...] = jnp.zeros_like(acc)
        total[...] = jnp.zeros_like(total)

    _, middle, scale = mid_norm(x_ref, a_ref, b_ref)
    hat = middle * scale
    back = g_ref[...].astype(f32) + h_ref[...].astype(f32)
    live = kf_ref[:, 4:5].astype(f32) >= 0.0
    cot = jnp.where(live, cot_ref[...].astype(f32), 0.0)
    total[...] += jnp.sum(back * hat, axis=0, keepdims=True)
    scaled = back * gain_ref[...]
    mean = jnp.mean(scaled * hat, axis=1, keepdims=True)
    grad_mid = cot + scale * (scaled - hat * mean)
    gm_ref[...] = grad_mid
    grad = grad_mid.astype(bf16)
    do_ref[...] = mm(grad, wo[...]).astype(bf16)
    acc[...] += mm(grad.T, o_ref[...])

    @pl.when(i == pl.num_programs(0) - 1)
    def _():
        gain_out[...] = total[...]
        dwo_ref[...] = acc[...]


def mid_backward(scalars, patches, a, b, g, h, cot, kf, gain, o, table, sources, rows, share, tile=256):
    n, d = a.shape
    steps = n // tile
    any_spec = pl.BlockSpec(memory_space=pl.ANY)
    own_spec = pl.BlockSpec((tile, d), lambda i, s: (s[0] * steps + i, 0))
    row_spec = pl.BlockSpec((tile, d), lambda i, s: (i, 0))
    head_spec = pl.BlockSpec((tile, 2 * share), lambda i, s: (i, 0))
    one_spec = pl.BlockSpec((1, d), lambda i, s: (0, 0))
    return pl.pallas_call(
        functools.partial(mid_kernel, table, len(sources), rows, share),
        out_shape=(
            jax.ShapeDtypeStruct((n, d), f32),
            jax.ShapeDtypeStruct((n, 2 * share), bf16),
            jax.ShapeDtypeStruct((d, 2 * share), f32),
            jax.ShapeDtypeStruct((1, d), f32),
        ),
        grid_spec=pltpu.PrefetchScalarGridSpec(
            num_scalar_prefetch=1,
            grid=(steps,),
            in_specs=[own_spec, row_spec, row_spec, row_spec, row_spec, own_spec]
            + [pl.BlockSpec((tile, LANES), lambda i, s: (s[0] * steps + i, 0)), one_spec, head_spec]
            + [any_spec] * len(sources),
            out_specs=[
                row_spec,
                head_spec,
                pl.BlockSpec((d, 2 * share), lambda i, s: (0, 0)),
                one_spec,
            ],
            scratch_shapes=[
                pltpu.VMEM((2, d, sources[0].shape[-1]), bf16),
                pltpu.VMEM((d, 2 * share), bf16),
                pltpu.VMEM((d, 2 * share), f32),
                pltpu.VMEM((1, d), f32),
                pltpu.SemaphoreType.DMA((len(table),)),
            ],
        ),
        compiler_params=pltpu.CompilerParams(vmem_limit_bytes=VMEM_LIMIT),
        cost_estimate=pl.CostEstimate(
            flops=8 * n * d * share, bytes_accessed=16 * n * d, transcendentals=0
        ),
        name="mid_backward",
    )(scalars, patches, a, b, g, h, cot, kf, gain, o, *sources)


def attend_back_kernel(
    chunk, q_ref, k_ref, v_ref, qf_ref, kf_ref, o_ref, do_ref, dq_ref, dk_ref, dv_ref, k_a, k_b, v_a, v_b, k_t, dk_acc, dv_acc
):
    lane, first, second = lane_halves()
    i = pl.program_id(1)

    @pl.when(i == 0)
    def _():
        k, v, kf = k_ref[...], v_ref[...], kf_ref[...]
        k_a[...] = k * first + kf * second
        k_b[...] = k * second + kf * first
        v_a[...] = v * first - ((lane >= 64) & (lane < 67)).astype(f32).astype(bf16)
        v_b[...] = v * second - (lane < 3).astype(f32).astype(bf16)
        k_t[...] = k.T
        dk_acc[...] = jnp.zeros_like(dk_acc)
        dv_acc[...] = jnp.zeros_like(dv_acc)

    q, qf, do = q_ref[...], qf_ref[...], do_ref[...]
    product = do.astype(f32) * o_ref[...].astype(f32)
    in_first = lane < HEAD_DIM
    sum_a = jnp.sum(jnp.where(in_first, product, 0.0), axis=1, keepdims=True)
    sum_b = jnp.sum(jnp.where(in_first, 0.0, product), axis=1, keepdims=True)
    features = jnp.zeros(q.shape, f32)
    for at, value in zip((64, 65, 66, 0, 1, 2), split3(sum_a) + split3(sum_b)):
        features = jnp.where(lane == at, value, features)
    features = features.astype(bf16)
    q_first, q_second, do_first, do_second = q * first, q * second, do * first, do * second
    queries = (q_first + qf * second, q_second + qf * first)
    grads = (do_first + features * second, do_second + features * first)
    q_both = jnp.concatenate([q_first, q_second], axis=0)
    do_both = jnp.concatenate([do_first, do_second], axis=0)
    keys = k_a.shape[0]
    dq = [None, None]
    for c in range(0, keys, chunk):
        probs, backs = [], []
        for head, (kk, vv) in enumerate(((k_a, v_a), (k_b, v_b))):
            p = jnp.exp(mm(kk[c : c + chunk, :], queries[head], NT))
            back = (p * mm(vv[c : c + chunk, :], grads[head], NT)).astype(bf16)
            probs.append(p.astype(bf16))
            backs.append(back)
            part = mm(k_t[head * HEAD_DIM : (head + 1) * HEAD_DIM, c : c + chunk], back)
            dq[head] = part if dq[head] is None else dq[head] + part
        dv_acc[c : c + chunk, :] += mm(jnp.concatenate(probs, axis=1), do_both)
        dk_acc[c : c + chunk, :] += mm(jnp.concatenate(backs, axis=1), q_both)
    dq_ref[...] = jnp.concatenate(dq, axis=0).T.astype(bf16)

    @pl.when(i == pl.num_programs(1) - 1)
    def _():
        dk_ref[...] = dk_acc[...].astype(bf16)
        dv_ref[...] = dv_acc[...].astype(bf16)


def attend_back(q, k, v, qf, kf, o, do, tile=512, chunk=512):
    n, width = q.shape
    keys = k.shape[0]
    row_spec = pl.BlockSpec((tile, LANES), lambda p, i: (i, p))
    key_spec = pl.BlockSpec((keys, LANES), lambda p, i: (0, p))
    return pl.pallas_call(
        functools.partial(attend_back_kernel, chunk),
        out_shape=(
            jax.ShapeDtypeStruct((n, width), bf16),
            jax.ShapeDtypeStruct((keys, width), bf16),
            jax.ShapeDtypeStruct((keys, width), bf16),
        ),
        grid=(width // LANES, n // tile),
        in_specs=[
            row_spec,
            key_spec,
            key_spec,
            row_spec,
            pl.BlockSpec((keys, LANES), lambda p, i: (0, 0)),
            row_spec,
            row_spec,
        ],
        out_specs=[row_spec, key_spec, key_spec],
        scratch_shapes=[pltpu.VMEM((keys, LANES), bf16)] * 4
        + [pltpu.VMEM((LANES, keys), bf16)]
        + [pltpu.VMEM((keys, LANES), f32)] * 2,
        compiler_params=pltpu.CompilerParams(vmem_limit_bytes=VMEM_LIMIT),
        cost_estimate=pl.CostEstimate(
            flops=10 * n * keys * width * 4, bytes_accessed=8 * keys * width, transcendentals=n * keys
        ),
        name="attend_back",
    )(q, k, v, qf, kf, o, do)


def last_kernel(
    table, n_src, rows, out_table, n_out, share, s_ref, x_ref, gain_ref, dq_ref, dk_ref, dv_ref, gm_ref, dwo_ref, *refs
):
    sources = refs[:n_src]
    gp_ref, gain_out = refs[n_src : n_src + 2]
    targets = refs[n_src + 2 : n_src + 2 + n_out]
    buf, wq, wk, wv, dwq, dwk, dwv, pack, total, sem = refs[n_src + 2 + n_out :]
    i = pl.program_id(0)
    half = pl.num_programs(0) // 2
    d = x_ref.shape[1]
    quarter = d // 4

    @pl.when(i == 0)
    def _():
        load_blocks(table, sources, buf, s_ref[1], rows, sem)
        wq[...] = lane_join(buf, 0, share)
        wk[...] = lane_join(buf, share, share)
        wv[...] = lane_join(buf, 2 * share, share)
        for ref in (dwq, dwk, dwv, total):
            ref[...] = jnp.zeros_like(ref)

    mine = i // half == s_ref[0]
    x = x_ref[...].astype(f32)
    scale = lax.rsqrt(jnp.mean(x * x, axis=1, keepdims=True) + epsilon)
    hat = x * scale
    normed_t = (hat * gain_ref[...]).astype(bf16).T
    dk, dv = dk_ref[...], dv_ref[...]
    dq = jnp.where(mine, dq_ref[...].astype(f32), 0.0).astype(bf16)
    dwk[...] += mm(normed_t, dk)
    dwv[...] += mm(normed_t, dv)
    dwq[...] += mm(normed_t, dq)
    back = mm(dk, wk[...], NT) + mm(dv, wv[...], NT) + mm(dq, wq[...], NT)
    total[...] += jnp.sum(back * hat, axis=0, keepdims=True)
    scaled = back * gain_ref[...]
    mean = jnp.mean(scaled * hat, axis=1, keepdims=True)
    grad = scale * (scaled - hat * mean) + jnp.where(mine, 0.5, 0.0) * gm_ref[...]
    grad_t = grad.T
    here = s_ref[2]
    buf_t = grad_t.astype(bf16)
    for block in range(4):
        at = here ^ block
        slot = jnp.where(at == 0, 0, jnp.where(at == 2, 1, jnp.where(at == 1, 2, 3)))
        gp_ref[pl.ds(pl.multiple_of(slot * quarter, 16), quarter), :] = buf_t[
            block * quarter : (block + 1) * quarter, :
        ]

    @pl.when(i == pl.num_programs(0) - 1)
    def _():
        gain_out[...] = total[...]
        for h in range(2):
            lanes = slice(h * share, (h + 1) * share)
            for at, ref in enumerate((dwq, dwk, dwv, dwo_ref)):
                pack[h, :, at * share : (at + 1) * share] = ref[:, lanes]
        store_blocks(out_table, pack, targets, s_ref[1], rows)


def last_backward(
    scalars, patches, gain, dq, dk, dv, gm, dwo, table, sources, rows, out_table, out_leads, share, tile=512
):
    n, d = patches.shape
    width = sources[0].shape[-1]
    steps = n // tile
    half = steps // 2
    any_spec = pl.BlockSpec(memory_space=pl.ANY)
    key_spec = pl.BlockSpec((tile, 2 * share), lambda i, s: (i, 0))
    one_spec = pl.BlockSpec((1, d), lambda i, s: (0, 0))
    return pl.pallas_call(
        functools.partial(last_kernel, table, len(sources), rows, out_table, len(out_leads), share),
        out_shape=(
            jax.ShapeDtypeStruct((d, n), bf16),
            jax.ShapeDtypeStruct((1, d), f32),
        )
        + tuple(jax.ShapeDtypeStruct((lead, rows, width), bf16) for lead in out_leads),
        grid_spec=pltpu.PrefetchScalarGridSpec(
            num_scalar_prefetch=1,
            grid=(steps,),
            in_specs=[
                pl.BlockSpec((tile, d), lambda i, s: (i, 0)),
                one_spec,
                pl.BlockSpec((tile, 2 * share), lambda i, s: (own_tile(i, s, half), 0)),
                key_spec,
                key_spec,
                pl.BlockSpec((tile, d), lambda i, s: (own_tile(i, s, half), 0)),
                pl.BlockSpec((d, 2 * share), lambda i, s: (0, 0)),
            ]
            + [any_spec] * len(sources),
            out_specs=[pl.BlockSpec((d, tile), lambda i, s: (0, i)), one_spec]
            + [
                pl.BlockSpec((lead, rows, width), lambda i, s: (0, 0, 0), pipeline_mode=pl.Buffered(1))
                for lead in out_leads
            ],
            scratch_shapes=[pltpu.VMEM((2, d, width), bf16)]
            + [pltpu.VMEM((d, 2 * share), bf16)] * 3
            + [pltpu.VMEM((d, 2 * share), f32)] * 3
            + [
                pltpu.VMEM((2, d, width), f32),
                pltpu.VMEM((1, d), f32),
                pltpu.SemaphoreType.DMA((len(table),)),
            ],
        ),
        compiler_params=pltpu.CompilerParams(vmem_limit_bytes=VMEM_LIMIT),
        cost_estimate=pl.CostEstimate(
            flops=2 * n * d * share * 10, bytes_accessed=10 * n * d, transcendentals=0
        ),
        name="last_backward",
    )(scalars, patches, gain, dq, dk, dv, gm, dwo, *sources)


def swap_core(value):
    return lax.ppermute(value, "narrow", [(i, i ^ 1) for i in range(4)])


def swap_x(value):
    return lax.ppermute(value, "narrow", [(i, i ^ 2) for i in range(4)])


def swap_wide(value, offset):
    n = lax.axis_size("wide")
    return lax.ppermute(value, "wide", [(i, i ^ offset) for i in range(n)])


GATHER_TABLE = (
    [(0, z, 0, 2 * z) for z in range(4)]
    + [(1, z, 0, 2 * z + 1) for z in range(4)]
    + [(2, z, 1, 2 * z) for z in range(4)]
    + [(3, z, 1, 2 * z + 1) for z in range(2)]
    + [(4, z, 1, 2 * z + 5) for z in range(2)]
)
REDUCE_TABLE = GATHER_TABLE
REDUCE_LEADS = (4, 4, 4, 2, 2)
WHOLE_TABLE = [(0, 0, 0, 0), (0, 1, 1, 0)]


def gather_shards(shard):
    if lax.axis_size("wide") != 8:
        full = lax.all_gather(shard, "wide", axis=0, tiled=True)
        return WHOLE_TABLE, [jnp.stack([full, swap_x(full)])], full.shape[0]
    column = jnp.stack([shard] + [swap_wide(shard, 2 * z) for z in (1, 2, 3)])
    from_y = swap_wide(column, 1)
    from_x = swap_x(column)
    corner_x = swap_x(from_y[:2])
    corner_y = swap_wide(from_x[2:], 1)
    return GATHER_TABLE, [column, from_y, from_x, corner_x, corner_y], shard.shape[0]


def reduce_tables():
    if lax.axis_size("wide") != 8:
        return WHOLE_TABLE, (2,)
    return REDUCE_TABLE, REDUCE_LEADS


def total(*terms):
    return functools.reduce(jnp.add, [t.astype(f32) for t in terms])


def reduce_shards(parts):
    if lax.axis_size("wide") != 8:
        both = total(parts[0][0], swap_x(parts[0][1])).astype(bf16)
        return lax.psum_scatter(both, "wide", scatter_dimension=0, tiled=True).astype(f32)
    column, to_y, to_x, corner_x, corner_y = parts
    got_x = swap_x(corner_x)
    got_y = swap_wide(corner_y, 1)
    to_y = jnp.concatenate([total(to_y[:2], got_x).astype(bf16), to_y[2:]])
    to_x = jnp.concatenate([to_x[:2], total(to_x[2:], got_y).astype(bf16)])
    column = total(column, swap_wide(to_y, 1), swap_x(to_x))
    sent = column[1:].astype(bf16)
    return total(column[0], *[swap_wide(sent[z - 1], 2 * z) for z in (1, 2, 3)])


def sum_all(value):
    if lax.axis_size("wide") != 8:
        return lax.psum(value, ("wide", "narrow"))
    value = value + swap_core(value)
    value = value + swap_x(value)
    for offset in (1, 2, 4):
        value = value + swap_wide(value, offset)
    return value


def mask_features(item_slots, valid_counts, rows):
    def spread(values):
        return jnp.repeat(values, rows // values.shape[0], total_repeat_length=rows)

    position = jnp.arange(rows, dtype=jnp.int32)
    start = position // spread(item_slots) * spread(item_slots)
    live = position - start < spread(valid_counts)
    unit = start // UNIT
    lane = jnp.arange(LANES, dtype=jnp.int32)[None, :] % HEAD_DIM
    same = unit[:, None] == lane
    query = jnp.where(lane < 4, jnp.where(same, 0.0, 1.0), jnp.where(lane == 4, 1.0, 0.0))
    key = jnp.where(lane < 4, jnp.where(same, -BIG, 0.0), 0.0)
    key = jnp.where(lane == 4, jnp.where(live[:, None], 0.0, -BIG), key)
    key = jnp.where((lane >= 5) & (lane < 8), -1.0, key)
    return query.astype(bf16), key.astype(bf16), live


def body(
    patches,
    norm_gain_attn,
    norm_gain_mlp,
    w_query,
    w_key,
    w_value,
    w_out,
    w_gate,
    w_up,
    w_down,
    cotangent,
    item_slots,
    valid_counts,
):
    rows, d = patches.shape
    share = w_query.shape[1]
    ff = w_gate.shape[1]
    half_rows = rows // 2
    quarter = d // 4
    narrow = lax.axis_index("narrow")
    wide = lax.axis_index("wide")
    x_half = narrow // 2
    exact_blocks = lax.axis_size("wide") == 8
    scalars = jnp.stack([x_half, wide if exact_blocks else 0 * wide, narrow]).astype(jnp.int32)

    head_table, head_parts, block_rows = gather_shards(
        jnp.concatenate([w_query, w_key, w_value, w_out.T], axis=1)
    )
    ff_table, ff_parts, _ = gather_shards(jnp.concatenate([w_gate, w_up, w_down.T], axis=1))
    out_table, out_leads = reduce_tables()

    gain_in = norm_gain_attn[None, :]
    gain_mid = norm_gain_mlp[None, :]
    query_mask, key_mask, live = mask_features(item_slots, valid_counts, rows)

    q, k, v = project(scalars, patches, gain_in, head_table, head_parts, block_rows, share)
    heads, query_aux, attn_part = attend(
        scalars, q, k, v, query_mask, key_mask, head_table, head_parts, block_rows, share
    )
    attn_other = swap_core(attn_part)
    mlp_part, mid_t, back_part, attn_square, *ff_grads = feed_forward(
        scalars, patches, attn_part, attn_other, cotangent, key_mask, gain_mid,
        ff_table, ff_parts, block_rows, out_table, out_leads,
    )
    back_other = swap_core(back_part)
    grad_mid, grad_heads, dwo, gain_mid_sum = mid_backward(
        scalars, patches, attn_part, attn_other, back_part, back_other, cotangent, key_mask,
        gain_mid, heads, head_table, head_parts, block_rows, share,
    )
    dq, dk, dv = attend_back(q, k, v, query_aux, key_mask, heads, grad_heads)
    grad_t, gain_in_sum, *head_grads = last_backward(
        scalars, patches, gain_in, dq, dk, dv, grad_mid, dwo,
        head_table, head_parts, block_rows, out_table, out_leads, share,
    )

    mlp_keep = total(mlp_part[: 2 * quarter], swap_core(mlp_part[2 * quarter :]))
    mid_keep = jnp.concatenate(
        [
            lax.dynamic_slice_in_dim(mid_t, narrow * quarter, quarter, 0),
            lax.dynamic_slice_in_dim(mid_t, (narrow ^ 2) * quarter, quarter, 0),
        ]
    )
    live_own = lax.dynamic_slice_in_dim(live, x_half * half_rows, half_rows)
    layer = jnp.where(live_own[None, :], mid_keep + mlp_keep, 0.0)
    layer16 = layer.astype(bf16)
    mlp_square = jnp.sum(jnp.where(live_own[None, :], mlp_keep * mlp_keep, 0.0))
    layer_square = jnp.sum(layer * layer)
    mine, theirs = layer16[:quarter], swap_x(layer16[quarter:])
    output = jnp.where(
        x_half == 0,
        jnp.concatenate([mine, theirs], axis=1),
        jnp.concatenate([theirs, mine], axis=1),
    ).T

    grad_keep = total(grad_t[: 2 * quarter], swap_core(grad_t[2 * quarter :]))
    grad_patches = total(grad_keep[:quarter], swap_x(grad_keep[quarter:].astype(bf16))).T

    head_own = reduce_shards(head_grads)
    ff_own = reduce_shards(ff_grads)

    stats = jnp.stack(
        [
            0.5 * jnp.sum(attn_square),
            mlp_square,
            layer_square,
            0.5 * jnp.sum(live_own.astype(f32)),
        ]
    )
    sums = sum_all(
        jnp.concatenate([gain_in_sum[0], 0.5 * gain_mid_sum[0], jnp.pad(stats, (0, LANES - 4))])
    )
    total_in, total_mid, totals = sums[:d], sums[d : 2 * d], sums[2 * d : 2 * d + 4]
    rms_values = jnp.sqrt(totals[:3] / (totals[3] * d))
    return (
        output,
        grad_patches,
        total_in,
        total_mid,
        head_own[:, :share],
        head_own[:, share : 2 * share],
        head_own[:, 2 * share : 3 * share],
        head_own[:, 3 * share :].T,
        ff_own[:, :ff],
        ff_own[:, ff : 2 * ff],
        ff_own[:, 2 * ff :].T,
        rms_values,
    )


def solution(mesh):
    return jax.shard_map(
        body,
        mesh=mesh,
        in_specs=(
            P("wide", None),
            P(),
            P(),
            P("wide", "narrow"),
            P("wide", "narrow"),
            P("wide", "narrow"),
            P("narrow", "wide"),
            P("wide", "narrow"),
            P("wide", "narrow"),
            P("narrow", "wide"),
            P("wide", None),
            P("wide"),
            P("wide"),
        ),
        out_specs=(
            P("wide", "narrow"),
            P("wide", "narrow"),
            P(),
            P(),
            P("wide", "narrow"),
            P("wide", "narrow"),
            P("wide", "narrow"),
            P("narrow", "wide"),
            P("wide", "narrow"),
            P("wide", "narrow"),
            P("narrow", "wide"),
            P(),
        ),
        check_vma=False,
    )
```

```python
import functools

import jax
import jax.numpy as jnp
from jax import lax
from jax.experimental import pallas as pl
from jax.experimental.pallas import tpu as pltpu
from jax.sharding import PartitionSpec as P

f32 = jnp.float32
bf16 = jnp.bfloat16
HEAD_DIM = 64
UNIT = 512
LANES = 128
epsilon = 1e-06
BIG = 1e30
GELU_C = 0.7978845608028654
GELU_A = 0.044715
HEAD_VMEM, FEED_VMEM, MID_VMEM, BACK_VMEM, LAST_VMEM = 24, 40, 40, 40, 40

NT = (((1,), (1,)), ((), ()))
NN = (((1,), (0,)), ((), ()))
TN = (((0,), (0,)), ((), ()))


def mm(a, b, dims=NN):
    return lax.dot_general(a, b, dims, preferred_element_type=f32)


def split3(v):
    high = v.astype(bf16)
    rest = v - high.astype(f32)
    middle = rest.astype(bf16)
    low = (rest - middle.astype(f32)).astype(bf16)
    return high.astype(f32), middle.astype(f32), low.astype(f32)


def lane_halves():
    lane = lax.broadcasted_iota(jnp.int32, (1, LANES), 1)
    first = (lane < HEAD_DIM).astype(f32)
    return lane, first.astype(bf16), (1.0 - first).astype(bf16)


def block_rows(index, rows, step):
    return pl.ds(pl.multiple_of(index * rows, step), rows)


def block_copies(table, sources, target, wide_index, rows, sem, columns=None):
    step = 16 if rows % 16 == 0 else 8
    copies = []
    for k, (src, lead, half, offset) in enumerate(table):
        source = sources[src].at[lead]
        if columns is not None:
            source = source.at[:, pl.ds(0, columns)]
        copies.append(
            pltpu.make_async_copy(
                source, target.at[half, block_rows(wide_index ^ offset, rows, step), :], sem.at[k]
            )
        )
    return copies


def start_all(copies):
    for copy in copies:
        copy.start()
    return copies


def wait_all(copies):
    for copy in copies:
        copy.wait()


def load_blocks(*args):
    wait_all(start_all(block_copies(*args)))


def store_blocks(table, acc, targets, wide_index, rows):
    for src, lead, half, offset in table:
        targets[src][lead] = acc[half, block_rows(wide_index ^ offset, rows, 8), :].astype(bf16)


def padded(weights, width):
    return jnp.concatenate(
        [weights, jnp.zeros((weights.shape[0], width - weights.shape[1]), weights.dtype)], axis=1
    )


X_HALF, WIDE, NARROW, ITEMS = 0, 1, 2, 3


def unit_item(s_ref, unit, units):
    start = (unit * UNIT) & -s_ref[ITEMS + unit]
    return start, s_ref[ITEMS + units + unit]


def live_rows(s_ref, first, tile, units):
    start, valid = unit_item(s_ref, first // UNIT, units)
    return first - start + lax.broadcasted_iota(jnp.int32, (tile, 1), 0) < valid


def query_mask(s_ref, first, lane, units):
    start, _ = unit_item(s_ref, first // UNIT, units)
    column = lane & (HEAD_DIM - 1)
    named = (column < units) & (column != start // UNIT)
    return jnp.where(named | (column == units), 1.0, 0.0)


def key_mask(s_ref, unit, lane, units):
    start, valid = unit_item(s_ref, unit, units)
    column = lane & (HEAD_DIM - 1)
    row = unit * UNIT - start + lax.broadcasted_iota(jnp.int32, (UNIT, 1), 0)
    fixed = jnp.where(column == start // UNIT, -BIG, 0.0)
    fixed = jnp.where((column > units) & (column < units + 4), -1.0, fixed)
    return jnp.where((column == units) & (row >= valid), -BIG, fixed)


def any_specs(arrays):
    return [pl.BlockSpec(memory_space=pl.ANY)] * len(arrays)


def own_tile(i, s, half):
    return jnp.clip(i - s[0] * half, 0, half - 1)


def params(mebibytes):
    return pltpu.CompilerParams(vmem_limit_bytes=mebibytes << 20)


def cost(flops, moved, exps=0):
    return pl.CostEstimate(flops=flops, bytes_accessed=moved, transcendentals=exps)


def once(shape):
    return pl.BlockSpec(shape, lambda *_: (0,) * len(shape), pipeline_mode=pl.Buffered(1))


def head_list(share):
    return [(h // 2, h % 2) for h in range(share // HEAD_DIM)]


def head_lanes(share):
    return -(-share // LANES) * LANES


def head_kernel(
    tables, counts, rows, share, first_shard, sub, chunk, s_ref, x_ref, gain_ref, *refs
):
    heads = head_list(share)
    lane, first, second = lane_halves()
    final = len(tables) == 2
    if final:
        before_ref, refs = refs[0], refs[1:]
    sources = [refs[: counts[0]], refs[counts[0] : sum(counts)]]
    refs = refs[sum(counts) :]
    if first_shard:
        normed_out, refs = refs[0], refs[1:]
    q_out, k_out, v_out, o_ref, aux_ref = refs[:5]
    refs = refs[5:]
    if final:
        part_ref, refs = refs[0], refs[1:]
    buf, weights, values_in, normed, qs, ks, vs, keys, values, sem, in_sem, out_sem = refs[:12]
    n, d = normed.shape
    n_q = qs.shape[0]
    units = n // UNIT
    loads = start_all(block_copies(tables[0], sources[0], buf, s_ref[WIDE], rows, sem.at[0]))
    target = values_in if first_shard else normed
    unit_rows = [slice(u * UNIT, (u + 1) * UNIT) for u in range(units)]
    inputs = start_all(
        [
            pltpu.make_async_copy(x_ref.at[here, :], target.at[here, :], in_sem.at[u])
            for u, here in enumerate(unit_rows)
        ]
    )
    if final:
        other = start_all(
            block_copies(tables[1], sources[1], refs[12], s_ref[WIDE], rows, sem.at[1], refs[12].shape[2])
        )
    wait_all(loads)
    for at in range(3):
        weights[at] = padded(buf[0, :, (at + 1) * share : (at + 2) * share], weights.shape[2])
    outputs = []

    def send(source, to):
        copy = pltpu.make_async_copy(source, to, out_sem.at[len(outputs)])
        copy.start()
        outputs.append(copy)

    ones = [(lane == 64).astype(f32).astype(bf16), (lane == 0).astype(f32).astype(bf16)]
    for u, here in enumerate(unit_rows):
        inputs[u].wait()
        if first_shard:
            x = values_in[here, :].astype(f32)
            scale = lax.rsqrt(jnp.mean(x * x, axis=1, keepdims=True) + epsilon)
            normed[here, :] = (x * scale * gain_ref[...]).astype(bf16)
            send(normed.at[here, :], normed_out.at[here, :])
        rows_in = normed[here, :]
        k = mm(rows_in, weights[1]).astype(bf16)
        v = mm(rows_in, weights[2]).astype(bf16)
        ks[here, :] = k
        vs[here, :] = v
        mask = key_mask(s_ref, u, lane, units).astype(bf16)
        for at, (pair, side) in enumerate(heads):
            lanes = slice(pair * LANES, (pair + 1) * LANES)
            own, rest = (second, first) if side else (first, second)
            keys[at, here, :] = k[:, lanes] * own + mask * rest
            values[at, here, :] = v[:, lanes] * own + ones[side]
    send(ks, k_out)
    send(vs, v_out)
    qs[...] = mm(normed[block_rows(s_ref[X_HALF], n_q, UNIT), :], weights[0]).astype(bf16)
    send(qs, q_out)

    jobs = [(r, at) for r in range(0, n_q, sub) for at in range(len(heads))]
    marks = {
        r: query_mask(s_ref, s_ref[X_HALF] * n_q + r, lane, units) for r in range(0, n_q, sub)
    }

    def scores(job):
        r, at = job
        pair, side = heads[at]
        own, rest = (second, first) if side else (first, second)
        query = qs[r : r + sub, pair * LANES : (pair + 1) * LANES] * own + marks[r].astype(bf16) * rest
        return [lambda c=c: mm(query, keys[at, c : c + chunk, :], NT) for c in range(0, n, chunk)]

    outs, sums = {}, {}
    current = [f() for f in scores(jobs[0])]
    for j, (r, at) in enumerate(jobs):
        ahead = scores(jobs[j + 1]) if j + 1 < len(jobs) else []
        following = []
        top = functools.reduce(jnp.maximum, [jnp.max(s, axis=1, keepdims=True) for s in current])
        mixed = None
        for i, s in enumerate(current):
            if ahead:
                following.append(ahead[i]())
            part = mm(jnp.exp(s - top).astype(bf16), values[at, i * chunk : (i + 1) * chunk, :])
            mixed = part if mixed is None else mixed + part
        pair, side = heads[at]
        row_sum = mixed[:, 0:1] if side else mixed[:, HEAD_DIM : HEAD_DIM + 1]
        outs[side] = mixed / row_sum
        sums[side] = top + jnp.log(row_sum)
        current = following
        if side == 0 and (pair, 1) in heads:
            continue
        here, lanes = slice(r, r + sub), slice(pair * LANES, (pair + 1) * LANES)
        features = jnp.broadcast_to(marks[r], (sub, LANES))
        for which, value in sums.items():
            for i, piece in enumerate(split3(value)):
                features = jnp.where(lane == (units + 1 if which else 64 + units + 1) + i, piece, features)
        aux_ref[here, lanes] = features.astype(bf16)
        right = outs[1] if 1 in outs else 0.0
        o_ref[here, lanes] = jnp.where(lane < HEAD_DIM, outs[0], right).astype(bf16)
        outs, sums = {}, {}
    if final:
        wait_all(other)
        lanes = o_ref.shape[1]
        part = mm(before_ref[...], refs[12][0], NT) + mm(o_ref[...], buf[0, :, :lanes], NT)
        part_ref[...] = part.astype(bf16)
    wait_all(outputs)


def head_forward(scalars, values, gain, weights, rows, share, first_shard, before=None, sub=256, chunk=512):
    n, d = values.shape
    lanes = head_lanes(share)
    heads = share // HEAD_DIM
    tables, sources = [weights[0][0]], [weights[0][1]]
    args = [scalars, values, gain]
    in_specs = [pl.BlockSpec(memory_space=pl.ANY), once((1, d))]
    width = sources[0][0].shape[-1]
    q_shape, k_shape = (n // 2, lanes), (n, lanes)
    shapes = [q_shape, k_shape, k_shape, q_shape, q_shape]
    if first_shard:
        shapes = [(n, d)] + shapes
    out_specs = [pl.BlockSpec(memory_space=pl.ANY)] * (len(shapes) - 2) + [once(q_shape)] * 2
    scratch = [
        pltpu.VMEM((1, d, width), bf16),
        pltpu.VMEM((3, d, lanes), bf16),
        pltpu.VMEM((n, d) if first_shard else (16, LANES), bf16),
        pltpu.VMEM((n, d), bf16),
        pltpu.VMEM(q_shape, bf16),
        pltpu.VMEM(k_shape, bf16),
        pltpu.VMEM(k_shape, bf16),
        pltpu.VMEM((heads, n, LANES), bf16),
        pltpu.VMEM((heads, n, LANES), bf16),
        pltpu.SemaphoreType.DMA((2, len(tables[0]))),
        pltpu.SemaphoreType.DMA((n // UNIT,)),
        pltpu.SemaphoreType.DMA((n // UNIT + 3,)),
    ]
    if before is not None:
        tables.append(weights[1][0])
        sources.append(weights[1][1])
        args.append(before)
        in_specs.append(once(before.shape))
        shapes.append((n // 2, d))
        out_specs.append(once((n // 2, d)))
        scratch.append(pltpu.VMEM((1, d, lanes), bf16))
    counts = tuple(len(part) for part in sources)
    for part in sources:
        args += part
        in_specs += any_specs(part)
    return pl.pallas_call(
        functools.partial(head_kernel, tables, counts, rows, share, first_shard, sub, chunk),
        out_shape=tuple(jax.ShapeDtypeStruct(shape, bf16) for shape in shapes),
        grid_spec=pltpu.PrefetchScalarGridSpec(
            num_scalar_prefetch=1,
            grid=(1,),
            in_specs=in_specs,
            out_specs=out_specs,
            scratch_shapes=scratch,
        ),
        compiler_params=params(HEAD_VMEM),
        cost_estimate=cost(20 * n * n * share // 2, 8 * n * d, n * n * heads),
        name="head_forward",
    )(*args)


def mid_norm(x_ref, a_ref, b_ref):
    attn = a_ref[...].astype(f32) + b_ref[...].astype(f32)
    middle = x_ref[...].astype(f32) + attn
    scale = lax.rsqrt(jnp.mean(middle * middle, axis=1, keepdims=True) + epsilon)
    return attn, middle, scale


def store_quarters(narrow_index, value, keep_ref, send_ref):
    quarter = value.shape[0] // 4
    for block in range(4):
        at = narrow_index ^ block
        here = block_rows(at // 2, quarter, 16)
        piece = value[block * quarter : (block + 1) * quarter, :]

        @pl.when(at % 2 == 0)
        def _():
            keep_ref[here, :] = piece.astype(keep_ref.dtype)

        if send_ref is not None:

            @pl.when(at % 2 == 1)
            def _():
                send_ref[here, :] = piece.astype(send_ref.dtype)


def feed_half(normed, grad, buf, acc, first):
    ff = buf.shape[2] // 3
    w_gate, w_up, w_down = [buf[0, :, at * ff : (at + 1) * ff] for at in range(3)]
    gate = mm(normed, w_gate)
    up = mm(normed, w_up)
    back_hidden = mm(grad, w_down)
    square = gate * gate
    cdf = 0.5 + 0.5 * jnp.tanh(gate * (GELU_C + GELU_C * GELU_A * square))
    act = gate * cdf
    slope = cdf + act * (1.0 - cdf) * (2.0 * GELU_C + 6.0 * GELU_C * GELU_A * square)
    hidden = (act * up).astype(bf16)
    grad_gate = (back_hidden * up * slope).astype(bf16)
    grad_up = (back_hidden * act).astype(bf16)
    normed_t, grad_t = normed.T, grad.T
    for at, (left, right) in enumerate(((normed_t, grad_gate), (normed_t, grad_up), (grad_t, hidden))):
        lanes = slice(at * ff, (at + 1) * ff)
        part = mm(left, right)

        @pl.when(first)
        def _():
            acc[0, :, lanes] = part

        @pl.when(jnp.logical_not(first))
        def _():
            acc[0, :, lanes] += part

    back = mm(grad_gate, w_gate, NT) + mm(grad_up, w_up, NT)
    return back, mm(w_down, hidden, NT)


def feed_own_kernel(
    table, n_src, rows, out_table, n_out, units, s_ref, x_ref, a_ref, b_ref, cot_ref, gain_ref, *refs
):
    sources = refs[:n_src]
    normed_ref, grad_ref, back_ref, mlp_ref, mid_ref, stat_ref = refs[n_src : n_src + 6]
    targets = refs[n_src + 6 : n_src + 6 + n_out]
    buf, acc, stat, sem = refs[n_src + 6 + n_out :]
    i = pl.program_id(0)
    copies = block_copies(table, sources, buf, s_ref[WIDE], rows, sem)

    @pl.when(i == 0)
    def _():
        start_all(copies)
        stat[...] = jnp.zeros_like(stat)

    attn, middle, scale = mid_norm(x_ref, a_ref, b_ref)
    tile, half_rows = x_ref.shape[0], x_ref.shape[0] * pl.num_programs(0)
    live = live_rows(s_ref, s_ref[X_HALF] * half_rows + i * tile, tile, units)
    stat[...] += jnp.sum(jnp.where(live, attn * attn, 0.0), axis=0, keepdims=True)
    normed = (middle * scale * gain_ref[...]).astype(bf16)
    grad = jnp.where(live, cot_ref[...].astype(f32), 0.0).astype(bf16)
    normed_ref[...] = normed
    grad_ref[...] = grad
    store_quarters(s_ref[NARROW], middle.T, mid_ref, None)

    @pl.when(i == 0)
    def _():
        wait_all(copies)

    back_ref[...], mlp_ref[...] = feed_half(normed, grad, buf, acc, i == 0)

    @pl.when(i == pl.num_programs(0) - 1)
    def _():
        stat_ref[...] = jnp.full(stat_ref.shape, jnp.sum(stat[...]))
        store_blocks(out_table, acc, targets, s_ref[WIDE], rows)


def feed_other_kernel(table, n_src, rows, out_table, n_out, s_ref, normed_ref, grad_ref, before_ref, mlp_ref, *refs):
    sources = refs[:n_src]
    back_ref, keep_ref, send_ref = refs[n_src : n_src + 3]
    targets = refs[n_src + 3 : n_src + 3 + n_out]
    buf, acc, sem = refs[n_src + 3 + n_out :]
    i = pl.program_id(0)

    @pl.when(i == 0)
    def _():
        load_blocks(table, sources, buf, s_ref[WIDE], rows, sem)

    back, out = feed_half(normed_ref[...], grad_ref[...], buf, acc, i == 0)
    back_ref[...] = (before_ref[...] + back).astype(bf16)
    store_quarters(s_ref[NARROW], mlp_ref[...] + out, keep_ref, send_ref)

    @pl.when(i == pl.num_programs(0) - 1)
    def _():
        store_blocks(out_table, acc, targets, s_ref[WIDE], rows)


def feed_forward(scalars, inputs, weights, rows, out, own, tile=512):
    table, sources = weights
    out_table, out_leads = out
    n, d = inputs[1].shape
    width = sources[0].shape[-1]
    steps = n // tile
    own_spec = pl.BlockSpec((tile, d), lambda i, s: (s[X_HALF] * steps + i, 0))
    row_spec = pl.BlockSpec((tile, d), lambda i, s: (i, 0))
    full_spec = pl.BlockSpec((d, tile), lambda i, s: (0, i))
    half_spec = pl.BlockSpec((d // 2, tile), lambda i, s: (0, i))
    block_specs = [once((lead, rows, width)) for lead in out_leads]
    block_shapes = tuple(jax.ShapeDtypeStruct((lead, rows, width), bf16) for lead in out_leads)
    scratch = [pltpu.VMEM((1, d, width), bf16), pltpu.VMEM((1, d, width), f32)]
    counts = (table, len(sources), rows, out_table, len(out_leads))
    if own:
        kernel = functools.partial(feed_own_kernel, *counts, 2 * n // UNIT)
        in_specs = [own_spec, row_spec, row_spec, own_spec, once((1, d))]
        out_shape = (
            jax.ShapeDtypeStruct((n, d), bf16),
            jax.ShapeDtypeStruct((n, d), bf16),
            jax.ShapeDtypeStruct((n, d), f32),
            jax.ShapeDtypeStruct((d, n), f32),
            jax.ShapeDtypeStruct((d // 2, n), f32),
            jax.ShapeDtypeStruct((1, LANES), f32),
        )
        out_specs = [row_spec, row_spec, row_spec, full_spec, half_spec, once((1, LANES))]
        scratch.append(pltpu.VMEM((1, d), f32))
    else:
        kernel = functools.partial(feed_other_kernel, *counts)
        in_specs = [row_spec, row_spec, row_spec, full_spec]
        out_shape = (
            jax.ShapeDtypeStruct((n, d), bf16),
            jax.ShapeDtypeStruct((d // 2, n), bf16),
            jax.ShapeDtypeStruct((d // 2, n), bf16),
        )
        out_specs = [row_spec, half_spec, half_spec]
    return pl.pallas_call(
        kernel,
        out_shape=out_shape + block_shapes,
        grid_spec=pltpu.PrefetchScalarGridSpec(
            num_scalar_prefetch=1,
            grid=(steps,),
            in_specs=in_specs + any_specs(sources),
            out_specs=out_specs + block_specs,
            scratch_shapes=scratch + [pltpu.SemaphoreType.DMA((len(table),))],
        ),
        compiler_params=params(FEED_VMEM),
        cost_estimate=cost(2 * n * d * width * 3, 10 * n * d, n * width // 3),
        name="feed_forward",
    )(scalars, *inputs, *sources)


def mid_kernel(
    tables, counts, rows, units, s_ref, x_ref, a_ref, b_ref, g_ref, h_ref, cot_ref, gain_ref, o0_ref, o1_ref, *refs
):
    sources = [refs[: counts[0]], refs[counts[0] : sum(counts)]]
    gm_ref, do0_ref, do1_ref, dwo_ref, gain_out, buf, total, sem = refs[sum(counts) :]
    i = pl.program_id(0)

    @pl.when(i == 0)
    def _():
        for at in range(2):
            load_blocks(
                tables[at], sources[at], buf.at[pl.ds(at, 1)], s_ref[WIDE], rows, sem.at[at], buf.shape[2]
            )
        total[...] = jnp.zeros_like(total)

    _, middle, scale = mid_norm(x_ref, a_ref, b_ref)
    hat = middle * scale
    back = g_ref[...].astype(f32) + h_ref[...].astype(f32)
    tile, half_rows = x_ref.shape[0], x_ref.shape[0] * pl.num_programs(0)
    live = live_rows(s_ref, s_ref[X_HALF] * half_rows + i * tile, tile, units)
    cot = jnp.where(live, cot_ref[...].astype(f32), 0.0)
    total[...] += jnp.sum(back * hat, axis=0, keepdims=True)
    scaled = back * gain_ref[...]
    mean = jnp.mean(scaled * hat, axis=1, keepdims=True)
    grad_mid = cot + scale * (scaled - hat * mean)
    grad = grad_mid.astype(bf16)
    grad_t = grad_mid.T
    gm_ref[...] = grad_t
    grad_t = grad_t.astype(bf16)
    for at, (o_ref, do_ref) in enumerate(((o0_ref, do0_ref), (o1_ref, do1_ref))):
        do_ref[...] = mm(grad, buf[at]).astype(bf16)
        part = mm(grad_t, o_ref[...])

        @pl.when(i == 0)
        def _():
            dwo_ref[at] = part

        @pl.when(i > 0)
        def _():
            dwo_ref[at] += part

    @pl.when(i == pl.num_programs(0) - 1)
    def _():
        gain_out[...] = total[...]


def mid_backward(scalars, patches, a, b, g, h, cot, gain, o, own, other, rows, tile=512):
    n, d = a.shape
    lanes = o[0].shape[1]
    steps = n // tile
    own_spec = pl.BlockSpec((tile, d), lambda i, s: (s[X_HALF] * steps + i, 0))
    row_spec = pl.BlockSpec((tile, d), lambda i, s: (i, 0))
    head_spec = pl.BlockSpec((tile, lanes), lambda i, s: (i, 0))
    return pl.pallas_call(
        functools.partial(
            mid_kernel, (own[0], other[0]), (len(own[1]), len(other[1])), rows, 2 * n // UNIT
        ),
        out_shape=(
            jax.ShapeDtypeStruct((d, n), f32),
            jax.ShapeDtypeStruct((n, lanes), bf16),
            jax.ShapeDtypeStruct((n, lanes), bf16),
            jax.ShapeDtypeStruct((2, d, lanes), f32),
            jax.ShapeDtypeStruct((1, d), f32),
        ),
        grid_spec=pltpu.PrefetchScalarGridSpec(
            num_scalar_prefetch=1,
            grid=(steps,),
            in_specs=[own_spec, row_spec, row_spec, row_spec, row_spec, own_spec]
            + [once((1, d)), head_spec, head_spec]
            + any_specs(own[1])
            + any_specs(other[1]),
            out_specs=[
                pl.BlockSpec((d, tile), lambda i, s: (0, i)),
                head_spec,
                head_spec,
                once((2, d, lanes)),
                once((1, d)),
            ],
            scratch_shapes=[
                pltpu.VMEM((2, d, lanes), bf16),
                pltpu.VMEM((1, d), f32),
                pltpu.SemaphoreType.DMA((2, len(own[0]))),
            ],
        ),
        compiler_params=params(MID_VMEM),
        cost_estimate=cost(8 * n * d * lanes, 16 * n * d),
        name="mid_backward",
    )(scalars, patches, a, b, g, h, cot, gain, *o, *own[1], *other[1])


def head_back_kernel(
    table, n_out, rows, share, chunk, s_ref, q_ref, k_ref, v_ref, do_ref, o_ref, aux_ref, dwo_ref, normed_ref, *refs
):
    dq_out, dk_out, dv_out = refs[:3]
    targets = refs[3 : 3 + n_out]
    normed, dq_buf, dk_buf, dv_buf, pack, sem = refs[3 + n_out :]
    heads = head_list(share)
    lane, first, second = lane_halves()
    in_first = lane < HEAD_DIM
    n, n_q = dk_buf.shape[0], dq_buf.shape[0]
    units = n // UNIT
    load = pltpu.make_async_copy(normed_ref, normed, sem.at[0])
    load.start()
    minus = [
        -((lane >= 64) & (lane < 67)).astype(f32).astype(bf16),
        -(lane < 3).astype(f32).astype(bf16),
    ]
    masks = [key_mask(s_ref, u, lane, units).astype(bf16) for u in range(units)]
    for pair in range(q_ref.shape[1] // LANES):
        members = [side for p, side in heads if p == pair]
        lanes = slice(pair * LANES, (pair + 1) * LANES)
        q, aux, do = q_ref[:, lanes], aux_ref[:, lanes], do_ref[:, lanes]
        product = do.astype(f32) * o_ref[:, lanes].astype(f32)
        features = jnp.zeros(q.shape, f32)
        for side in members:
            inside = ~in_first if side else in_first
            row_sum = jnp.sum(jnp.where(inside, product, 0.0), axis=1, keepdims=True)
            for j, value in enumerate(split3(row_sum)):
                features = jnp.where(lane == (j if side else 64 + j), value, features)
        features = features.astype(bf16)
        sides = [(second, first) if side else (first, second) for side in members]
        q_own = [q * own for own, _ in sides]
        do_own = [do * own for own, _ in sides]
        queries = [part + aux * rest for part, (_, rest) in zip(q_own, sides)]
        grads = [part + features * rest for part, (_, rest) in zip(do_own, sides)]
        q_own, do_own = jnp.concatenate(q_own, axis=0), jnp.concatenate(do_own, axis=0)
        dq = None
        for c in range(0, n, chunk):
            k, v = k_ref[c : c + chunk, lanes], v_ref[c : c + chunk, lanes]
            mask = masks[c // UNIT]
            probs, backs, k_own = [], [], []
            for j, side in enumerate(members):
                own, rest = sides[j]
                k_own.append(k * own)
                p = jnp.exp(mm(k_own[j] + mask * rest, queries[j], NT))
                backs.append((p * mm(v * own + minus[side], grads[j], NT)).astype(bf16))
                probs.append(p.astype(bf16))
            part = mm(jnp.concatenate(k_own, axis=0).T, jnp.concatenate(backs, axis=0))
            dq = part if dq is None else dq + part
            dv_buf[c : c + chunk, lanes] = mm(jnp.concatenate(probs, axis=1), do_own).astype(bf16)
            dk_buf[c : c + chunk, lanes] = mm(jnp.concatenate(backs, axis=1), q_own).astype(bf16)
        dq_buf[:, lanes] = dq.T.astype(bf16)
    copies = start_all(
        [
            pltpu.make_async_copy(source, to, sem.at[1 + at])
            for at, (source, to) in enumerate(((dq_buf, dq_out), (dk_buf, dk_out), (dv_buf, dv_out)))
        ]
    )
    load.wait()
    pack[0, :, 0:share] = dwo_ref[0, :, 0:share]
    mine = normed[block_rows(s_ref[X_HALF], n_q, UNIT), :]
    pack[0, :, share : 2 * share] = mm(mine, dq_buf[...], TN)[:, 0:share]
    both = mm(normed[...], jnp.concatenate([dk_buf[...], dv_buf[...]], axis=1), TN)
    pack[0, :, 2 * share : 3 * share] = both[:, 0:share]
    pack[0, :, 3 * share : 4 * share] = both[:, dk_buf.shape[1] : dk_buf.shape[1] + share]
    store_blocks(table, pack, targets, s_ref[WIDE], rows)
    wait_all(copies)


def head_backward(scalars, q, k, v, do, o, aux, dwo, which, normed, out, rows, share, chunk=512):
    n, d = normed.shape
    n_q, lanes = q.shape
    out_table, out_leads = out
    shapes = [(n_q, lanes), (n, lanes), (n, lanes)]
    blocks = [(lead, rows, 4 * share) for lead in out_leads]
    q_spec, k_spec = once((n_q, lanes)), once((n, lanes))
    any_spec = pl.BlockSpec(memory_space=pl.ANY)
    return pl.pallas_call(
        functools.partial(head_back_kernel, out_table, len(blocks), rows, share, chunk),
        out_shape=tuple(jax.ShapeDtypeStruct(shape, bf16) for shape in shapes + blocks),
        grid_spec=pltpu.PrefetchScalarGridSpec(
            num_scalar_prefetch=1,
            grid=(1,),
            in_specs=[q_spec, k_spec, k_spec, q_spec, q_spec, q_spec]
            + [
                pl.BlockSpec((1, d, lanes), lambda i, s: (which, 0, 0), pipeline_mode=pl.Buffered(1)),
                any_spec,
            ],
            out_specs=[any_spec] * 3 + [once(block) for block in blocks],
            scratch_shapes=[pltpu.VMEM((n, d), bf16)]
            + [pltpu.VMEM(shape, bf16) for shape in shapes]
            + [pltpu.VMEM((1, d, 4 * share), f32), pltpu.SemaphoreType.DMA((4,))],
        ),
        compiler_params=params(BACK_VMEM),
        cost_estimate=cost(20 * n * n * share, 8 * n * d, n * n * share // 128),
        name="head_backward",
    )(scalars, q, k, v, do, o, aux, dwo, normed)


def last_kernel(tables, counts, rows, share, s_ref, x_ref, gain_ref, gm_ref, *refs):
    grads = refs[:6]
    refs = refs[6:]
    sources = [refs[: counts[0]], refs[counts[0] : sum(counts)]]
    keep_ref, send_ref, gain_out, buf, weights, total, gain, sem = refs[sum(counts) :]
    i = pl.program_id(0)
    half = pl.num_programs(0) // 2
    d = x_ref.shape[1]

    @pl.when(i == 0)
    def _():
        for at in range(2):
            load_blocks(tables[at], sources[at], buf.at[pl.ds(at, 1)], s_ref[WIDE], rows, sem.at[at])
        for at in range(2):
            for j in range(3):
                weights[3 * at + j] = padded(
                    buf[at, :, (j + 1) * share : (j + 2) * share], weights.shape[2]
                )
        total[...] = jnp.zeros_like(total)
        gain[...] = jnp.broadcast_to(gain_ref[...], (LANES, d)).T[:, :1]

    mine = i // half == s_ref[X_HALF]
    x = x_ref[...].T.astype(f32)
    scale = lax.rsqrt(jnp.mean(x * x, axis=0, keepdims=True) + epsilon)
    hat = x * scale
    back = None
    for at in range(2):
        for j in range(3):
            value = grads[3 * at + j][...]
            if j == 0:
                value = jnp.where(mine, value.astype(f32), 0.0).astype(bf16)
            part = mm(weights[3 * at + j], value, NT)
            back = part if back is None else back + part
    total[...] += jnp.sum(back * hat, axis=1, keepdims=True)
    scaled = back * gain[...]
    mean = jnp.mean(scaled * hat, axis=0, keepdims=True)
    grad = scale * (scaled - hat * mean) + jnp.where(mine, 0.5, 0.0) * gm_ref[...]
    store_quarters(s_ref[NARROW], grad, keep_ref, send_ref)

    @pl.when(i == pl.num_programs(0) - 1)
    def _():
        gain_out[...] = jnp.broadcast_to(total[...], (d, LANES)).T[:1, :]


def last_backward(scalars, patches, gain, gm_t, grads, own, other, rows, share, tile=512):
    n, d = patches.shape
    width = own[1][0].shape[-1]
    lanes = grads[0].shape[1]
    steps = n // tile
    half = steps // 2
    key_spec = pl.BlockSpec((tile, lanes), lambda i, s: (i, 0))
    own_spec = pl.BlockSpec((tile, lanes), lambda i, s: (own_tile(i, s, half), 0))
    half_spec = pl.BlockSpec((d // 2, tile), lambda i, s: (0, i))
    return pl.pallas_call(
        functools.partial(last_kernel, (own[0], other[0]), (len(own[1]), len(other[1])), rows, share),
        out_shape=(
            jax.ShapeDtypeStruct((d // 2, n), bf16),
            jax.ShapeDtypeStruct((d // 2, n), bf16),
            jax.ShapeDtypeStruct((1, d), f32),
        ),
        grid_spec=pltpu.PrefetchScalarGridSpec(
            num_scalar_prefetch=1,
            grid=(steps,),
            in_specs=[
                pl.BlockSpec((tile, d), lambda i, s: (i, 0)),
                once((1, d)),
                pl.BlockSpec((d, tile), lambda i, s: (0, own_tile(i, s, half))),
            ]
            + [own_spec, key_spec, key_spec] * 2
            + any_specs(own[1])
            + any_specs(other[1]),
            out_specs=[half_spec, half_spec, once((1, d))],
            scratch_shapes=[
                pltpu.VMEM((2, d, width), bf16),
                pltpu.VMEM((6, d, lanes), bf16),
                pltpu.VMEM((d, 1), f32),
                pltpu.VMEM((d, 1), f32),
                pltpu.SemaphoreType.DMA((2, len(own[0]))),
            ],
        ),
        compiler_params=params(LAST_VMEM),
        cost_estimate=cost(2 * n * d * lanes * 5, 10 * n * d),
        name="last_backward",
    )(scalars, patches, gain, gm_t, *grads, *own[1], *other[1])


def swap_core(value):
    return lax.ppermute(value, "narrow", [(i, i ^ 1) for i in range(4)])


def swap_x(value):
    return lax.ppermute(value, "narrow", [(i, i ^ 2) for i in range(4)])


def swap_wide(value, offset):
    n = lax.axis_size("wide")
    return lax.ppermute(value, "wide", [(i, i ^ offset) for i in range(n)])


def after(value, *others):
    return lax.optimization_barrier((value,) + others)[0]


def small_slice():
    return lax.axis_size("wide") == 8


def along_z(first, second, half, flip):
    return [(first, 0, half, flip)] + [(second, z - 1, half, 2 * z + flip) for z in (1, 2, 3)]


OWN_TABLE = along_z(0, 1, 0, 0) + along_z(2, 3, 0, 1)
OTHER_TABLE = along_z(0, 1, 0, 0) + along_z(2, 3, 0, 1)
CORNER = ((2, 0, 1), (3, 0, 3), (3, 1, 5), (4, 0, 7))
FF_TABLE = along_z(0, 1, 0, 0) + [(src, lead, 0, offset) for src, lead, offset in CORNER]
FLAT_TABLE = [(0, r, 0, r) for r in range(8)]
COLUMN_TABLE = [(0, z, 0, 2 * z) for z in range(4)] + [(1, z, 0, 2 * z + 1) for z in range(4)]
ACROSS_TABLE = (
    [(0, z, 0, 2 * z) for z in range(4)]
    + [(1, z, 0, 2 * z + 1) for z in range(2)]
    + [(2, z, 0, 2 * z + 5) for z in range(2)]
)
WHOLE_TABLE = [(0, 0, 0, 0)]


def gather_whole(shard):
    full = lax.all_gather(shard, "wide", axis=0, tiled=True)[None]
    return full, swap_x(full)


def total(*terms):
    return functools.reduce(jnp.add, [t.astype(f32) for t in terms])


def sum_all(value):
    if not small_slice():
        return lax.psum(value, ("wide", "narrow"))
    value = value + swap_core(value)
    value = value + swap_x(value)
    for offset in (1, 2, 4):
        value = value + swap_wide(value, offset)
    return value


def reduce_whole(part):
    return lax.psum_scatter(part, "wide", scatter_dimension=0, tiled=True).astype(f32)


def body(
    patches,
    norm_gain_attn,
    norm_gain_mlp,
    w_query,
    w_key,
    w_value,
    w_out,
    w_gate,
    w_up,
    w_down,
    cotangent,
    item_slots,
    valid_counts,
):
    rows, d = patches.shape
    share = w_query.shape[1]
    ff = w_gate.shape[1]
    half_rows = rows // 2
    quarter = d // 4
    small = small_slice()
    narrow = lax.axis_index("narrow")
    wide = lax.axis_index("wide")
    x_half = narrow // 2
    scalars = jnp.concatenate(
        [jnp.stack([x_half, wide if small else 0 * wide, narrow]), item_slots, valid_counts]
    ).astype(jnp.int32)
    gain_in, gain_mid = norm_gain_attn[None, :], norm_gain_mlp[None, :]

    def own_units(counts):
        units = half_rows // UNIT
        mine = lax.dynamic_slice_in_dim(counts, x_half * units, units)
        return (mine[:, None] + jnp.zeros((1, UNIT), jnp.int32)).reshape(1, half_rows)

    position = x_half * half_rows + jnp.arange(half_rows, dtype=jnp.int32)[None, :]
    live_own = (position & (own_units(item_slots) - 1)) < own_units(valid_counts)
    live_count = 0.5 * jnp.sum(live_own.astype(f32))

    head_shard = jnp.concatenate([w_out.T, w_query, w_key, w_value], axis=1)[None]
    ff_shard = jnp.concatenate([w_gate, w_up, w_down.T], axis=1)[None]
    if small:
        block = head_shard.shape[1]
        first = [swap_wide(head_shard, 2 * z) for z in (1, 2, 3)]
        first += [swap_wide(head_shard, 1), swap_x(head_shard)]
        ff_early = after(ff_shard, head_shard)
        first += [swap_wide(ff_early, 1), swap_x(ff_early)]
        z1, z2, z4, y0, x0, ff_y0, ff_x0 = lax.optimization_barrier(first)
        z3 = jnp.concatenate([z1, z2, z4])
        y3, x3 = swap_wide(z3, 1), swap_x(z3)
        own = (OWN_TABLE, [head_shard, z3, y0, y3])
        other = (OTHER_TABLE, [x0, x3, swap_wide(x0, 1), swap_x(y3)])
        ff_late = after(ff_shard, z3)
        ff_z = [swap_wide(ff_late, 2 * z) for z in (1, 2, 3)]
        early = (y3,)
        own_out = (COLUMN_TABLE, (4, 4))
        other_out = (FLAT_TABLE, (8,))
        across_out = (ACROSS_TABLE, (4, 2, 2))
    else:
        block = d
        own, other = [(WHOLE_TABLE, [full]) for full in gather_whole(head_shard[0])]
        ff_own_weights, ff_other_weights = [(WHOLE_TABLE, [full]) for full in gather_whole(ff_shard[0])]
        own_out = other_out = across_out = (WHOLE_TABLE, (1,))
        early = ()

    values = after(patches, scalars, gain_in, gain_mid, live_own, live_count, *early)
    normed, q0, k0, v0, o0, aux0 = head_forward(scalars, values, gain_in, [own], block, share, True)
    normed = after(normed, o0)
    if small:
        *ff_z, normed = lax.optimization_barrier((*ff_z, normed))
        ff_z3 = jnp.concatenate(ff_z)
        ff_z3, normed = lax.optimization_barrier((ff_z3, normed))
        ff_y3, ff_x3 = swap_wide(ff_z3, 1), swap_x(ff_z3)
        ff_own_weights = (OWN_TABLE, [ff_shard, ff_z3, ff_y0, ff_y3])
    q1, k1, v1, o1, aux1, attn_part = head_forward(
        scalars, normed, gain_in, [other, own], block, share, False, before=o0
    )
    if small:
        ff_y3, ff_x3, ff_x0, attn_part = lax.optimization_barrier((ff_y3, ff_x3, ff_x0, attn_part))
        ff_own_weights[1][3] = ff_y3
        corner = [swap_wide(ff_x0, 1), swap_x(ff_y3[:2]), swap_wide(ff_x3[2:], 1)]
        ff_other_weights = (FF_TABLE, [ff_x0, ff_x3, *corner])
    attn_other = swap_core(attn_part)
    normed_mid, grad_mlp, back_own, mlp_own, mid_keep, attn_square, *ff_own_grads = feed_forward(
        scalars, (values, attn_part, attn_other, cotangent, gain_mid), ff_own_weights, block, own_out, True
    )
    back_part, mlp_keep, mlp_send, *ff_other_grads = feed_forward(
        scalars, (normed_mid, grad_mlp, back_own, mlp_own), ff_other_weights, block, across_out, False
    )
    back_other = swap_core(back_part)
    if small:
        column, to_y = ff_own_grads
        to_x, corner_x, corner_y = ff_other_grads
        got_x, got_y = swap_x(corner_x), swap_wide(corner_y, 1)
    gm_t, do0, do1, dwo, gain_mid_sum = mid_backward(
        scalars, values, attn_part, attn_other, back_part, back_other, cotangent, gain_mid,
        (o0, o1), own, other, block,
    )
    if small:
        got_x, got_y, to_x, to_y = lax.optimization_barrier((got_x, got_y, to_x, to_y, do1))[:4]
        to_y = jnp.concatenate([total(to_y[:2], got_x).astype(bf16), to_y[2:]])
        to_x = jnp.concatenate([to_x[:2], total(to_x[2:], got_y).astype(bf16)])
        got_y, got_x = swap_wide(to_y, 1), swap_x(to_x)
        do1 = after(do1, to_y, to_x)
    *grads1, head1 = head_backward(
        scalars, q1, k1, v1, do1, o1, aux1, dwo, 1, normed, other_out, block, share
    )

    mlp = total(mlp_keep, after(swap_core(after(mlp_send, do1)), head1))
    layer = jnp.where(live_own, mid_keep + mlp, 0.0)
    layer16 = layer.astype(bf16)
    mlp_square = jnp.sum(jnp.where(live_own, mlp * mlp, 0.0))
    layer_square = jnp.sum(layer * layer)
    stats = jnp.stack([mlp_square, layer_square, live_count])[None]
    stats = jnp.concatenate(
        [0.5 * gain_mid_sum, 0.5 * attn_square[:, :1], jnp.pad(stats, ((0, 0), (0, LANES - 4)))],
        axis=1,
    )

    head1_other = swap_x(head1)
    layer_mine, layer_sent = layer16[:quarter], layer16[quarter:]
    layer_got = swap_x(layer_sent)
    do0 = after(do0, head1, stats, layer_mine, layer_sent)
    if small:
        column = total(column, after(got_y, head1), after(got_x, head1))
        sent = [column[z].astype(bf16) for z in (1, 2, 3)]
        do0 = after(do0, *sent)
        back = [swap_wide(sent[z - 1], 2 * z) for z in (1, 2, 3)]
    *grads0, head0, head0_y = head_backward(
        scalars, q0, k0, v0, do0, o0, aux0, dwo, 0, normed, own_out, block, share
    ) + (() if small else (None,))
    dq0, head1_other = lax.optimization_barrier((grads0[0], head1_other))
    if small:
        head_y = total(head0_y, head1_other[1::2]).astype(bf16)
        dq0 = after(dq0, head_y)
        head_y = swap_wide(head_y, 1)
    grad_keep, grad_send, gain_in_sum = last_backward(
        scalars, values, gain_in, gm_t, [dq0, *grads0[1:], *grads1], own, other, block, share
    )

    if small:
        grad_keep, grad_send, gain_in_sum, head_y = lax.optimization_barrier(
            (grad_keep, grad_send, gain_in_sum, head_y)
        )
    grad_got = swap_core(grad_send)
    grad_sent = total(grad_keep[quarter:], grad_got[quarter:]).astype(bf16)
    if small:
        head_column = total(head0, head1_other[::2], head_y)
        head_sent = [head_column[z].astype(bf16) for z in (1, 2, 3)]
        gain_in_sum, layer_got, *back = lax.optimization_barrier(
            (gain_in_sum, layer_got, *back, grad_sent, *head_sent)
        )[: 2 + len(back)]
        head_own = total(
            head_column[0], *[swap_wide(head_sent[z - 1], 2 * z) for z in (1, 2, 3)]
        )
        ff_own = total(column[0], *back)
    else:
        both = total(ff_own_grads[0][0], swap_x(ff_other_grads[0][0])).astype(bf16)
        ff_own = reduce_whole(both)
        head_own = reduce_whole(total(head0[0], head1_other[0]).astype(bf16))
    output = jnp.where(
        x_half == 0,
        jnp.concatenate([layer_mine, layer_got], axis=1),
        jnp.concatenate([layer_got, layer_mine], axis=1),
    )
    grad_patches = total(grad_keep[:quarter], grad_got[:quarter], swap_x(grad_sent))

    sums = sum_all(jnp.concatenate([gain_in_sum, stats], axis=1))[0]
    total_in, total_mid, totals = sums[:d], sums[d : 2 * d], sums[2 * d : 2 * d + 4]
    rms_values = jnp.sqrt(totals[:3] / (totals[3] * d))
    return (
        output.T,
        grad_patches.T,
        total_in,
        total_mid,
        head_own[:, share : 2 * share],
        head_own[:, 2 * share : 3 * share],
        head_own[:, 3 * share :],
        head_own[:, :share].T,
        ff_own[:, :ff],
        ff_own[:, ff : 2 * ff],
        ff_own[:, 2 * ff :].T,
        rms_values,
    )


def solution(mesh):
    return jax.shard_map(
        body,
        mesh=mesh,
        in_specs=(
            P("wide", None),
            P(),
            P(),
            P("wide", "narrow"),
            P("wide", "narrow"),
            P("wide", "narrow"),
            P("narrow", "wide"),
            P("wide", "narrow"),
            P("wide", "narrow"),
            P("narrow", "wide"),
            P("wide", None),
            P("wide"),
            P("wide"),
        ),
        out_specs=(
            P("wide", "narrow"),
            P("wide", "narrow"),
            P(),
            P(),
            P("wide", "narrow"),
            P("wide", "narrow"),
            P("wide", "narrow"),
            P("narrow", "wide"),
            P("wide", "narrow"),
            P("wide", "narrow"),
            P("narrow", "wide"),
            P(),
        ),
        check_vma=False,
    )
```

```python
import functools

import jax
import jax.numpy as jnp
from jax import lax
from jax.experimental import pallas as pl
from jax.experimental.pallas import tpu as pltpu
from jax.sharding import PartitionSpec as P

f32 = jnp.float32
bf16 = jnp.bfloat16
HEAD_DIM = 64
UNIT = 512
LANES = 128
epsilon = 1e-06
BIG = 1e30
GELU_C = 0.7978845608028654
GELU_A = 0.044715
HEAD_VMEM, FEED_VMEM, MID_VMEM, BACK_VMEM, LAST_VMEM = 24, 40, 40, 40, 40

NT = (((1,), (1,)), ((), ()))
NN = (((1,), (0,)), ((), ()))
TN = (((0,), (0,)), ((), ()))


def mm(a, b, dims=NN):
    return lax.dot_general(a, b, dims, preferred_element_type=f32)


def split3(v):
    high = v.astype(bf16)
    rest = v - high.astype(f32)
    middle = rest.astype(bf16)
    low = (rest - middle.astype(f32)).astype(bf16)
    return high.astype(f32), middle.astype(f32), low.astype(f32)


def lane_halves():
    lane = lax.broadcasted_iota(jnp.int32, (1, LANES), 1)
    first = (lane < HEAD_DIM).astype(f32)
    return lane, first.astype(bf16), (1.0 - first).astype(bf16)


def block_rows(index, rows, step):
    return pl.ds(pl.multiple_of(index * rows, step), rows)


def block_copies(table, sources, target, wide_index, rows, sem, columns=None):
    step = 16 if rows % 16 == 0 else 8
    copies = []
    for k, (src, lead, half, offset) in enumerate(table):
        source = sources[src].at[lead]
        if columns is not None:
            source = source.at[:, pl.ds(0, columns)]
        copies.append(
            pltpu.make_async_copy(
                source, target.at[half, block_rows(wide_index ^ offset, rows, step), :], sem.at[k]
            )
        )
    return copies


def start_all(copies):
    for copy in copies:
        copy.start()
    return copies


def wait_all(copies):
    for copy in copies:
        copy.wait()


def load_blocks(*args):
    wait_all(start_all(block_copies(*args)))


def store_blocks(table, acc, targets, wide_index, rows):
    for src, lead, half, offset in table:
        targets[src][lead] = acc[half, block_rows(wide_index ^ offset, rows, 8), :].astype(bf16)


def padded(weights, width):
    return jnp.concatenate(
        [weights, jnp.zeros((weights.shape[0], width - weights.shape[1]), weights.dtype)], axis=1
    )


X_HALF, WIDE, NARROW, ITEMS = 0, 1, 2, 3


def unit_item(s_ref, unit, units):
    start = (unit * UNIT) & -s_ref[ITEMS + unit]
    return start, s_ref[ITEMS + units + unit]


def live_rows(s_ref, first, tile, units):
    start, valid = unit_item(s_ref, first // UNIT, units)
    return first - start + lax.broadcasted_iota(jnp.int32, (tile, 1), 0) < valid


def query_mask(s_ref, first, lane, units):
    start, _ = unit_item(s_ref, first // UNIT, units)
    column = lane & (HEAD_DIM - 1)
    named = (column < units) & (column != start // UNIT)
    return jnp.where(named | (column == units), 1.0, 0.0)


def key_mask(s_ref, unit, lane, units):
    start, valid = unit_item(s_ref, unit, units)
    column = lane & (HEAD_DIM - 1)
    row = unit * UNIT - start + lax.broadcasted_iota(jnp.int32, (UNIT, 1), 0)
    fixed = jnp.where(column == start // UNIT, -BIG, 0.0)
    fixed = jnp.where((column > units) & (column < units + 4), -1.0, fixed)
    return jnp.where((column == units) & (row >= valid), -BIG, fixed)


def any_specs(arrays):
    return [pl.BlockSpec(memory_space=pltpu.HBM)] * len(arrays)


def own_tile(i, s, half):
    return jnp.clip(i - s[0] * half, 0, half - 1)


def keep_in_hbm(value):
    return pltpu.with_memory_space_constraint(value, pltpu.HBM)


def params(mebibytes):
    return pltpu.CompilerParams(vmem_limit_bytes=mebibytes << 20)


def cost(flops, moved, exps=0):
    return pl.CostEstimate(flops=flops, bytes_accessed=moved, transcendentals=exps)


def once(shape):
    return pl.BlockSpec(shape, lambda *_: (0,) * len(shape), pipeline_mode=pl.Buffered(1))


def head_list(share):
    return [(h // 2, h % 2) for h in range(share // HEAD_DIM)]


def head_lanes(share):
    return -(-share // LANES) * LANES


def head_kernel(
    tables, counts, rows, share, first_shard, sub, chunk, s_ref, x_ref, gain_ref, *refs
):
    heads = head_list(share)
    lane, first, second = lane_halves()
    final = len(tables) == 2
    if final:
        before_ref, refs = refs[0], refs[1:]
    sources = [refs[: counts[0]], refs[counts[0] : sum(counts)]]
    refs = refs[sum(counts) :]
    if first_shard:
        normed_out, refs = refs[0], refs[1:]
    q_out, k_out, v_out, o_ref, aux_ref = refs[:5]
    refs = refs[5:]
    if final:
        part_ref, refs = refs[0], refs[1:]
    buf, weights, values_in, normed, qs, ks, vs, keys, values, sem, in_sem, out_sem = refs[:12]
    n, d = normed.shape
    n_q = qs.shape[0]
    units = n // UNIT
    loads = start_all(block_copies(tables[0], sources[0], buf, s_ref[WIDE], rows, sem.at[0]))
    target = values_in if first_shard else normed
    unit_rows = [slice(u * UNIT, (u + 1) * UNIT) for u in range(units)]
    inputs = start_all(
        [
            pltpu.make_async_copy(x_ref.at[here, :], target.at[here, :], in_sem.at[u])
            for u, here in enumerate(unit_rows)
        ]
    )
    if final:
        other = start_all(
            block_copies(tables[1], sources[1], refs[12], s_ref[WIDE], rows, sem.at[1], refs[12].shape[2])
        )
    wait_all(loads)
    for at in range(3):
        weights[at] = padded(buf[0, :, (at + 1) * share : (at + 2) * share], weights.shape[2])
    outputs = []

    def send(source, to):
        copy = pltpu.make_async_copy(source, to, out_sem.at[len(outputs)])
        copy.start()
        outputs.append(copy)

    ones = [(lane == 64).astype(f32).astype(bf16), (lane == 0).astype(f32).astype(bf16)]
    for u, here in enumerate(unit_rows):
        inputs[u].wait()
        if first_shard:
            x = values_in[here, :].astype(f32)
            scale = lax.rsqrt(jnp.mean(x * x, axis=1, keepdims=True) + epsilon)
            normed[here, :] = (x * scale * gain_ref[...]).astype(bf16)
            send(normed.at[here, :], normed_out.at[here, :])
        rows_in = normed[here, :]
        k = mm(rows_in, weights[1]).astype(bf16)
        v = mm(rows_in, weights[2]).astype(bf16)
        ks[here, :] = k
        vs[here, :] = v
        mask = key_mask(s_ref, u, lane, units).astype(bf16)
        for at, (pair, side) in enumerate(heads):
            lanes = slice(pair * LANES, (pair + 1) * LANES)
            own, rest = (second, first) if side else (first, second)
            keys[at, here, :] = k[:, lanes] * own + mask * rest
            values[at, here, :] = v[:, lanes] * own + ones[side]
    send(ks, k_out)
    send(vs, v_out)
    qs[...] = mm(normed[block_rows(s_ref[X_HALF], n_q, UNIT), :], weights[0]).astype(bf16)
    send(qs, q_out)

    jobs = [(r, at) for r in range(0, n_q, sub) for at in range(len(heads))]
    marks = {
        r: query_mask(s_ref, s_ref[X_HALF] * n_q + r, lane, units) for r in range(0, n_q, sub)
    }

    def scores(job):
        r, at = job
        pair, side = heads[at]
        own, rest = (second, first) if side else (first, second)
        query = qs[r : r + sub, pair * LANES : (pair + 1) * LANES] * own + marks[r].astype(bf16) * rest
        return [lambda c=c: mm(query, keys[at, c : c + chunk, :], NT) for c in range(0, n, chunk)]

    outs, sums = {}, {}
    current = [f() for f in scores(jobs[0])]
    for j, (r, at) in enumerate(jobs):
        ahead = scores(jobs[j + 1]) if j + 1 < len(jobs) else []
        following = []
        top = functools.reduce(jnp.maximum, [jnp.max(s, axis=1, keepdims=True) for s in current])
        mixed = None
        for i, s in enumerate(current):
            if ahead:
                following.append(ahead[i]())
            part = mm(jnp.exp(s - top).astype(bf16), values[at, i * chunk : (i + 1) * chunk, :])
            mixed = part if mixed is None else mixed + part
        pair, side = heads[at]
        row_sum = mixed[:, 0:1] if side else mixed[:, HEAD_DIM : HEAD_DIM + 1]
        outs[side] = mixed / row_sum
        sums[side] = top + jnp.log(row_sum)
        current = following
        if side == 0 and (pair, 1) in heads:
            continue
        here, lanes = slice(r, r + sub), slice(pair * LANES, (pair + 1) * LANES)
        features = jnp.broadcast_to(marks[r], (sub, LANES))
        for which, value in sums.items():
            for i, piece in enumerate(split3(value)):
                features = jnp.where(lane == (units + 1 if which else 64 + units + 1) + i, piece, features)
        aux_ref[here, lanes] = features.astype(bf16)
        right = outs[1] if 1 in outs else 0.0
        o_ref[here, lanes] = jnp.where(lane < HEAD_DIM, outs[0], right).astype(bf16)
        outs, sums = {}, {}
    if final:
        wait_all(other)
        lanes = o_ref.shape[1]
        part = mm(before_ref[...], refs[12][0], NT) + mm(o_ref[...], buf[0, :, :lanes], NT)
        part_ref[...] = part.astype(bf16)
    wait_all(outputs)


def head_forward(scalars, values, gain, weights, rows, share, first_shard, before=None, sub=256, chunk=512):
    n, d = values.shape
    lanes = head_lanes(share)
    heads = share // HEAD_DIM
    tables, sources = [weights[0][0]], [weights[0][1]]
    args = [scalars, values, gain]
    in_specs = [pl.BlockSpec(memory_space=pl.ANY), once((1, d))]
    width = sources[0][0].shape[-1]
    q_shape, k_shape = (n // 2, lanes), (n, lanes)
    shapes = [q_shape, k_shape, k_shape, q_shape, q_shape]
    if first_shard:
        shapes = [(n, d)] + shapes
    out_specs = [pl.BlockSpec(memory_space=pltpu.HBM)] * (len(shapes) - 2) + [once(q_shape)] * 2
    scratch = [
        pltpu.VMEM((1, d, width), bf16),
        pltpu.VMEM((3, d, lanes), bf16),
        pltpu.VMEM((n, d) if first_shard else (16, LANES), bf16),
        pltpu.VMEM((n, d), bf16),
        pltpu.VMEM(q_shape, bf16),
        pltpu.VMEM(k_shape, bf16),
        pltpu.VMEM(k_shape, bf16),
        pltpu.VMEM((heads, n, LANES), bf16),
        pltpu.VMEM((heads, n, LANES), bf16),
        pltpu.SemaphoreType.DMA((2, len(tables[0]))),
        pltpu.SemaphoreType.DMA((n // UNIT,)),
        pltpu.SemaphoreType.DMA((n // UNIT + 3,)),
    ]
    if before is not None:
        tables.append(weights[1][0])
        sources.append(weights[1][1])
        args.append(before)
        in_specs.append(once(before.shape))
        shapes.append((n // 2, d))
        out_specs.append(once((n // 2, d)))
        scratch.append(pltpu.VMEM((1, d, lanes), bf16))
    counts = tuple(len(part) for part in sources)
    for part in sources:
        args += part
        in_specs += any_specs(part)
    return pl.pallas_call(
        functools.partial(head_kernel, tables, counts, rows, share, first_shard, sub, chunk),
        out_shape=tuple(jax.ShapeDtypeStruct(shape, bf16) for shape in shapes),
        grid_spec=pltpu.PrefetchScalarGridSpec(
            num_scalar_prefetch=1,
            grid=(1,),
            in_specs=in_specs,
            out_specs=out_specs,
            scratch_shapes=scratch,
        ),
        compiler_params=params(HEAD_VMEM),
        cost_estimate=cost(20 * n * n * share // 2, 8 * n * d, n * n * heads),
        name="head_forward",
    )(*args)


def mid_norm(x_ref, a_ref, b_ref):
    attn = a_ref[...].astype(f32) + b_ref[...].astype(f32)
    middle = x_ref[...].astype(f32) + attn
    scale = lax.rsqrt(jnp.mean(middle * middle, axis=1, keepdims=True) + epsilon)
    return attn, middle, scale


def store_quarters(narrow_index, value, keep_ref, send_ref):
    quarter = value.shape[0] // 4
    for block in range(4):
        at = narrow_index ^ block
        here = block_rows(at // 2, quarter, 16)
        piece = value[block * quarter : (block + 1) * quarter, :]

        @pl.when(at % 2 == 0)
        def _():
            keep_ref[here, :] = piece.astype(keep_ref.dtype)

        if send_ref is not None:

            @pl.when(at % 2 == 1)
            def _():
                send_ref[here, :] = piece.astype(send_ref.dtype)


def feed_half(normed, grad, buf, acc, first):
    ff = buf.shape[2] // 3
    w_gate, w_up, w_down = [buf[0, :, at * ff : (at + 1) * ff] for at in range(3)]
    gate = mm(normed, w_gate)
    up = mm(normed, w_up)
    back_hidden = mm(grad, w_down)
    square = gate * gate
    cdf = 0.5 + 0.5 * jnp.tanh(gate * (GELU_C + GELU_C * GELU_A * square))
    act = gate * cdf
    slope = cdf + act * (1.0 - cdf) * (2.0 * GELU_C + 6.0 * GELU_C * GELU_A * square)
    hidden = (act * up).astype(bf16)
    grad_gate = (back_hidden * up * slope).astype(bf16)
    grad_up = (back_hidden * act).astype(bf16)
    normed_t, grad_t = normed.T, grad.T
    for at, (left, right) in enumerate(((normed_t, grad_gate), (normed_t, grad_up), (grad_t, hidden))):
        lanes = slice(at * ff, (at + 1) * ff)
        part = mm(left, right)

        @pl.when(first)
        def _():
            acc[0, :, lanes] = part

        @pl.when(jnp.logical_not(first))
        def _():
            acc[0, :, lanes] += part

    back = mm(grad_gate, w_gate, NT) + mm(grad_up, w_up, NT)
    return back, mm(w_down, hidden, NT)


def feed_own_kernel(
    table, n_src, rows, out_table, n_out, units, s_ref, x_ref, a_ref, b_ref, cot_ref, gain_ref, *refs
):
    sources = refs[:n_src]
    normed_ref, grad_ref, back_ref, mlp_ref, mid_ref, stat_ref = refs[n_src : n_src + 6]
    targets = refs[n_src + 6 : n_src + 6 + n_out]
    buf, acc, stat, sem = refs[n_src + 6 + n_out :]
    i = pl.program_id(0)
    copies = block_copies(table, sources, buf, s_ref[WIDE], rows, sem)

    @pl.when(i == 0)
    def _():
        start_all(copies)
        stat[...] = jnp.zeros_like(stat)

    attn, middle, scale = mid_norm(x_ref, a_ref, b_ref)
    tile, half_rows = x_ref.shape[0], x_ref.shape[0] * pl.num_programs(0)
    live = live_rows(s_ref, s_ref[X_HALF] * half_rows + i * tile, tile, units)
    stat[...] += jnp.sum(jnp.where(live, attn * attn, 0.0), axis=0, keepdims=True)
    normed = (middle * scale * gain_ref[...]).astype(bf16)
    grad = jnp.where(live, cot_ref[...].astype(f32), 0.0).astype(bf16)
    normed_ref[...] = normed
    grad_ref[...] = grad
    store_quarters(s_ref[NARROW], middle.T, mid_ref, None)

    @pl.when(i == 0)
    def _():
        wait_all(copies)

    back_ref[...], mlp_ref[...] = feed_half(normed, grad, buf, acc, i == 0)

    @pl.when(i == pl.num_programs(0) - 1)
    def _():
        stat_ref[...] = jnp.full(stat_ref.shape, jnp.sum(stat[...]))
        store_blocks(out_table, acc, targets, s_ref[WIDE], rows)


def feed_other_kernel(table, n_src, rows, out_table, n_out, s_ref, normed_ref, grad_ref, before_ref, mlp_ref, *refs):
    sources = refs[:n_src]
    back_ref, keep_ref, send_ref = refs[n_src : n_src + 3]
    targets = refs[n_src + 3 : n_src + 3 + n_out]
    buf, acc, sem = refs[n_src + 3 + n_out :]
    i = pl.program_id(0)

    @pl.when(i == 0)
    def _():
        load_blocks(table, sources, buf, s_ref[WIDE], rows, sem)

    back, out = feed_half(normed_ref[...], grad_ref[...], buf, acc, i == 0)
    back_ref[...] = (before_ref[...] + back).astype(bf16)
    store_quarters(s_ref[NARROW], mlp_ref[...] + out, keep_ref, send_ref)

    @pl.when(i == pl.num_programs(0) - 1)
    def _():
        store_blocks(out_table, acc, targets, s_ref[WIDE], rows)


def feed_forward(scalars, inputs, weights, rows, out, own, tile=512):
    table, sources = weights
    out_table, out_leads = out
    n, d = inputs[1].shape
    width = sources[0].shape[-1]
    steps = n // tile
    own_spec = pl.BlockSpec((tile, d), lambda i, s: (s[X_HALF] * steps + i, 0))
    row_spec = pl.BlockSpec((tile, d), lambda i, s: (i, 0))
    full_spec = pl.BlockSpec((d, tile), lambda i, s: (0, i))
    half_spec = pl.BlockSpec((d // 2, tile), lambda i, s: (0, i))
    block_specs = [once((lead, rows, width)) for lead in out_leads]
    block_shapes = tuple(jax.ShapeDtypeStruct((lead, rows, width), bf16) for lead in out_leads)
    scratch = [pltpu.VMEM((1, d, width), bf16), pltpu.VMEM((1, d, width), f32)]
    counts = (table, len(sources), rows, out_table, len(out_leads))
    if own:
        kernel = functools.partial(feed_own_kernel, *counts, 2 * n // UNIT)
        in_specs = [own_spec, row_spec, row_spec, own_spec, once((1, d))]
        out_shape = (
            jax.ShapeDtypeStruct((n, d), bf16),
            jax.ShapeDtypeStruct((n, d), bf16),
            jax.ShapeDtypeStruct((n, d), f32),
            jax.ShapeDtypeStruct((d, n), f32),
            jax.ShapeDtypeStruct((d // 2, n), f32),
            jax.ShapeDtypeStruct((1, LANES), f32),
        )
        out_specs = [row_spec, row_spec, row_spec, full_spec, half_spec, once((1, LANES))]
        scratch.append(pltpu.VMEM((1, d), f32))
    else:
        kernel = functools.partial(feed_other_kernel, *counts)
        in_specs = [row_spec, row_spec, row_spec, full_spec]
        out_shape = (
            jax.ShapeDtypeStruct((n, d), bf16),
            jax.ShapeDtypeStruct((d // 2, n), bf16),
            jax.ShapeDtypeStruct((d // 2, n), bf16),
        )
        out_specs = [row_spec, half_spec, half_spec]
    return pl.pallas_call(
        kernel,
        out_shape=out_shape + block_shapes,
        grid_spec=pltpu.PrefetchScalarGridSpec(
            num_scalar_prefetch=1,
            grid=(steps,),
            in_specs=in_specs + any_specs(sources),
            out_specs=out_specs + block_specs,
            scratch_shapes=scratch + [pltpu.SemaphoreType.DMA((len(table),))],
        ),
        compiler_params=params(FEED_VMEM),
        cost_estimate=cost(2 * n * d * width * 3, 10 * n * d, n * width // 3),
        name="feed_forward",
    )(scalars, *[keep_in_hbm(x) for x in inputs], *sources)


def mid_kernel(
    tables, counts, rows, units, s_ref, x_ref, a_ref, b_ref, g_ref, h_ref, cot_ref, gain_ref, o0_ref, o1_ref, *refs
):
    sources = [refs[: counts[0]], refs[counts[0] : sum(counts)]]
    gm_ref, do0_ref, do1_ref, dwo_ref, gain_out, buf, total, sem = refs[sum(counts) :]
    i = pl.program_id(0)

    @pl.when(i == 0)
    def _():
        for at in range(2):
            load_blocks(
                tables[at], sources[at], buf.at[pl.ds(at, 1)], s_ref[WIDE], rows, sem.at[at], buf.shape[2]
            )
        total[...] = jnp.zeros_like(total)

    _, middle, scale = mid_norm(x_ref, a_ref, b_ref)
    hat = middle * scale
    back = g_ref[...].astype(f32) + h_ref[...].astype(f32)
    tile, half_rows = x_ref.shape[0], x_ref.shape[0] * pl.num_programs(0)
    live = live_rows(s_ref, s_ref[X_HALF] * half_rows + i * tile, tile, units)
    cot = jnp.where(live, cot_ref[...].astype(f32), 0.0)
    total[...] += jnp.sum(back * hat, axis=0, keepdims=True)
    scaled = back * gain_ref[...]
    mean = jnp.mean(scaled * hat, axis=1, keepdims=True)
    grad_mid = cot + scale * (scaled - hat * mean)
    grad = grad_mid.astype(bf16)
    grad_t = grad_mid.T
    gm_ref[...] = grad_t
    grad_t = grad_t.astype(bf16)
    for at, (o_ref, do_ref) in enumerate(((o0_ref, do0_ref), (o1_ref, do1_ref))):
        do_ref[...] = mm(grad, buf[at]).astype(bf16)
        part = mm(grad_t, o_ref[...])

        @pl.when(i == 0)
        def _():
            dwo_ref[at] = part

        @pl.when(i > 0)
        def _():
            dwo_ref[at] += part

    @pl.when(i == pl.num_programs(0) - 1)
    def _():
        gain_out[...] = total[...]


def mid_backward(scalars, patches, a, b, g, h, cot, gain, o, own, other, rows, tile=512):
    n, d = a.shape
    lanes = o[0].shape[1]
    steps = n // tile
    own_spec = pl.BlockSpec((tile, d), lambda i, s: (s[X_HALF] * steps + i, 0))
    row_spec = pl.BlockSpec((tile, d), lambda i, s: (i, 0))
    head_spec = pl.BlockSpec((tile, lanes), lambda i, s: (i, 0))
    return pl.pallas_call(
        functools.partial(
            mid_kernel, (own[0], other[0]), (len(own[1]), len(other[1])), rows, 2 * n // UNIT
        ),
        out_shape=(
            jax.ShapeDtypeStruct((d, n), f32),
            jax.ShapeDtypeStruct((n, lanes), bf16),
            jax.ShapeDtypeStruct((n, lanes), bf16),
            jax.ShapeDtypeStruct((2, d, lanes), f32),
            jax.ShapeDtypeStruct((1, d), f32),
        ),
        grid_spec=pltpu.PrefetchScalarGridSpec(
            num_scalar_prefetch=1,
            grid=(steps,),
            in_specs=[own_spec, row_spec, row_spec, row_spec, row_spec, own_spec]
            + [once((1, d)), head_spec, head_spec]
            + any_specs(own[1])
            + any_specs(other[1]),
            out_specs=[
                pl.BlockSpec((d, tile), lambda i, s: (0, i)),
                head_spec,
                head_spec,
                once((2, d, lanes)),
                once((1, d)),
            ],
            scratch_shapes=[
                pltpu.VMEM((2, d, lanes), bf16),
                pltpu.VMEM((1, d), f32),
                pltpu.SemaphoreType.DMA((2, len(own[0]))),
            ],
        ),
        compiler_params=params(MID_VMEM),
        cost_estimate=cost(8 * n * d * lanes, 16 * n * d),
        name="mid_backward",
    )(scalars, *[keep_in_hbm(t) for t in (patches, a, b, g, h, cot)], gain, *o, *own[1], *other[1])


def head_back_kernel(
    table, n_out, rows, share, chunk, s_ref, q_ref, k_ref, v_ref, do_ref, o_ref, aux_ref, dwo_ref, normed_ref, *refs
):
    dq_out, dk_out, dv_out = refs[:3]
    targets = refs[3 : 3 + n_out]
    normed, dq_buf, dk_buf, dv_buf, pack, sem = refs[3 + n_out :]
    heads = head_list(share)
    lane, first, second = lane_halves()
    in_first = lane < HEAD_DIM
    n, n_q = dk_buf.shape[0], dq_buf.shape[0]
    units = n // UNIT
    load = pltpu.make_async_copy(normed_ref, normed, sem.at[0])
    load.start()
    minus = [
        -((lane >= 64) & (lane < 67)).astype(f32).astype(bf16),
        -(lane < 3).astype(f32).astype(bf16),
    ]
    masks = [key_mask(s_ref, u, lane, units).astype(bf16) for u in range(units)]
    for pair in range(q_ref.shape[1] // LANES):
        members = [side for p, side in heads if p == pair]
        lanes = slice(pair * LANES, (pair + 1) * LANES)
        q, aux, do = q_ref[:, lanes], aux_ref[:, lanes], do_ref[:, lanes]
        product = do.astype(f32) * o_ref[:, lanes].astype(f32)
        features = jnp.zeros(q.shape, f32)
        for side in members:
            inside = ~in_first if side else in_first
            row_sum = jnp.sum(jnp.where(inside, product, 0.0), axis=1, keepdims=True)
            for j, value in enumerate(split3(row_sum)):
                features = jnp.where(lane == (j if side else 64 + j), value, features)
        features = features.astype(bf16)
        sides = [(second, first) if side else (first, second) for side in members]
        q_own = [q * own for own, _ in sides]
        do_own = [do * own for own, _ in sides]
        queries = [part + aux * rest for part, (_, rest) in zip(q_own, sides)]
        grads = [part + features * rest for part, (_, rest) in zip(do_own, sides)]
        q_own, do_own = jnp.concatenate(q_own, axis=0), jnp.concatenate(do_own, axis=0)
        dq = None
        for c in range(0, n, chunk):
            k, v = k_ref[c : c + chunk, lanes], v_ref[c : c + chunk, lanes]
            mask = masks[c // UNIT]
            probs, backs, k_own = [], [], []
            for j, side in enumerate(members):
                own, rest = sides[j]
                k_own.append(k * own)
                p = jnp.exp(mm(k_own[j] + mask * rest, queries[j], NT))
                backs.append((p * mm(v * own + minus[side], grads[j], NT)).astype(bf16))
                probs.append(p.astype(bf16))
            part = mm(jnp.concatenate(k_own, axis=0).T, jnp.concatenate(backs, axis=0))
            dq = part if dq is None else dq + part
            dv_buf[c : c + chunk, lanes] = mm(jnp.concatenate(probs, axis=1), do_own).astype(bf16)
            dk_buf[c : c + chunk, lanes] = mm(jnp.concatenate(backs, axis=1), q_own).astype(bf16)
        dq_buf[:, lanes] = dq.T.astype(bf16)
    copies = start_all(
        [
            pltpu.make_async_copy(source, to, sem.at[1 + at])
            for at, (source, to) in enumerate(((dq_buf, dq_out), (dk_buf, dk_out), (dv_buf, dv_out)))
        ]
    )
    load.wait()
    pack[0, :, 0:share] = dwo_ref[0, :, 0:share]
    mine = normed[block_rows(s_ref[X_HALF], n_q, UNIT), :]
    pack[0, :, share : 2 * share] = mm(mine, dq_buf[...], TN)[:, 0:share]
    both = mm(normed[...], jnp.concatenate([dk_buf[...], dv_buf[...]], axis=1), TN)
    pack[0, :, 2 * share : 3 * share] = both[:, 0:share]
    pack[0, :, 3 * share : 4 * share] = both[:, dk_buf.shape[1] : dk_buf.shape[1] + share]
    store_blocks(table, pack, targets, s_ref[WIDE], rows)
    wait_all(copies)


def head_backward(scalars, q, k, v, do, o, aux, dwo, which, normed, out, rows, share, chunk=512):
    n, d = normed.shape
    n_q, lanes = q.shape
    out_table, out_leads = out
    shapes = [(n_q, lanes), (n, lanes), (n, lanes)]
    blocks = [(lead, rows, 4 * share) for lead in out_leads]
    q_spec, k_spec = once((n_q, lanes)), once((n, lanes))
    any_spec = pl.BlockSpec(memory_space=pl.ANY)
    return pl.pallas_call(
        functools.partial(head_back_kernel, out_table, len(blocks), rows, share, chunk),
        out_shape=tuple(jax.ShapeDtypeStruct(shape, bf16) for shape in shapes + blocks),
        grid_spec=pltpu.PrefetchScalarGridSpec(
            num_scalar_prefetch=1,
            grid=(1,),
            in_specs=[q_spec, k_spec, k_spec, q_spec, q_spec, q_spec]
            + [
                pl.BlockSpec((1, d, lanes), lambda i, s: (which, 0, 0), pipeline_mode=pl.Buffered(1)),
                any_spec,
            ],
            out_specs=[any_spec] * 3 + [once(block) for block in blocks],
            scratch_shapes=[pltpu.VMEM((n, d), bf16)]
            + [pltpu.VMEM(shape, bf16) for shape in shapes]
            + [pltpu.VMEM((1, d, 4 * share), f32), pltpu.SemaphoreType.DMA((4,))],
        ),
        compiler_params=params(BACK_VMEM),
        cost_estimate=cost(20 * n * n * share, 8 * n * d, n * n * share // 128),
        name="head_backward",
    )(scalars, *[keep_in_hbm(t) for t in (q, k, v, do, o, aux, dwo)], normed)


def last_kernel(tables, counts, rows, share, s_ref, x_ref, gain_ref, gm_ref, *refs):
    grads = refs[:6]
    refs = refs[6:]
    sources = [refs[: counts[0]], refs[counts[0] : sum(counts)]]
    keep_ref, send_ref, gain_out, buf, weights, total, gain, sem = refs[sum(counts) :]
    i = pl.program_id(0)
    half = pl.num_programs(0) // 2
    d = x_ref.shape[1]

    @pl.when(i == 0)
    def _():
        for at in range(2):
            load_blocks(tables[at], sources[at], buf.at[pl.ds(at, 1)], s_ref[WIDE], rows, sem.at[at])
        for at in range(2):
            for j in range(3):
                weights[3 * at + j] = padded(
                    buf[at, :, (j + 1) * share : (j + 2) * share], weights.shape[2]
                )
        total[...] = jnp.zeros_like(total)
        gain[...] = jnp.broadcast_to(gain_ref[...], (LANES, d)).T[:, :1]

    mine = i // half == s_ref[X_HALF]
    x = x_ref[...].T.astype(f32)
    scale = lax.rsqrt(jnp.mean(x * x, axis=0, keepdims=True) + epsilon)
    hat = x * scale
    back = None
    for at in range(2):
        for j in range(3):
            value = grads[3 * at + j][...]
            if j == 0:
                value = jnp.where(mine, value.astype(f32), 0.0).astype(bf16)
            part = mm(weights[3 * at + j], value, NT)
            back = part if back is None else back + part
    total[...] += jnp.sum(back * hat, axis=1, keepdims=True)
    scaled = back * gain[...]
    mean = jnp.mean(scaled * hat, axis=0, keepdims=True)
    grad = scale * (scaled - hat * mean) + jnp.where(mine, 0.5, 0.0) * gm_ref[...]
    store_quarters(s_ref[NARROW], grad, keep_ref, send_ref)

    @pl.when(i == pl.num_programs(0) - 1)
    def _():
        gain_out[...] = jnp.broadcast_to(total[...], (d, LANES)).T[:1, :]


def last_backward(scalars, patches, gain, gm_t, grads, own, other, rows, share, tile=512):
    n, d = patches.shape
    width = own[1][0].shape[-1]
    lanes = grads[0].shape[1]
    steps = n // tile
    half = steps // 2
    key_spec = pl.BlockSpec((tile, lanes), lambda i, s: (i, 0))
    own_spec = pl.BlockSpec((tile, lanes), lambda i, s: (own_tile(i, s, half), 0))
    half_spec = pl.BlockSpec((d // 2, tile), lambda i, s: (0, i))
    return pl.pallas_call(
        functools.partial(last_kernel, (own[0], other[0]), (len(own[1]), len(other[1])), rows, share),
        out_shape=(
            jax.ShapeDtypeStruct((d // 2, n), bf16),
            jax.ShapeDtypeStruct((d // 2, n), bf16),
            jax.ShapeDtypeStruct((1, d), f32),
        ),
        grid_spec=pltpu.PrefetchScalarGridSpec(
            num_scalar_prefetch=1,
            grid=(steps,),
            in_specs=[
                pl.BlockSpec((tile, d), lambda i, s: (i, 0)),
                once((1, d)),
                pl.BlockSpec((d, tile), lambda i, s: (0, own_tile(i, s, half))),
            ]
            + [own_spec, key_spec, key_spec] * 2
            + any_specs(own[1])
            + any_specs(other[1]),
            out_specs=[half_spec, half_spec, once((1, d))],
            scratch_shapes=[
                pltpu.VMEM((2, d, width), bf16),
                pltpu.VMEM((6, d, lanes), bf16),
                pltpu.VMEM((d, 1), f32),
                pltpu.VMEM((d, 1), f32),
                pltpu.SemaphoreType.DMA((2, len(own[0]))),
            ],
        ),
        compiler_params=params(LAST_VMEM),
        cost_estimate=cost(2 * n * d * lanes * 5, 10 * n * d),
        name="last_backward",
    )(scalars, patches, gain, gm_t, *grads, *own[1], *other[1])


def swap_core(value):
    return lax.ppermute(value, "narrow", [(i, i ^ 1) for i in range(4)])


def swap_x(value):
    return lax.ppermute(value, "narrow", [(i, i ^ 2) for i in range(4)])


def swap_wide(value, offset):
    n = lax.axis_size("wide")
    return lax.ppermute(value, "wide", [(i, i ^ offset) for i in range(n)])


def after(value, *others):
    return lax.optimization_barrier((value,) + others)[0]


def small_slice():
    return lax.axis_size("wide") == 8


def along_z(first, second, half, flip):
    return [(first, 0, half, flip)] + [(second, z - 1, half, 2 * z + flip) for z in (1, 2, 3)]


OWN_TABLE = along_z(0, 1, 0, 0) + along_z(2, 3, 0, 1)
OTHER_TABLE = along_z(0, 1, 0, 0) + along_z(2, 3, 0, 1)
CORNER = ((2, 0, 1), (3, 0, 3), (3, 1, 5), (4, 0, 7))
FF_TABLE = along_z(0, 1, 0, 0) + [(src, lead, 0, offset) for src, lead, offset in CORNER]
FLAT_TABLE = [(0, r, 0, r) for r in range(8)]
COLUMN_TABLE = [(0, z, 0, 2 * z) for z in range(4)] + [(1, z, 0, 2 * z + 1) for z in range(4)]
FF_COLUMN_TABLE = (
    [(0, z, 0, 2 * z) for z in range(4)]
    + [(1, z, 0, 2 * z + 1) for z in range(2)]
    + [(2, z, 0, 2 * z + 5) for z in range(2)]
)
ACROSS_TABLE = (
    [(0, z, 0, 2 * z) for z in range(2)]
    + [(1, z, 0, 2 * z + 4) for z in range(2)]
    + [(2, z, 0, 2 * z + 1) for z in range(2)]
    + [(3, z, 0, 2 * z + 5) for z in range(2)]
)
WHOLE_TABLE = [(0, 0, 0, 0)]


def gather_whole(shard):
    full = lax.all_gather(shard, "wide", axis=0, tiled=True)[None]
    return full, swap_x(full)


def total(*terms):
    return functools.reduce(jnp.add, [t.astype(f32) for t in terms])


def sum_all(value):
    if not small_slice():
        return lax.psum(value, ("wide", "narrow"))
    value = value + swap_core(value)
    value = value + swap_x(value)
    for offset in (1, 2, 4):
        value = value + swap_wide(value, offset)
    return value


def reduce_whole(part):
    return lax.psum_scatter(part, "wide", scatter_dimension=0, tiled=True).astype(f32)


def body(
    patches,
    norm_gain_attn,
    norm_gain_mlp,
    w_query,
    w_key,
    w_value,
    w_out,
    w_gate,
    w_up,
    w_down,
    cotangent,
    item_slots,
    valid_counts,
):
    rows, d = patches.shape
    share = w_query.shape[1]
    ff = w_gate.shape[1]
    half_rows = rows // 2
    quarter = d // 4
    small = small_slice()
    narrow = lax.axis_index("narrow")
    wide = lax.axis_index("wide")
    x_half = narrow // 2
    scalars = jnp.concatenate(
        [jnp.stack([x_half, wide if small else 0 * wide, narrow]), item_slots, valid_counts]
    ).astype(jnp.int32)
    gain_in, gain_mid = norm_gain_attn[None, :], norm_gain_mlp[None, :]

    def own_units(counts):
        units = half_rows // UNIT
        mine = lax.dynamic_slice_in_dim(counts, x_half * units, units)
        return (mine[:, None] + jnp.zeros((1, UNIT), jnp.int32)).reshape(1, half_rows)

    position = x_half * half_rows + jnp.arange(half_rows, dtype=jnp.int32)[None, :]
    live_own = (position & (own_units(item_slots) - 1)) < own_units(valid_counts)
    live_count = 0.5 * jnp.sum(live_own.astype(f32))

    head_shard = jnp.concatenate([w_out.T, w_query, w_key, w_value], axis=1)[None]
    ff_shard = jnp.concatenate([w_gate, w_up, w_down.T], axis=1)[None]
    if small:
        block = head_shard.shape[1]
        first = [swap_wide(head_shard, 2 * z) for z in (1, 2, 3)]
        first += [swap_wide(head_shard, 1), swap_x(head_shard)]
        ff_early = after(ff_shard, head_shard)
        first += [swap_wide(ff_early, 1), swap_x(ff_early)]
        z1, z2, z4, y0, x0, ff_y0, ff_x0 = lax.optimization_barrier(first)
        z3 = jnp.concatenate([z1, z2, z4])
        y3, x3 = swap_wide(z3, 1), swap_x(z3)
        corner = swap_wide(x0, 1)
        own = (OWN_TABLE, [head_shard, z3, y0, y3])
        other = (OTHER_TABLE, [x0, x3, corner, swap_x(y3)])
        ff_late = after(ff_shard, z3)
        ff_z = [swap_wide(ff_late, 2 * z) for z in (1, 2, 3)]
        early = (y3, corner)
        own_out = (COLUMN_TABLE, (4, 4))
        other_out = (FLAT_TABLE, (8,))
        ff_out = (FF_COLUMN_TABLE, (4, 2, 2))
        across_out = (ACROSS_TABLE, (2, 2, 2, 2))
    else:
        block = d
        own, other = [(WHOLE_TABLE, [full]) for full in gather_whole(head_shard[0])]
        ff_own_weights, ff_other_weights = [(WHOLE_TABLE, [full]) for full in gather_whole(ff_shard[0])]
        own_out = other_out = ff_out = across_out = (WHOLE_TABLE, (1,))
        early = ()

    values = after(patches, scalars, gain_in, gain_mid, live_own, live_count, *early)
    normed, q0, k0, v0, o0, aux0 = head_forward(scalars, values, gain_in, [own], block, share, True)
    normed = after(normed, o0)
    if small:
        *ff_z, normed = lax.optimization_barrier((*ff_z, normed))
        ff_z3 = jnp.concatenate(ff_z)
        ff_z3, normed = lax.optimization_barrier((ff_z3, normed))
        ff_y3, ff_x3 = swap_wide(ff_z3, 1), swap_x(ff_z3)
        ff_own_weights = (OWN_TABLE, [ff_shard, ff_z3, ff_y0, ff_y3])
    q1, k1, v1, o1, aux1, attn_part = head_forward(
        scalars, normed, gain_in, [other, own], block, share, False, before=o0
    )
    if small:
        ff_y3, ff_x3, ff_x0, attn_part = lax.optimization_barrier((ff_y3, ff_x3, ff_x0, attn_part))
        ff_own_weights[1][3] = ff_y3
        corner = [swap_wide(ff_x0, 1), swap_x(ff_y3[:2]), swap_wide(ff_x3[2:], 1)]
        ff_other_weights = (FF_TABLE, [ff_x0, ff_x3, *corner])
    attn_other = swap_core(attn_part)
    normed_mid, grad_mlp, back_own, mlp_own, mid_keep, attn_square, *ff_own_grads = feed_forward(
        scalars, (values, attn_part, attn_other, cotangent, gain_mid), ff_own_weights, block, ff_out, True
    )
    back_part, mlp_keep, mlp_send, *ff_other_grads = feed_forward(
        scalars, (normed_mid, grad_mlp, back_own, mlp_own), ff_other_weights, block, across_out, False
    )
    back_other = swap_core(back_part)
    if small:
        column, to_y, early_y = ff_own_grads
        early_x, to_x, corner_x, corner_y = ff_other_grads
        got_early_y = swap_wide(early_y, 1)
        got_x, got_y = swap_x(corner_x), swap_wide(corner_y, 1)
        got_early_x = swap_x(after(early_x, back_other))
    gm_t, do0, do1, dwo, gain_mid_sum = mid_backward(
        scalars, values, attn_part, attn_other, back_part, back_other, cotangent, gain_mid,
        (o0, o1), own, other, block,
    )
    if small:
        got_x, got_y, to_x, to_y = lax.optimization_barrier((got_x, got_y, to_x, to_y, do1))[:4]
        to_y, to_x = total(to_y, got_x).astype(bf16), total(to_x, got_y).astype(bf16)
        got_y, got_x = swap_wide(to_y, 1), swap_x(to_x)
        do1 = after(do1, to_y, to_x)
    *grads1, head1 = head_backward(
        scalars, q1, k1, v1, do1, o1, aux1, dwo, 1, normed, other_out, block, share
    )

    mlp = total(mlp_keep, after(swap_core(after(mlp_send, do1)), head1))
    layer = jnp.where(live_own, mid_keep + mlp, 0.0)
    layer16 = layer.astype(bf16)
    mlp_square = jnp.sum(jnp.where(live_own, mlp * mlp, 0.0))
    layer_square = jnp.sum(layer * layer)
    stats = jnp.stack([mlp_square, layer_square, live_count])[None]
    stats = jnp.concatenate(
        [0.5 * gain_mid_sum, 0.5 * attn_square[:, :1], jnp.pad(stats, ((0, 0), (0, LANES - 4)))],
        axis=1,
    )

    head1_other = swap_x(head1)
    layer_mine, layer_sent = layer16[:quarter], layer16[quarter:]
    do0, stats, layer_mine, layer_sent = lax.optimization_barrier(
        (do0, stats, layer_mine, layer_sent, head1)
    )[:4]
    layer_got = swap_x(layer_sent)
    if small:
        got_x, got_y, got_early_x, got_early_y = lax.optimization_barrier(
            (got_x, got_y, got_early_x, got_early_y, head1)
        )[:4]
        column = total(
            column, jnp.concatenate([got_y, got_early_y]), jnp.concatenate([got_early_x, got_x])
        )
        sent = [column[z].astype(bf16) for z in (1, 2, 3)]
        do0 = after(do0, *sent)
        back = [swap_wide(sent[z - 1], 2 * z) for z in (1, 2, 3)]
    *grads0, head0, head0_y = head_backward(
        scalars, q0, k0, v0, do0, o0, aux0, dwo, 0, normed, own_out, block, share
    ) + (() if small else (None,))
    dq0, head1_other = lax.optimization_barrier((grads0[0], head1_other))
    if small:
        head_y = total(head0_y, head1_other[1::2]).astype(bf16)
        dq0, head_y, *back = lax.optimization_barrier((dq0, head_y, *back))
        head_y = swap_wide(head_y, 1)
    grad_keep, grad_send, gain_in_sum = last_backward(
        scalars, values, gain_in, gm_t, [dq0, *grads0[1:], *grads1], own, other, block, share
    )

    if small:
        grad_keep, grad_send, gain_in_sum, head_y, layer_got = lax.optimization_barrier(
            (grad_keep, grad_send, gain_in_sum, head_y, layer_got)
        )
    grad_got = swap_core(grad_send)
    grad_sent = total(grad_keep[quarter:], grad_got[quarter:]).astype(bf16)
    if small:
        head_column = total(head0, head1_other[::2], head_y)
        head_sent = [head_column[z].astype(bf16) for z in (1, 2, 3)]
        gain_in_sum, grad_sent = lax.optimization_barrier(
            (gain_in_sum, grad_sent, *head_sent)
        )[:2]
        head_got = [swap_wide(head_sent[z - 1], 2 * z) for z in (1, 2, 3)]
        ff_own = total(column[0], *back)
    else:
        both = total(ff_own_grads[0][0], swap_x(ff_other_grads[0][0])).astype(bf16)
        ff_own = reduce_whole(both)
        head_own = reduce_whole(total(head0[0], head1_other[0]).astype(bf16))
    output = jnp.where(
        x_half == 0,
        jnp.concatenate([layer_mine, layer_got], axis=1),
        jnp.concatenate([layer_got, layer_mine], axis=1),
    )
    grad_patches = total(grad_keep[:quarter], grad_got[:quarter], swap_x(grad_sent))

    sums = sum_all(jnp.concatenate([gain_in_sum, stats], axis=1))
    if small:
        sums, *head_got = lax.optimization_barrier((sums, *head_got))
        head_own = total(head_column[0], *head_got)
    sums = sums[0]
    total_in, total_mid, totals = sums[:d], sums[d : 2 * d], sums[2 * d : 2 * d + 4]
    rms_values = jnp.sqrt(totals[:3] / (totals[3] * d))
    return (
        output.T,
        grad_patches.T,
        total_in,
        total_mid,
        head_own[:, share : 2 * share],
        head_own[:, 2 * share : 3 * share],
        head_own[:, 3 * share :],
        head_own[:, :share].T,
        ff_own[:, :ff],
        ff_own[:, ff : 2 * ff],
        ff_own[:, 2 * ff :].T,
        rms_values,
    )


def solution(mesh):
    return jax.shard_map(
        body,
        mesh=mesh,
        in_specs=(
            P("wide", None),
            P(),
            P(),
            P("wide", "narrow"),
            P("wide", "narrow"),
            P("wide", "narrow"),
            P("narrow", "wide"),
            P("wide", "narrow"),
            P("wide", "narrow"),
            P("narrow", "wide"),
            P("wide", None),
            P("wide"),
            P("wide"),
        ),
        out_specs=(
            P("wide", "narrow"),
            P("wide", "narrow"),
            P(),
            P(),
            P("wide", "narrow"),
            P("wide", "narrow"),
            P("wide", "narrow"),
            P("narrow", "wide"),
            P("wide", "narrow"),
            P("wide", "narrow"),
            P("narrow", "wide"),
            P(),
        ),
        check_vma=False,
    )
```

```python
import functools

import jax
import jax.numpy as jnp
from jax import lax
from jax.experimental import pallas as pl
from jax.experimental.pallas import tpu as pltpu
from jax.sharding import PartitionSpec as P

f32 = jnp.float32
bf16 = jnp.bfloat16
HEAD_DIM = 64
UNIT = 512
LANES = 128
epsilon = 1e-06
BIG = 1e30
GELU_C = 0.7978845608028654
GELU_A = 0.044715
HEAD_VMEM, FEED_VMEM, MID_VMEM, BACK_VMEM, LAST_VMEM = 24, 40, 40, 40, 40

NT = (((1,), (1,)), ((), ()))
NN = (((1,), (0,)), ((), ()))
TN = (((0,), (0,)), ((), ()))


def mm(a, b, dims=NN):
    return lax.dot_general(a, b, dims, preferred_element_type=f32)


def split3(v):
    high = v.astype(bf16)
    rest = v - high.astype(f32)
    middle = rest.astype(bf16)
    low = (rest - middle.astype(f32)).astype(bf16)
    return high.astype(f32), middle.astype(f32), low.astype(f32)


def lane_halves():
    lane = lax.broadcasted_iota(jnp.int32, (1, LANES), 1)
    first = (lane < HEAD_DIM).astype(f32)
    return lane, first.astype(bf16), (1.0 - first).astype(bf16)


def block_rows(index, rows, step):
    return pl.ds(pl.multiple_of(index * rows, step), rows)


def block_copies(table, sources, target, wide_index, rows, sem, columns=None):
    step = 16 if rows % 16 == 0 else 8
    copies = []
    for k, (src, lead, half, offset) in enumerate(table):
        source = sources[src].at[lead]
        if columns is not None:
            source = source.at[:, pl.ds(0, columns)]
        copies.append(
            pltpu.make_async_copy(
                source, target.at[half, block_rows(wide_index ^ offset, rows, step), :], sem.at[k]
            )
        )
    return copies


def start_all(copies):
    for copy in copies:
        copy.start()
    return copies


def wait_all(copies):
    for copy in copies:
        copy.wait()


def load_blocks(*args):
    wait_all(start_all(block_copies(*args)))


def store_blocks(table, acc, targets, wide_index, rows):
    for src, lead, half, offset in table:
        targets[src][lead] = acc[half, block_rows(wide_index ^ offset, rows, 8), :].astype(bf16)


def padded(weights, width):
    return jnp.concatenate(
        [weights, jnp.zeros((weights.shape[0], width - weights.shape[1]), weights.dtype)], axis=1
    )


X_HALF, WIDE, NARROW, ITEMS = 0, 1, 2, 3


def unit_item(s_ref, unit, units):
    start = (unit * UNIT) & -s_ref[ITEMS + unit]
    return start, s_ref[ITEMS + units + unit]


def live_rows(s_ref, first, tile, units):
    start, valid = unit_item(s_ref, first // UNIT, units)
    return first - start + lax.broadcasted_iota(jnp.int32, (tile, 1), 0) < valid


def query_mask(s_ref, first, lane, units):
    start, _ = unit_item(s_ref, first // UNIT, units)
    column = lane & (HEAD_DIM - 1)
    named = (column < units) & (column != start // UNIT)
    return jnp.where(named | (column == units), 1.0, 0.0)


def key_mask(s_ref, unit, lane, units):
    start, valid = unit_item(s_ref, unit, units)
    column = lane & (HEAD_DIM - 1)
    row = unit * UNIT - start + lax.broadcasted_iota(jnp.int32, (UNIT, 1), 0)
    fixed = jnp.where(column == start // UNIT, -BIG, 0.0)
    fixed = jnp.where((column > units) & (column < units + 4), -1.0, fixed)
    return jnp.where((column == units) & (row >= valid), -BIG, fixed)


def any_specs(arrays):
    return [pl.BlockSpec(memory_space=pltpu.HBM)] * len(arrays)


def own_tile(i, s, half):
    return jnp.clip(i - s[0] * half, 0, half - 1)


def keep_in_hbm(value):
    return pltpu.with_memory_space_constraint(value, pltpu.HBM)


def params(mebibytes):
    return pltpu.CompilerParams(vmem_limit_bytes=mebibytes << 20)


def cost(flops, moved, exps=0):
    return pl.CostEstimate(flops=flops, bytes_accessed=moved, transcendentals=exps)


def once(shape):
    return pl.BlockSpec(shape, lambda *_: (0,) * len(shape), pipeline_mode=pl.Buffered(1))


def head_list(share):
    return [(h // 2, h % 2) for h in range(share // HEAD_DIM)]


def head_lanes(share):
    return -(-share // LANES) * LANES


def head_kernel(
    tables, counts, rows, share, first_shard, sub, chunk, s_ref, x_ref, gain_ref, *refs
):
    heads = head_list(share)
    lane, first, second = lane_halves()
    final = len(tables) == 2
    if final:
        before_ref, refs = refs[0], refs[1:]
    sources = [refs[: counts[0]], refs[counts[0] : sum(counts)]]
    refs = refs[sum(counts) :]
    if first_shard:
        normed_out, refs = refs[0], refs[1:]
    q_out, k_out, v_out, o_ref, aux_ref = refs[:5]
    refs = refs[5:]
    if final:
        part_ref, refs = refs[0], refs[1:]
    buf, weights, values_in, normed, qs, ks, vs, keys, values, sem, in_sem, out_sem = refs[:12]
    n, d = normed.shape
    n_q = qs.shape[0]
    units = n // UNIT
    loads = start_all(block_copies(tables[0], sources[0], buf, s_ref[WIDE], rows, sem.at[0]))
    target = values_in if first_shard else normed
    unit_rows = [slice(u * UNIT, (u + 1) * UNIT) for u in range(units)]
    inputs = start_all(
        [
            pltpu.make_async_copy(x_ref.at[here, :], target.at[here, :], in_sem.at[u])
            for u, here in enumerate(unit_rows)
        ]
    )
    if final:
        other = start_all(
            block_copies(tables[1], sources[1], refs[12], s_ref[WIDE], rows, sem.at[1], refs[12].shape[2])
        )
    wait_all(loads)
    for at in range(3):
        weights[at] = padded(buf[0, :, (at + 1) * share : (at + 2) * share], weights.shape[2])
    outputs = []

    def send(source, to):
        copy = pltpu.make_async_copy(source, to, out_sem.at[len(outputs)])
        copy.start()
        outputs.append(copy)

    ones = [(lane == 64).astype(f32).astype(bf16), (lane == 0).astype(f32).astype(bf16)]
    for u, here in enumerate(unit_rows):
        inputs[u].wait()
        if first_shard:
            x = values_in[here, :].astype(f32)
            scale = lax.rsqrt(jnp.mean(x * x, axis=1, keepdims=True) + epsilon)
            normed[here, :] = (x * scale * gain_ref[...]).astype(bf16)
            send(normed.at[here, :], normed_out.at[here, :])
        rows_in = normed[here, :]
        k = mm(rows_in, weights[1]).astype(bf16)
        v = mm(rows_in, weights[2]).astype(bf16)
        ks[here, :] = k
        vs[here, :] = v
        mask = key_mask(s_ref, u, lane, units).astype(bf16)
        for at, (pair, side) in enumerate(heads):
            lanes = slice(pair * LANES, (pair + 1) * LANES)
            own, rest = (second, first) if side else (first, second)
            keys[at, here, :] = k[:, lanes] * own + mask * rest
            values[at, here, :] = v[:, lanes] * own + ones[side]
    send(ks, k_out)
    send(vs, v_out)
    qs[...] = mm(normed[block_rows(s_ref[X_HALF], n_q, UNIT), :], weights[0]).astype(bf16)
    send(qs, q_out)

    jobs = [(r, at) for r in range(0, n_q, sub) for at in range(len(heads))]
    marks = {
        r: query_mask(s_ref, s_ref[X_HALF] * n_q + r, lane, units) for r in range(0, n_q, sub)
    }

    def scores(job):
        r, at = job
        pair, side = heads[at]
        own, rest = (second, first) if side else (first, second)
        query = qs[r : r + sub, pair * LANES : (pair + 1) * LANES] * own + marks[r].astype(bf16) * rest
        return [lambda c=c: mm(query, keys[at, c : c + chunk, :], NT) for c in range(0, n, chunk)]

    outs, sums = {}, {}
    current = [f() for f in scores(jobs[0])]
    for j, (r, at) in enumerate(jobs):
        ahead = scores(jobs[j + 1]) if j + 1 < len(jobs) else []
        following = []
        top = functools.reduce(jnp.maximum, [jnp.max(s, axis=1, keepdims=True) for s in current])
        mixed = None
        for i, s in enumerate(current):
            if ahead:
                following.append(ahead[i]())
            part = mm(jnp.exp(s - top).astype(bf16), values[at, i * chunk : (i + 1) * chunk, :])
            mixed = part if mixed is None else mixed + part
        pair, side = heads[at]
        row_sum = mixed[:, 0:1] if side else mixed[:, HEAD_DIM : HEAD_DIM + 1]
        outs[side] = mixed / row_sum
        sums[side] = top + jnp.log(row_sum)
        current = following
        if side == 0 and (pair, 1) in heads:
            continue
        here, lanes = slice(r, r + sub), slice(pair * LANES, (pair + 1) * LANES)
        features = jnp.broadcast_to(marks[r], (sub, LANES))
        for which, value in sums.items():
            for i, piece in enumerate(split3(value)):
                features = jnp.where(lane == (units + 1 if which else 64 + units + 1) + i, piece, features)
        aux_ref[here, lanes] = features.astype(bf16)
        right = outs[1] if 1 in outs else 0.0
        o_ref[here, lanes] = jnp.where(lane < HEAD_DIM, outs[0], right).astype(bf16)
        outs, sums = {}, {}
    if final:
        wait_all(other)
        lanes = o_ref.shape[1]
        part = mm(before_ref[...], refs[12][0], NT) + mm(o_ref[...], buf[0, :, :lanes], NT)
        part_ref[...] = part.astype(bf16)
    wait_all(outputs)


def head_forward(scalars, values, gain, weights, rows, share, first_shard, before=None, sub=256, chunk=512):
    n, d = values.shape
    lanes = head_lanes(share)
    heads = share // HEAD_DIM
    tables, sources = [weights[0][0]], [weights[0][1]]
    args = [scalars, values, gain]
    in_specs = [pl.BlockSpec(memory_space=pl.ANY), once((1, d))]
    width = sources[0][0].shape[-1]
    q_shape, k_shape = (n // 2, lanes), (n, lanes)
    shapes = [q_shape, k_shape, k_shape, q_shape, q_shape]
    if first_shard:
        shapes = [(n, d)] + shapes
    out_specs = [pl.BlockSpec(memory_space=pltpu.HBM)] * (len(shapes) - 2) + [once(q_shape)] * 2
    scratch = [
        pltpu.VMEM((1, d, width), bf16),
        pltpu.VMEM((3, d, lanes), bf16),
        pltpu.VMEM((n, d) if first_shard else (16, LANES), bf16),
        pltpu.VMEM((n, d), bf16),
        pltpu.VMEM(q_shape, bf16),
        pltpu.VMEM(k_shape, bf16),
        pltpu.VMEM(k_shape, bf16),
        pltpu.VMEM((heads, n, LANES), bf16),
        pltpu.VMEM((heads, n, LANES), bf16),
        pltpu.SemaphoreType.DMA((2, len(tables[0]))),
        pltpu.SemaphoreType.DMA((n // UNIT,)),
        pltpu.SemaphoreType.DMA((n // UNIT + 3,)),
    ]
    if before is not None:
        tables.append(weights[1][0])
        sources.append(weights[1][1])
        args.append(before)
        in_specs.append(once(before.shape))
        shapes.append((n // 2, d))
        out_specs.append(once((n // 2, d)))
        scratch.append(pltpu.VMEM((1, d, lanes), bf16))
    counts = tuple(len(part) for part in sources)
    for part in sources:
        args += [keep_in_hbm(t) for t in part]
        in_specs += any_specs(part)
    return pl.pallas_call(
        functools.partial(head_kernel, tables, counts, rows, share, first_shard, sub, chunk),
        out_shape=tuple(jax.ShapeDtypeStruct(shape, bf16) for shape in shapes),
        grid_spec=pltpu.PrefetchScalarGridSpec(
            num_scalar_prefetch=1,
            grid=(1,),
            in_specs=in_specs,
            out_specs=out_specs,
            scratch_shapes=scratch,
        ),
        compiler_params=params(HEAD_VMEM),
        cost_estimate=cost(20 * n * n * share // 2, 8 * n * d, n * n * heads),
        name="head_forward",
    )(*args)


def mid_norm(x_ref, a_ref, b_ref):
    attn = a_ref[...].astype(f32) + b_ref[...].astype(f32)
    middle = x_ref[...].astype(f32) + attn
    scale = lax.rsqrt(jnp.mean(middle * middle, axis=1, keepdims=True) + epsilon)
    return attn, middle, scale


def store_quarters(narrow_index, value, keep_ref, send_ref):
    quarter = value.shape[0] // 4
    for block in range(4):
        at = narrow_index ^ block
        here = block_rows(at // 2, quarter, 16)
        piece = value[block * quarter : (block + 1) * quarter, :]

        @pl.when(at % 2 == 0)
        def _():
            keep_ref[here, :] = piece.astype(keep_ref.dtype)

        if send_ref is not None:

            @pl.when(at % 2 == 1)
            def _():
                send_ref[here, :] = piece.astype(send_ref.dtype)


def feed_half(normed, grad, buf, acc, first):
    ff = buf.shape[2] // 3
    w_gate, w_up, w_down = [buf[0, :, at * ff : (at + 1) * ff] for at in range(3)]
    gate = mm(normed, w_gate)
    up = mm(normed, w_up)
    back_hidden = mm(grad, w_down)
    square = gate * gate
    cdf = 0.5 + 0.5 * jnp.tanh(gate * (GELU_C + GELU_C * GELU_A * square))
    act = gate * cdf
    slope = cdf + act * (1.0 - cdf) * (2.0 * GELU_C + 6.0 * GELU_C * GELU_A * square)
    hidden = (act * up).astype(bf16)
    grad_gate = (back_hidden * up * slope).astype(bf16)
    grad_up = (back_hidden * act).astype(bf16)
    normed_t, grad_t = normed.T, grad.T
    for at, (left, right) in enumerate(((normed_t, grad_gate), (normed_t, grad_up), (grad_t, hidden))):
        lanes = slice(at * ff, (at + 1) * ff)
        part = mm(left, right)

        @pl.when(first)
        def _():
            acc[0, :, lanes] = part

        @pl.when(jnp.logical_not(first))
        def _():
            acc[0, :, lanes] += part

    back = mm(grad_gate, w_gate, NT) + mm(grad_up, w_up, NT)
    return back, mm(w_down, hidden, NT)


def feed_own_kernel(
    table, n_src, rows, out_table, n_out, units, s_ref, x_ref, a_ref, b_ref, cot_ref, gain_ref, *refs
):
    sources = refs[:n_src]
    normed_ref, grad_ref, back_ref, mlp_ref, mid_ref, stat_ref = refs[n_src : n_src + 6]
    targets = refs[n_src + 6 : n_src + 6 + n_out]
    buf, acc, stat, sem = refs[n_src + 6 + n_out :]
    i = pl.program_id(0)
    copies = block_copies(table, sources, buf, s_ref[WIDE], rows, sem)

    @pl.when(i == 0)
    def _():
        start_all(copies)
        stat[...] = jnp.zeros_like(stat)

    attn, middle, scale = mid_norm(x_ref, a_ref, b_ref)
    tile, half_rows = x_ref.shape[0], x_ref.shape[0] * pl.num_programs(0)
    live = live_rows(s_ref, s_ref[X_HALF] * half_rows + i * tile, tile, units)
    stat[...] += jnp.sum(jnp.where(live, attn * attn, 0.0), axis=0, keepdims=True)
    normed = (middle * scale * gain_ref[...]).astype(bf16)
    grad = jnp.where(live, cot_ref[...].astype(f32), 0.0).astype(bf16)
    normed_ref[...] = normed
    grad_ref[...] = grad
    store_quarters(s_ref[NARROW], middle.T, mid_ref, None)

    @pl.when(i == 0)
    def _():
        wait_all(copies)

    back, out = feed_half(normed, grad, buf, acc, i == 0)
    back_ref[...] = back.astype(bf16)
    mlp_ref[...] = out.astype(bf16)

    @pl.when(i == pl.num_programs(0) - 1)
    def _():
        stat_ref[...] = jnp.full(stat_ref.shape, jnp.sum(stat[...]))
        store_blocks(out_table, acc, targets, s_ref[WIDE], rows)


def feed_other_kernel(table, n_src, rows, out_table, n_out, s_ref, normed_ref, grad_ref, before_ref, mlp_ref, *refs):
    sources = refs[:n_src]
    back_ref, keep_ref, send_ref = refs[n_src : n_src + 3]
    targets = refs[n_src + 3 : n_src + 3 + n_out]
    buf, acc, sem = refs[n_src + 3 + n_out :]
    i = pl.program_id(0)

    @pl.when(i == 0)
    def _():
        load_blocks(table, sources, buf, s_ref[WIDE], rows, sem)

    back, out = feed_half(normed_ref[...], grad_ref[...], buf, acc, i == 0)
    back_ref[...] = (before_ref[...].astype(f32) + back).astype(bf16)
    store_quarters(s_ref[NARROW], mlp_ref[...].astype(f32) + out, keep_ref, send_ref)

    @pl.when(i == pl.num_programs(0) - 1)
    def _():
        store_blocks(out_table, acc, targets, s_ref[WIDE], rows)


def feed_forward(scalars, inputs, weights, rows, out, own, tile=512):
    table, sources = weights
    out_table, out_leads = out
    n, d = inputs[1].shape
    width = sources[0].shape[-1]
    steps = n // tile
    own_spec = pl.BlockSpec((tile, d), lambda i, s: (s[X_HALF] * steps + i, 0))
    row_spec = pl.BlockSpec((tile, d), lambda i, s: (i, 0))
    full_spec = pl.BlockSpec((d, tile), lambda i, s: (0, i))
    half_spec = pl.BlockSpec((d // 2, tile), lambda i, s: (0, i))
    block_specs = [once((lead, rows, width)) for lead in out_leads]
    block_shapes = tuple(jax.ShapeDtypeStruct((lead, rows, width), bf16) for lead in out_leads)
    scratch = [pltpu.VMEM((1, d, width), bf16), pltpu.VMEM((1, d, width), f32)]
    counts = (table, len(sources), rows, out_table, len(out_leads))
    if own:
        kernel = functools.partial(feed_own_kernel, *counts, 2 * n // UNIT)
        in_specs = [own_spec, row_spec, row_spec, own_spec, once((1, d))]
        out_shape = (
            jax.ShapeDtypeStruct((n, d), bf16),
            jax.ShapeDtypeStruct((n, d), bf16),
            jax.ShapeDtypeStruct((n, d), bf16),
            jax.ShapeDtypeStruct((d, n), bf16),
            jax.ShapeDtypeStruct((d // 2, n), f32),
            jax.ShapeDtypeStruct((1, LANES), f32),
        )
        out_specs = [row_spec, row_spec, row_spec, full_spec, half_spec, once((1, LANES))]
        scratch.append(pltpu.VMEM((1, d), f32))
    else:
        kernel = functools.partial(feed_other_kernel, *counts)
        in_specs = [row_spec, row_spec, row_spec, full_spec]
        out_shape = (
            jax.ShapeDtypeStruct((n, d), bf16),
            jax.ShapeDtypeStruct((d // 2, n), bf16),
            jax.ShapeDtypeStruct((d // 2, n), bf16),
        )
        out_specs = [row_spec, half_spec, half_spec]
    return pl.pallas_call(
        kernel,
        out_shape=out_shape + block_shapes,
        grid_spec=pltpu.PrefetchScalarGridSpec(
            num_scalar_prefetch=1,
            grid=(steps,),
            in_specs=in_specs + any_specs(sources),
            out_specs=out_specs + block_specs,
            scratch_shapes=scratch + [pltpu.SemaphoreType.DMA((len(table),))],
        ),
        compiler_params=params(FEED_VMEM),
        cost_estimate=cost(2 * n * d * width * 3, 10 * n * d, n * width // 3),
        name="feed_forward",
    )(scalars, *[keep_in_hbm(x) for x in (*inputs, *sources)])


def mid_kernel(
    tables, counts, rows, units, s_ref, x_ref, a_ref, b_ref, g_ref, h_ref, cot_ref, gain_ref, o0_ref, o1_ref, *refs
):
    sources = [refs[: counts[0]], refs[counts[0] : sum(counts)]]
    gm_ref, do0_ref, do1_ref, dwo_ref, gain_out, buf, total, sem = refs[sum(counts) :]
    i = pl.program_id(0)

    @pl.when(i == 0)
    def _():
        for at in range(2):
            load_blocks(
                tables[at], sources[at], buf.at[pl.ds(at, 1)], s_ref[WIDE], rows, sem.at[at], buf.shape[2]
            )
        total[...] = jnp.zeros_like(total)

    _, middle, scale = mid_norm(x_ref, a_ref, b_ref)
    hat = middle * scale
    back = g_ref[...].astype(f32) + h_ref[...].astype(f32)
    tile, half_rows = x_ref.shape[0], x_ref.shape[0] * pl.num_programs(0)
    live = live_rows(s_ref, s_ref[X_HALF] * half_rows + i * tile, tile, units)
    cot = jnp.where(live, cot_ref[...].astype(f32), 0.0)
    total[...] += jnp.sum(back * hat, axis=0, keepdims=True)
    scaled = back * gain_ref[...]
    mean = jnp.mean(scaled * hat, axis=1, keepdims=True)
    grad_mid = cot + scale * (scaled - hat * mean)
    grad = grad_mid.astype(bf16)
    grad_t = grad_mid.T
    gm_ref[...] = grad_t
    grad_t = grad_t.astype(bf16)
    for at, (o_ref, do_ref) in enumerate(((o0_ref, do0_ref), (o1_ref, do1_ref))):
        do_ref[...] = mm(grad, buf[at]).astype(bf16)
        part = mm(grad_t, o_ref[...])

        @pl.when(i == 0)
        def _():
            dwo_ref[at] = part

        @pl.when(i > 0)
        def _():
            dwo_ref[at] += part

    @pl.when(i == pl.num_programs(0) - 1)
    def _():
        gain_out[...] = total[...]


def mid_backward(scalars, patches, a, b, g, h, cot, gain, o, own, other, rows, tile=512):
    n, d = a.shape
    lanes = o[0].shape[1]
    steps = n // tile
    own_spec = pl.BlockSpec((tile, d), lambda i, s: (s[X_HALF] * steps + i, 0))
    row_spec = pl.BlockSpec((tile, d), lambda i, s: (i, 0))
    head_spec = pl.BlockSpec((tile, lanes), lambda i, s: (i, 0))
    return pl.pallas_call(
        functools.partial(
            mid_kernel, (own[0], other[0]), (len(own[1]), len(other[1])), rows, 2 * n // UNIT
        ),
        out_shape=(
            pltpu.HBM((d, n), f32),
            pltpu.HBM((n, lanes), bf16),
            jax.ShapeDtypeStruct((n, lanes), bf16),
            jax.ShapeDtypeStruct((2, d, lanes), f32),
            jax.ShapeDtypeStruct((1, d), f32),
        ),
        grid_spec=pltpu.PrefetchScalarGridSpec(
            num_scalar_prefetch=1,
            grid=(steps,),
            in_specs=[own_spec, row_spec, row_spec, row_spec, row_spec, own_spec]
            + [once((1, d)), head_spec, head_spec]
            + any_specs(own[1])
            + any_specs(other[1]),
            out_specs=[
                pl.BlockSpec((d, tile), lambda i, s: (0, i)),
                head_spec,
                head_spec,
                once((2, d, lanes)),
                once((1, d)),
            ],
            scratch_shapes=[
                pltpu.VMEM((2, d, lanes), bf16),
                pltpu.VMEM((1, d), f32),
                pltpu.SemaphoreType.DMA((2, len(own[0]))),
            ],
        ),
        compiler_params=params(MID_VMEM),
        cost_estimate=cost(8 * n * d * lanes, 16 * n * d),
        name="mid_backward",
    )(scalars, *[keep_in_hbm(t) for t in (patches, a, b, g, h, cot)], gain, *o, *[keep_in_hbm(t) for t in (*own[1], *other[1])])


def head_back_kernel(
    in_table, n_src, table, n_out, rows, share, chunk, s_ref, q_ref, k_ref, v_ref, do_ref, o_ref, aux_ref, dwo_ref, gain_ref, normed_ref, *refs
):
    sources = refs[:n_src]
    dq_out, dk_out, dv_out, gain_out = refs[n_src : n_src + 4]
    targets = refs[n_src + 4 : n_src + 4 + n_out]
    normed, dq_buf, dk_buf, dv_buf, pack, weights, sem, load_sem = refs[n_src + 4 + n_out :]
    heads = head_list(share)
    lane, first, second = lane_halves()
    in_first = lane < HEAD_DIM
    n, n_q = dk_buf.shape[0], dq_buf.shape[0]
    units = n // UNIT
    load = pltpu.make_async_copy(normed_ref, normed, sem.at[0])
    load.start()
    loads = start_all(block_copies(in_table, sources, weights, s_ref[WIDE], rows, load_sem))
    minus = [
        -((lane >= 64) & (lane < 67)).astype(f32).astype(bf16),
        -(lane < 3).astype(f32).astype(bf16),
    ]
    masks = [key_mask(s_ref, u, lane, units).astype(bf16) for u in range(units)]
    for pair in range(q_ref.shape[1] // LANES):
        members = [side for p, side in heads if p == pair]
        lanes = slice(pair * LANES, (pair + 1) * LANES)
        q, aux, do = q_ref[:, lanes], aux_ref[:, lanes], do_ref[:, lanes]
        product = do.astype(f32) * o_ref[:, lanes].astype(f32)
        features = jnp.zeros(q.shape, f32)
        for side in members:
            inside = ~in_first if side else in_first
            row_sum = jnp.sum(jnp.where(inside, product, 0.0), axis=1, keepdims=True)
            for j, value in enumerate(split3(row_sum)):
                features = jnp.where(lane == (j if side else 64 + j), value, features)
        features = features.astype(bf16)
        sides = [(second, first) if side else (first, second) for side in members]
        q_own = [q * own for own, _ in sides]
        do_own = [do * own for own, _ in sides]
        queries = [part + aux * rest for part, (_, rest) in zip(q_own, sides)]
        grads = [part + features * rest for part, (_, rest) in zip(do_own, sides)]
        q_own, do_own = jnp.concatenate(q_own, axis=0), jnp.concatenate(do_own, axis=0)
        dq = None
        for c in range(0, n, chunk):
            k, v = k_ref[c : c + chunk, lanes], v_ref[c : c + chunk, lanes]
            mask = masks[c // UNIT]
            probs, backs, k_own = [], [], []
            for j, side in enumerate(members):
                own, rest = sides[j]
                k_own.append(k * own)
                p = jnp.exp(mm(k_own[j] + mask * rest, queries[j], NT))
                backs.append((p * mm(v * own + minus[side], grads[j], NT)).astype(bf16))
                probs.append(p.astype(bf16))
            part = mm(jnp.concatenate(k_own, axis=0).T, jnp.concatenate(backs, axis=0))
            dq = part if dq is None else dq + part
            dv_buf[c : c + chunk, lanes] = mm(jnp.concatenate(probs, axis=1), do_own).astype(bf16)
            dk_buf[c : c + chunk, lanes] = mm(jnp.concatenate(backs, axis=1), q_own).astype(bf16)
        dq_buf[:, lanes] = dq.T.astype(bf16)
    copies = start_all(
        [
            pltpu.make_async_copy(source, to, sem.at[1 + at])
            for at, (source, to) in enumerate(((dq_buf, dq_out), (dk_buf, dk_out), (dv_buf, dv_out)))
        ]
    )
    load.wait()
    pack[0, :, 0:share] = dwo_ref[0, :, 0:share]
    mine = normed[block_rows(s_ref[X_HALF], n_q, UNIT), :]
    pack[0, :, share : 2 * share] = mm(mine, dq_buf[...], TN)[:, 0:share]
    both = mm(normed[...], jnp.concatenate([dk_buf[...], dv_buf[...]], axis=1), TN)
    pack[0, :, 2 * share : 3 * share] = both[:, 0:share]
    pack[0, :, 3 * share : 4 * share] = both[:, dk_buf.shape[1] : dk_buf.shape[1] + share]
    store_blocks(table, pack, targets, s_ref[WIDE], rows)
    wait_all(loads)
    product = weights[0, :, share : 4 * share].astype(f32) * pack[0, :, share : 4 * share]
    row_sum = jnp.sum(product, axis=1, keepdims=True)
    gain_out[...] = jnp.broadcast_to(row_sum, (row_sum.shape[0], LANES)).T[:1, :] / gain_ref[...]
    wait_all(copies)


def head_backward(
    scalars, q, k, v, do, o, aux, dwo, which, gain, normed, weights, out, rows, share, chunk=512
):
    n, d = normed.shape
    n_q, lanes = q.shape
    out_table, out_leads = out
    shapes = [(n_q, lanes), (n, lanes), (n, lanes)]
    blocks = [(lead, rows, 4 * share) for lead in out_leads]
    q_spec, k_spec = once((n_q, lanes)), once((n, lanes))
    any_spec = pl.BlockSpec(memory_space=pl.ANY)
    return pl.pallas_call(
        functools.partial(
            head_back_kernel, weights[0], len(weights[1]), out_table, len(blocks), rows, share, chunk
        ),
        out_shape=tuple(jax.ShapeDtypeStruct(shape, bf16) for shape in shapes)
        + (jax.ShapeDtypeStruct((1, d), f32),)
        + tuple(jax.ShapeDtypeStruct(shape, bf16) for shape in blocks),
        grid_spec=pltpu.PrefetchScalarGridSpec(
            num_scalar_prefetch=1,
            grid=(1,),
            in_specs=[q_spec, k_spec, k_spec, q_spec, q_spec, q_spec]
            + [
                pl.BlockSpec((1, d, lanes), lambda i, s: (which, 0, 0), pipeline_mode=pl.Buffered(1)),
                once((1, d)),
                any_spec,
            ]
            + any_specs(weights[1]),
            out_specs=[any_spec] * 3 + [once((1, d))] + [once(block) for block in blocks],
            scratch_shapes=[pltpu.VMEM((n, d), bf16)]
            + [pltpu.VMEM(shape, bf16) for shape in shapes]
            + [
                pltpu.VMEM((1, d, 4 * share), f32),
                pltpu.VMEM((1, d, 4 * share), bf16),
                pltpu.SemaphoreType.DMA((4,)),
                pltpu.SemaphoreType.DMA((len(weights[0]),)),
            ],
        ),
        compiler_params=params(BACK_VMEM),
        cost_estimate=cost(20 * n * n * share, 8 * n * d, n * n * share // 128),
        name="head_backward",
    )(scalars, *[keep_in_hbm(t) for t in (q, k, v)], do, o, keep_in_hbm(aux), dwo, gain, *[keep_in_hbm(t) for t in (normed, *weights[1])])


def last_kernel(tables, counts, rows, share, s_ref, x_ref, gain_ref, gm_ref, *refs):
    grads = refs[:6]
    refs = refs[6:]
    sources = [refs[: counts[0]], refs[counts[0] : sum(counts)]]
    keep_ref, send_ref, buf, weights, gain, sem = refs[sum(counts) :]
    i = pl.program_id(0)
    half = pl.num_programs(0) // 2
    d = x_ref.shape[1]

    @pl.when(i == 0)
    def _():
        for at in range(2):
            load_blocks(tables[at], sources[at], buf.at[pl.ds(at, 1)], s_ref[WIDE], rows, sem.at[at])
        for at in range(2):
            for j in range(3):
                weights[3 * at + j] = padded(
                    buf[at, :, (j + 1) * share : (j + 2) * share], weights.shape[2]
                )
        gain[...] = jnp.broadcast_to(gain_ref[...], (LANES, d)).T[:, :1]

    mine = i // half == s_ref[X_HALF]
    x = x_ref[...].T.astype(f32)
    scale = lax.rsqrt(jnp.mean(x * x, axis=0, keepdims=True) + epsilon)
    hat = x * scale
    back = None
    for at in range(2):
        for j in range(3):
            value = grads[3 * at + j][...]
            if j == 0:
                value = jnp.where(mine, value.astype(f32), 0.0).astype(bf16)
            part = mm(weights[3 * at + j], value, NT)
            back = part if back is None else back + part
    scaled = back * gain[...]
    mean = jnp.mean(scaled * hat, axis=0, keepdims=True)
    grad = scale * (scaled - hat * mean) + jnp.where(mine, 0.5, 0.0) * gm_ref[...]
    store_quarters(s_ref[NARROW], grad, keep_ref, send_ref)


def last_backward(scalars, patches, gain, gm_t, grads, own, other, rows, share, tile=512):
    n, d = patches.shape
    width = own[1][0].shape[-1]
    lanes = grads[0].shape[1]
    steps = n // tile
    half = steps // 2
    key_spec = pl.BlockSpec((tile, lanes), lambda i, s: (i, 0))
    own_spec = pl.BlockSpec((tile, lanes), lambda i, s: (own_tile(i, s, half), 0))
    half_spec = pl.BlockSpec((d // 2, tile), lambda i, s: (0, i))
    return pl.pallas_call(
        functools.partial(last_kernel, (own[0], other[0]), (len(own[1]), len(other[1])), rows, share),
        out_shape=(
            jax.ShapeDtypeStruct((d // 2, n), bf16),
            jax.ShapeDtypeStruct((d // 2, n), bf16),
        ),
        grid_spec=pltpu.PrefetchScalarGridSpec(
            num_scalar_prefetch=1,
            grid=(steps,),
            in_specs=[
                pl.BlockSpec((tile, d), lambda i, s: (i, 0)),
                once((1, d)),
                pl.BlockSpec((d, tile), lambda i, s: (0, own_tile(i, s, half))),
            ]
            + [own_spec, key_spec, key_spec] * 2
            + any_specs(own[1])
            + any_specs(other[1]),
            out_specs=[half_spec, half_spec],
            scratch_shapes=[
                pltpu.VMEM((2, d, width), bf16),
                pltpu.VMEM((6, d, lanes), bf16),
                pltpu.VMEM((d, 1), f32),
                pltpu.SemaphoreType.DMA((2, len(own[0]))),
            ],
        ),
        compiler_params=params(LAST_VMEM),
        cost_estimate=cost(2 * n * d * lanes * 5, 10 * n * d),
        name="last_backward",
    )(scalars, patches, gain, gm_t, *grads, *[keep_in_hbm(t) for t in (*own[1], *other[1])])


def swap_core(value):
    return lax.ppermute(value, "narrow", [(i, i ^ 1) for i in range(4)])


def swap_x(value):
    return lax.ppermute(value, "narrow", [(i, i ^ 2) for i in range(4)])


def swap_wide(value, offset):
    n = lax.axis_size("wide")
    return lax.ppermute(value, "wide", [(i, i ^ offset) for i in range(n)])


def after(value, *others):
    return lax.optimization_barrier((value,) + others)[0]


def small_slice():
    return lax.axis_size("wide") == 8


def along_z(first, second, half, flip):
    return [(first, 0, half, flip)] + [(second, z - 1, half, 2 * z + flip) for z in (1, 2, 3)]


OWN_TABLE = along_z(0, 1, 0, 0) + along_z(2, 3, 0, 1)
OTHER_TABLE = along_z(0, 1, 0, 0) + along_z(2, 3, 0, 1)
CORNER = ((2, 0, 1), (3, 0, 3), (3, 1, 5), (4, 0, 7))
FF_TABLE = along_z(0, 1, 0, 0) + [(src, lead, 0, offset) for src, lead, offset in CORNER]
FLAT_TABLE = [(0, r, 0, r) for r in range(8)]
COLUMN_TABLE = [(0, z, 0, 2 * z) for z in range(4)] + [(1, z, 0, 2 * z + 1) for z in range(4)]
FF_COLUMN_TABLE = (
    [(0, z, 0, 2 * z) for z in range(4)]
    + [(1, z, 0, 2 * z + 1) for z in range(2)]
    + [(2, z, 0, 2 * z + 5) for z in range(2)]
)
ACROSS_TABLE = (
    [(0, z, 0, 2 * z) for z in range(2)]
    + [(1, z, 0, 2 * z + 4) for z in range(2)]
    + [(2, z, 0, 2 * z + 1) for z in range(2)]
    + [(3, z, 0, 2 * z + 5) for z in range(2)]
)
WHOLE_TABLE = [(0, 0, 0, 0)]


def gather_whole(shard):
    full = lax.all_gather(shard, "wide", axis=0, tiled=True)[None]
    return full, swap_x(full)


def total(*terms):
    return functools.reduce(jnp.add, [t.astype(f32) for t in terms])


def reduce_whole(part):
    return lax.psum_scatter(part, "wide", scatter_dimension=0, tiled=True).astype(f32)


def body(
    patches,
    norm_gain_attn,
    norm_gain_mlp,
    w_query,
    w_key,
    w_value,
    w_out,
    w_gate,
    w_up,
    w_down,
    cotangent,
    item_slots,
    valid_counts,
):
    rows, d = patches.shape
    share = w_query.shape[1]
    ff = w_gate.shape[1]
    half_rows = rows // 2
    quarter = d // 4
    small = small_slice()
    narrow = lax.axis_index("narrow")
    wide = lax.axis_index("wide")
    x_half = narrow // 2
    scalars = jnp.concatenate(
        [jnp.stack([x_half, wide if small else 0 * wide, narrow]), item_slots, valid_counts]
    ).astype(jnp.int32)
    gain_in, gain_mid = norm_gain_attn[None, :], norm_gain_mlp[None, :]

    def own_units(counts):
        units = half_rows // UNIT
        mine = lax.dynamic_slice_in_dim(counts, x_half * units, units)
        return (mine[:, None] + jnp.zeros((1, UNIT), jnp.int32)).reshape(1, half_rows)

    position = x_half * half_rows + jnp.arange(half_rows, dtype=jnp.int32)[None, :]
    live_own = (position & (own_units(item_slots) - 1)) < own_units(valid_counts)
    live_count = 0.5 * jnp.sum(live_own.astype(f32))

    head_shard = jnp.concatenate([w_out.T, w_query, w_key, w_value], axis=1)[None]
    ff_shard = jnp.concatenate([w_gate, w_up, w_down.T], axis=1)[None]
    if small:
        block = head_shard.shape[1]
        first = [swap_wide(head_shard, 2 * z) for z in (1, 2, 3)]
        first += [swap_wide(head_shard, 1), swap_x(head_shard)]
        ff_early = after(ff_shard, head_shard)
        first += [swap_wide(ff_early, 1), swap_x(ff_early), swap_x(first[3])]
        z1, z2, z4, y0, x0, ff_y0, ff_x0, corner = lax.optimization_barrier(first)
        z3 = jnp.concatenate([z1, z2, z4])
        y3, x3 = swap_wide(z3, 1), swap_x(z3)
        own = (OWN_TABLE, [head_shard, z3, y0, y3])
        other = (OTHER_TABLE, [x0, x3, corner, swap_x(y3)])
        ff_late = after(ff_shard, z3)
        ff_z = [swap_wide(ff_late, 2 * z) for z in (1, 2, 3)]
        early = (y3,)
        own_out = (COLUMN_TABLE, (4, 4))
        other_out = (FLAT_TABLE, (8,))
        ff_out = (FF_COLUMN_TABLE, (4, 2, 2))
        across_out = (ACROSS_TABLE, (2, 2, 2, 2))
    else:
        block = d
        own, other = [(WHOLE_TABLE, [full]) for full in gather_whole(head_shard[0])]
        ff_own_weights, ff_other_weights = [(WHOLE_TABLE, [full]) for full in gather_whole(ff_shard[0])]
        own_out = other_out = ff_out = across_out = (WHOLE_TABLE, (1,))
        early = ()

    values = after(patches, scalars, gain_in, gain_mid, live_own, live_count, *early)
    normed, q0, k0, v0, o0, aux0 = head_forward(scalars, values, gain_in, [own], block, share, True)
    normed = after(normed, o0)
    if small:
        *ff_z, normed = lax.optimization_barrier((*ff_z, normed))
        ff_z3 = jnp.concatenate(ff_z)
        ff_z3, normed = lax.optimization_barrier((ff_z3, normed))
        ff_y3, ff_x3 = swap_wide(ff_z3, 1), swap_x(ff_z3)
        ff_own_weights = (OWN_TABLE, [ff_shard, ff_z3, ff_y0, ff_y3])
    q1, k1, v1, o1, aux1, attn_part = head_forward(
        scalars, normed, gain_in, [other, own], block, share, False, before=o0
    )
    if small:
        ff_y3, ff_x3, ff_x0, attn_part = lax.optimization_barrier((ff_y3, ff_x3, ff_x0, attn_part))
        ff_own_weights[1][3] = ff_y3
        corner = [swap_wide(ff_x0, 1), swap_x(ff_y3[:2]), swap_wide(ff_x3[2:], 1)]
        ff_other_weights = (FF_TABLE, [ff_x0, ff_x3, *corner])
    attn_other = swap_core(attn_part)
    normed_mid, grad_mlp, back_own, mlp_own, mid_keep, attn_square, *ff_own_grads = feed_forward(
        scalars, (values, attn_part, attn_other, cotangent, gain_mid), ff_own_weights, block, ff_out, True
    )
    back_part, mlp_keep, mlp_send, *ff_other_grads = feed_forward(
        scalars, (normed_mid, grad_mlp, back_own, mlp_own), ff_other_weights, block, across_out, False
    )
    back_other = swap_core(back_part)
    if small:
        column, to_y, early_y = ff_own_grads
        early_x, to_x, corner_x, corner_y = ff_other_grads
        got_early_y = swap_wide(early_y, 1)
        got_x, got_y = swap_x(corner_x), swap_wide(corner_y, 1)
        got_early_x = swap_x(after(early_x, back_other))
    gm_t, do0, do1, dwo, gain_mid_sum = mid_backward(
        scalars, values, attn_part, attn_other, back_part, back_other, cotangent, gain_mid,
        (o0, o1), own, other, block,
    )
    if small:
        got_x, got_y, to_x, to_y = lax.optimization_barrier((got_x, got_y, to_x, to_y, do1))[:4]
        to_y, to_x = total(to_y, got_x).astype(bf16), total(to_x, got_y).astype(bf16)
        got_y, got_x = swap_wide(to_y, 1), swap_x(to_x)
        do1 = after(do1, to_y, to_x)
    *grads1, gain1, head1 = head_backward(
        scalars, q1, k1, v1, do1, o1, aux1, dwo, 1, gain_in, normed, other, other_out, block, share
    )

    mlp = total(mlp_keep, after(swap_core(after(mlp_send, do1)), head1))
    layer = jnp.where(live_own, mid_keep + mlp, 0.0)
    layer16 = layer.astype(bf16)
    mlp_square = jnp.sum(jnp.where(live_own, mlp * mlp, 0.0))
    layer_square = jnp.sum(layer * layer)
    stats = jnp.stack([mlp_square, layer_square, live_count])[None]
    stats = jnp.concatenate(
        [0.5 * gain_mid_sum, 0.5 * attn_square[:, :1], jnp.pad(stats, ((0, 0), (0, LANES - 4)))],
        axis=1,
    )

    head1_other = swap_x(head1)
    layer_mine, layer_sent = layer16[:quarter], layer16[quarter:]
    do0, stats, layer_mine, layer_sent = lax.optimization_barrier(
        (do0, stats, layer_mine, layer_sent, head1)
    )[:4]
    layer_got = swap_x(layer_sent)
    if small:
        got_x, got_y, got_early_x, got_early_y = lax.optimization_barrier(
            (got_x, got_y, got_early_x, got_early_y, head1)
        )[:4]
        column = total(
            column, jnp.concatenate([got_y, got_early_y]), jnp.concatenate([got_early_x, got_x])
        )
        sent = [column[z].astype(bf16) for z in (1, 2, 3)]
        do0 = after(do0, *sent)
        back = [swap_wide(sent[z - 1], 2 * z) for z in (1, 2, 3)]
    *grads0, gain0, head0, head0_y = head_backward(
        scalars, q0, k0, v0, do0, o0, aux0, dwo, 0, gain_in, normed, own, own_out, block, share
    ) + (() if small else (None,))
    dq0, head1_other = lax.optimization_barrier((grads0[0], head1_other))
    if small:
        head_y = total(head0_y, head1_other[1::2]).astype(bf16)
        dq0, head_y, *back = lax.optimization_barrier((dq0, head_y, *back))
        head_y = swap_wide(head_y, 1)
    sums = jnp.concatenate([gain0 + gain1, stats], axis=1)
    if small:
        sums = sums + swap_core(sums)
        dq0, sums = lax.optimization_barrier((dq0, sums))
        sums_x = swap_x(sums)
    grad_keep, grad_send = last_backward(
        scalars, values, gain_in, gm_t, [dq0, *grads0[1:], *grads1], own, other, block, share
    )

    if small:
        grad_keep, grad_send, sums_x, head_y, layer_got = lax.optimization_barrier(
            (grad_keep, grad_send, sums_x, head_y, layer_got)
        )
        sums = sums + sums_x
        ff_own = total(column[0], *back)
    output = jnp.where(
        x_half == 0,
        jnp.concatenate([layer_mine, layer_got], axis=1),
        jnp.concatenate([layer_got, layer_mine], axis=1),
    )
    grad_got = swap_core(grad_send)
    grad_sent = total(grad_keep[quarter:], grad_got[quarter:]).astype(bf16)
    if small:
        sums = sums + swap_wide(sums, 1)
        head_column = total(head0, head1_other[::2], head_y)
        head_sent = [head_column[z].astype(bf16) for z in (1, 2, 3)]
        grad_sent, sums, *head_sent, output, ff_own = lax.optimization_barrier(
            (grad_sent, sums, *head_sent, output, ff_own)
        )
        grad_other = swap_x(grad_sent)
        head_got = [swap_wide(head_sent[z - 1], 2 * z) for z in (1, 2, 3)]
        sums_got = [swap_wide(sums, 2 * z) for z in (1, 2, 3)]
        grad_other, *got = lax.optimization_barrier((grad_other, *head_got, *sums_got))
        head_own = total(head_column[0], *got[:3])
        sums = total(sums, *got[3:])
    else:
        both = total(ff_own_grads[0][0], swap_x(ff_other_grads[0][0])).astype(bf16)
        ff_own = reduce_whole(both)
        head_own = reduce_whole(total(head0[0], head1_other[0]).astype(bf16))
        grad_other = swap_x(grad_sent)
        sums = lax.psum(sums, ("wide", "narrow"))
    grad_patches = total(grad_keep[:quarter], grad_got[:quarter], grad_other)
    sums = sums[0]
    total_in, total_mid, totals = sums[:d], sums[d : 2 * d], sums[2 * d : 2 * d + 4]
    rms_values = jnp.sqrt(totals[:3] / (totals[3] * d))
    return (
        output.T,
        grad_patches.T,
        total_in,
        total_mid,
        head_own[:, share : 2 * share],
        head_own[:, 2 * share : 3 * share],
        head_own[:, 3 * share :],
        head_own[:, :share].T,
        ff_own[:, :ff],
        ff_own[:, ff : 2 * ff],
        ff_own[:, 2 * ff :].T,
        rms_values,
    )


def solution(mesh):
    return jax.shard_map(
        body,
        mesh=mesh,
        in_specs=(
            P("wide", None),
            P(),
            P(),
            P("wide", "narrow"),
            P("wide", "narrow"),
            P("wide", "narrow"),
            P("narrow", "wide"),
            P("wide", "narrow"),
            P("wide", "narrow"),
            P("narrow", "wide"),
            P("wide", None),
            P("wide"),
            P("wide"),
        ),
        out_specs=(
            P("wide", "narrow"),
            P("wide", "narrow"),
            P(),
            P(),
            P("wide", "narrow"),
            P("wide", "narrow"),
            P("wide", "narrow"),
            P("narrow", "wide"),
            P("wide", "narrow"),
            P("wide", "narrow"),
            P("narrow", "wide"),
            P(),
        ),
        check_vma=False,
    )
```

```python
import functools

import jax
import jax.numpy as jnp
from jax import lax
from jax.experimental import pallas as pl
from jax.experimental.pallas import tpu as pltpu
from jax.sharding import PartitionSpec as P

f32 = jnp.float32
bf16 = jnp.bfloat16
HEAD_DIM = 64
UNIT = 512
LANES = 128
epsilon = 1e-06
BIG = 1e30
GELU_C = 0.7978845608028654
GELU_A = 0.044715
HEAD_VMEM, FEED_VMEM, MID_VMEM, BACK_VMEM, LAST_VMEM = 24, 40, 40, 40, 40

NT = (((1,), (1,)), ((), ()))
NN = (((1,), (0,)), ((), ()))
TN = (((0,), (0,)), ((), ()))


def mm(a, b, dims=NN):
    return lax.dot_general(a, b, dims, preferred_element_type=f32)


def split3(v):
    high = v.astype(bf16)
    rest = v - high.astype(f32)
    middle = rest.astype(bf16)
    low = (rest - middle.astype(f32)).astype(bf16)
    return high.astype(f32), middle.astype(f32), low.astype(f32)


def lane_halves():
    lane = lax.broadcasted_iota(jnp.int32, (1, LANES), 1)
    first = (lane < HEAD_DIM).astype(f32)
    return lane, first.astype(bf16), (1.0 - first).astype(bf16)


def block_rows(index, rows, step):
    return pl.ds(pl.multiple_of(index * rows, step), rows)


def block_copies(table, sources, target, wide_index, rows, sem, columns=None):
    step = 16 if rows % 16 == 0 else 8
    copies = []
    for k, (src, lead, half, offset) in enumerate(table):
        source = sources[src].at[lead]
        if columns is not None:
            source = source.at[:, pl.ds(0, columns)]
        copies.append(
            pltpu.make_async_copy(
                source, target.at[half, block_rows(wide_index ^ offset, rows, step), :], sem.at[k]
            )
        )
    return copies


def start_all(copies):
    for copy in copies:
        copy.start()
    return copies


def wait_all(copies):
    for copy in copies:
        copy.wait()


def load_blocks(*args):
    wait_all(start_all(block_copies(*args)))


def store_blocks(table, acc, targets, wide_index, rows):
    for src, lead, half, offset in table:
        targets[src][lead] = acc[half, block_rows(wide_index ^ offset, rows, 8), :].astype(bf16)


def padded(weights, width):
    return jnp.concatenate(
        [weights, jnp.zeros((weights.shape[0], width - weights.shape[1]), weights.dtype)], axis=1
    )


X_HALF, WIDE, NARROW, ITEMS = 0, 1, 2, 3


def unit_item(s_ref, unit, units):
    start = (unit * UNIT) & -s_ref[ITEMS + unit]
    return start, s_ref[ITEMS + units + unit]


def live_rows(s_ref, first, tile, units):
    start, valid = unit_item(s_ref, first // UNIT, units)
    return first - start + lax.broadcasted_iota(jnp.int32, (tile, 1), 0) < valid


def query_mask(s_ref, first, lane, units):
    start, _ = unit_item(s_ref, first // UNIT, units)
    column = lane & (HEAD_DIM - 1)
    named = (column < units) & (column != start // UNIT)
    return jnp.where(named | (column == units), 1.0, 0.0)


def key_mask(s_ref, unit, lane, units):
    start, valid = unit_item(s_ref, unit, units)
    column = lane & (HEAD_DIM - 1)
    row = unit * UNIT - start + lax.broadcasted_iota(jnp.int32, (UNIT, 1), 0)
    fixed = jnp.where(column == start // UNIT, -BIG, 0.0)
    fixed = jnp.where((column > units) & (column < units + 4), -1.0, fixed)
    return jnp.where((column == units) & (row >= valid), -BIG, fixed)


def any_specs(arrays):
    return [pl.BlockSpec(memory_space=pltpu.HBM)] * len(arrays)


def own_tile(i, s, half):
    return jnp.clip(i - s[0] * half, 0, half - 1)


def keep_in_hbm(value):
    return pltpu.with_memory_space_constraint(value, pltpu.HBM)


def params(mebibytes):
    return pltpu.CompilerParams(vmem_limit_bytes=mebibytes << 20)


def cost(flops, moved, exps=0):
    return pl.CostEstimate(flops=flops, bytes_accessed=moved, transcendentals=exps)


def once(shape):
    return pl.BlockSpec(shape, lambda *_: (0,) * len(shape), pipeline_mode=pl.Buffered(1))


def head_list(share):
    return [(h // 2, h % 2) for h in range(share // HEAD_DIM)]


def head_lanes(share):
    return -(-share // LANES) * LANES


def head_kernel(
    tables, counts, rows, share, first_shard, sub, chunk, s_ref, x_ref, gain_ref, *refs
):
    heads = head_list(share)
    lane, first, second = lane_halves()
    final = len(tables) == 2
    if final:
        before_ref, refs = refs[0], refs[1:]
    sources = [refs[: counts[0]], refs[counts[0] : sum(counts)]]
    refs = refs[sum(counts) :]
    if first_shard:
        normed_out, refs = refs[0], refs[1:]
    q_out, k_out, v_out, o_ref, aux_ref = refs[:5]
    refs = refs[5:]
    if final:
        part_ref, refs = refs[0], refs[1:]
    buf, weights, values_in, normed, qs, ks, vs, keys, values, sem, in_sem, out_sem = refs[:12]
    n, d = normed.shape
    n_q = qs.shape[0]
    units = n // UNIT
    loads = start_all(block_copies(tables[0], sources[0], buf, s_ref[WIDE], rows, sem.at[0]))
    target = values_in if first_shard else normed
    unit_rows = [slice(u * UNIT, (u + 1) * UNIT) for u in range(units)]
    inputs = start_all(
        [
            pltpu.make_async_copy(x_ref.at[here, :], target.at[here, :], in_sem.at[u])
            for u, here in enumerate(unit_rows)
        ]
    )
    if final:
        other = start_all(
            block_copies(tables[1], sources[1], refs[12], s_ref[WIDE], rows, sem.at[1], refs[12].shape[2])
        )
    wait_all(loads)
    for at in range(3):
        weights[at] = padded(buf[0, :, (at + 1) * share : (at + 2) * share], weights.shape[2])
    outputs = []

    def send(source, to):
        copy = pltpu.make_async_copy(source, to, out_sem.at[len(outputs)])
        copy.start()
        outputs.append(copy)

    ones = [(lane == 64).astype(f32).astype(bf16), (lane == 0).astype(f32).astype(bf16)]
    for u, here in enumerate(unit_rows):
        inputs[u].wait()
        if first_shard:
            x = values_in[here, :].astype(f32)
            scale = lax.rsqrt(jnp.mean(x * x, axis=1, keepdims=True) + epsilon)
            normed[here, :] = (x * scale * gain_ref[...]).astype(bf16)
            send(normed.at[here, :], normed_out.at[here, :])
        rows_in = normed[here, :]
        k = mm(rows_in, weights[1]).astype(bf16)
        v = mm(rows_in, weights[2]).astype(bf16)
        ks[here, :] = k
        vs[here, :] = v
        mask = key_mask(s_ref, u, lane, units).astype(bf16)
        for at, (pair, side) in enumerate(heads):
            lanes = slice(pair * LANES, (pair + 1) * LANES)
            own, rest = (second, first) if side else (first, second)
            keys[at, here, :] = k[:, lanes] * own + mask * rest
            values[at, here, :] = v[:, lanes] * own + ones[side]
    send(ks, k_out)
    send(vs, v_out)
    qs[...] = mm(normed[block_rows(s_ref[X_HALF], n_q, UNIT), :], weights[0]).astype(bf16)
    send(qs, q_out)

    jobs = [(r, at) for r in range(0, n_q, sub) for at in range(len(heads))]
    marks = {
        r: query_mask(s_ref, s_ref[X_HALF] * n_q + r, lane, units) for r in range(0, n_q, sub)
    }

    def scores(job):
        r, at = job
        pair, side = heads[at]
        own, rest = (second, first) if side else (first, second)
        query = qs[r : r + sub, pair * LANES : (pair + 1) * LANES] * own + marks[r].astype(bf16) * rest
        return [lambda c=c: mm(query, keys[at, c : c + chunk, :], NT) for c in range(0, n, chunk)]

    outs, sums = {}, {}
    current = [f() for f in scores(jobs[0])]
    for j, (r, at) in enumerate(jobs):
        ahead = scores(jobs[j + 1]) if j + 1 < len(jobs) else []
        following = []
        top = functools.reduce(jnp.maximum, [jnp.max(s, axis=1, keepdims=True) for s in current])
        mixed = None
        for i, s in enumerate(current):
            if ahead:
                following.append(ahead[i]())
            part = mm(jnp.exp(s - top).astype(bf16), values[at, i * chunk : (i + 1) * chunk, :])
            mixed = part if mixed is None else mixed + part
        pair, side = heads[at]
        row_sum = mixed[:, 0:1] if side else mixed[:, HEAD_DIM : HEAD_DIM + 1]
        outs[side] = mixed / row_sum
        sums[side] = top + jnp.log(row_sum)
        current = following
        if side == 0 and (pair, 1) in heads:
            continue
        here, lanes = slice(r, r + sub), slice(pair * LANES, (pair + 1) * LANES)
        features = jnp.broadcast_to(marks[r], (sub, LANES))
        for which, value in sums.items():
            for i, piece in enumerate(split3(value)):
                features = jnp.where(lane == (units + 1 if which else 64 + units + 1) + i, piece, features)
        aux_ref[here, lanes] = features.astype(bf16)
        right = outs[1] if 1 in outs else 0.0
        o_ref[here, lanes] = jnp.where(lane < HEAD_DIM, outs[0], right).astype(bf16)
        outs, sums = {}, {}
    if final:
        wait_all(other)
        lanes = o_ref.shape[1]
        part = mm(before_ref[...], refs[12][0], NT) + mm(o_ref[...], buf[0, :, :lanes], NT)
        part_ref[...] = part.astype(bf16)
    wait_all(outputs)


def head_forward(scalars, values, gain, weights, rows, share, first_shard, before=None, sub=256, chunk=512):
    n, d = values.shape
    lanes = head_lanes(share)
    heads = share // HEAD_DIM
    tables, sources = [weights[0][0]], [weights[0][1]]
    args = [scalars, values, gain]
    in_specs = [pl.BlockSpec(memory_space=pl.ANY), once((1, d))]
    width = sources[0][0].shape[-1]
    q_shape, k_shape = (n // 2, lanes), (n, lanes)
    shapes = [q_shape, k_shape, k_shape, q_shape, q_shape]
    if first_shard:
        shapes = [(n, d)] + shapes
    out_specs = [pl.BlockSpec(memory_space=pltpu.HBM)] * (len(shapes) - 2) + [once(q_shape)] * 2
    scratch = [
        pltpu.VMEM((1, d, width), bf16),
        pltpu.VMEM((3, d, lanes), bf16),
        pltpu.VMEM((n, d) if first_shard else (16, LANES), bf16),
        pltpu.VMEM((n, d), bf16),
        pltpu.VMEM(q_shape, bf16),
        pltpu.VMEM(k_shape, bf16),
        pltpu.VMEM(k_shape, bf16),
        pltpu.VMEM((heads, n, LANES), bf16),
        pltpu.VMEM((heads, n, LANES), bf16),
        pltpu.SemaphoreType.DMA((2, len(tables[0]))),
        pltpu.SemaphoreType.DMA((n // UNIT,)),
        pltpu.SemaphoreType.DMA((n // UNIT + 3,)),
    ]
    if before is not None:
        tables.append(weights[1][0])
        sources.append(weights[1][1])
        args.append(before)
        in_specs.append(once(before.shape))
        shapes.append((n // 2, d))
        out_specs.append(once((n // 2, d)))
        scratch.append(pltpu.VMEM((1, d, lanes), bf16))
    counts = tuple(len(part) for part in sources)
    for part in sources:
        args += [keep_in_hbm(t) for t in part]
        in_specs += any_specs(part)
    return pl.pallas_call(
        functools.partial(head_kernel, tables, counts, rows, share, first_shard, sub, chunk),
        out_shape=tuple(jax.ShapeDtypeStruct(shape, bf16) for shape in shapes),
        grid_spec=pltpu.PrefetchScalarGridSpec(
            num_scalar_prefetch=1,
            grid=(1,),
            in_specs=in_specs,
            out_specs=out_specs,
            scratch_shapes=scratch,
        ),
        compiler_params=params(HEAD_VMEM),
        cost_estimate=cost(20 * n * n * share // 2, 8 * n * d, n * n * heads),
        name="head_forward",
    )(*args)


def mid_norm(x_ref, a_ref, b_ref):
    attn = a_ref[...].astype(f32) + b_ref[...].astype(f32)
    middle = x_ref[...].astype(f32) + attn
    scale = lax.rsqrt(jnp.mean(middle * middle, axis=1, keepdims=True) + epsilon)
    return attn, middle, scale


def store_quarters(narrow_index, value, keep_ref, send_ref):
    quarter = value.shape[0] // 4
    for block in range(4):
        at = narrow_index ^ block
        here = block_rows(at // 2, quarter, 16)
        piece = value[block * quarter : (block + 1) * quarter, :]

        @pl.when(at % 2 == 0)
        def _():
            keep_ref[here, :] = piece.astype(keep_ref.dtype)

        if send_ref is not None:

            @pl.when(at % 2 == 1)
            def _():
                send_ref[here, :] = piece.astype(send_ref.dtype)


def feed_half(normed, grad, buf, acc, first):
    ff = buf.shape[2] // 3
    w_gate, w_up, w_down = [buf[0, :, at * ff : (at + 1) * ff] for at in range(3)]
    gate = mm(normed, w_gate)
    up = mm(normed, w_up)
    back_hidden = mm(grad, w_down)
    square = gate * gate
    cdf = 0.5 + 0.5 * jnp.tanh(gate * (GELU_C + GELU_C * GELU_A * square))
    act = gate * cdf
    slope = cdf + act * (1.0 - cdf) * (2.0 * GELU_C + 6.0 * GELU_C * GELU_A * square)
    hidden = (act * up).astype(bf16)
    grad_gate = (back_hidden * up * slope).astype(bf16)
    grad_up = (back_hidden * act).astype(bf16)
    normed_t, grad_t = normed.T, grad.T
    for at, (left, right) in enumerate(((normed_t, grad_gate), (normed_t, grad_up), (grad_t, hidden))):
        lanes = slice(at * ff, (at + 1) * ff)
        part = mm(left, right)

        @pl.when(first)
        def _():
            acc[0, :, lanes] = part

        @pl.when(jnp.logical_not(first))
        def _():
            acc[0, :, lanes] += part

    back = mm(grad_gate, w_gate, NT) + mm(grad_up, w_up, NT)
    return back, mm(w_down, hidden, NT)


def feed_own_kernel(
    table, n_src, rows, out_table, n_out, units, s_ref, x_ref, a_ref, b_ref, cot_ref, gain_ref, *refs
):
    sources = refs[:n_src]
    normed_ref, grad_ref, back_ref, mlp_ref, mid_ref, stat_ref = refs[n_src : n_src + 6]
    targets = refs[n_src + 6 : n_src + 6 + n_out]
    buf, acc, stat, sem = refs[n_src + 6 + n_out :]
    i = pl.program_id(0)
    copies = block_copies(table, sources, buf, s_ref[WIDE], rows, sem)

    @pl.when(i == 0)
    def _():
        start_all(copies)
        stat[...] = jnp.zeros_like(stat)

    attn, middle, scale = mid_norm(x_ref, a_ref, b_ref)
    tile, half_rows = x_ref.shape[0], x_ref.shape[0] * pl.num_programs(0)
    live = live_rows(s_ref, s_ref[X_HALF] * half_rows + i * tile, tile, units)
    stat[...] += jnp.sum(jnp.where(live, attn * attn, 0.0), axis=0, keepdims=True)
    normed = (middle * scale * gain_ref[...]).astype(bf16)
    grad = jnp.where(live, cot_ref[...].astype(f32), 0.0).astype(bf16)
    normed_ref[...] = normed
    grad_ref[...] = grad
    store_quarters(s_ref[NARROW], middle.T, mid_ref, None)

    @pl.when(i == 0)
    def _():
        wait_all(copies)

    back, out = feed_half(normed, grad, buf, acc, i == 0)
    back_ref[...] = back.astype(bf16)
    mlp_ref[...] = out.astype(bf16)

    @pl.when(i == pl.num_programs(0) - 1)
    def _():
        stat_ref[...] = jnp.full(stat_ref.shape, jnp.sum(stat[...]))
        store_blocks(out_table, acc, targets, s_ref[WIDE], rows)


def feed_other_kernel(table, n_src, rows, out_table, n_out, s_ref, normed_ref, grad_ref, before_ref, mlp_ref, *refs):
    sources = refs[:n_src]
    back_ref, keep_ref, send_ref = refs[n_src : n_src + 3]
    targets = refs[n_src + 3 : n_src + 3 + n_out]
    buf, acc, sem = refs[n_src + 3 + n_out :]
    i = pl.program_id(0)

    @pl.when(i == 0)
    def _():
        load_blocks(table, sources, buf, s_ref[WIDE], rows, sem)

    back, out = feed_half(normed_ref[...], grad_ref[...], buf, acc, i == 0)
    back_ref[...] = (before_ref[...].astype(f32) + back).astype(bf16)
    store_quarters(s_ref[NARROW], mlp_ref[...].astype(f32) + out, keep_ref, send_ref)

    @pl.when(i == pl.num_programs(0) - 1)
    def _():
        store_blocks(out_table, acc, targets, s_ref[WIDE], rows)


def feed_forward(scalars, inputs, weights, rows, out, own, tile=512):
    table, sources = weights
    out_table, out_leads = out
    n, d = inputs[1].shape
    width = sources[0].shape[-1]
    steps = n // tile
    own_spec = pl.BlockSpec((tile, d), lambda i, s: (s[X_HALF] * steps + i, 0))
    row_spec = pl.BlockSpec((tile, d), lambda i, s: (i, 0))
    full_spec = pl.BlockSpec((d, tile), lambda i, s: (0, i))
    half_spec = pl.BlockSpec((d // 2, tile), lambda i, s: (0, i))
    block_specs = [once((lead, rows, width)) for lead in out_leads]
    block_shapes = tuple(jax.ShapeDtypeStruct((lead, rows, width), bf16) for lead in out_leads)
    scratch = [pltpu.VMEM((1, d, width), bf16), pltpu.VMEM((1, d, width), f32)]
    counts = (table, len(sources), rows, out_table, len(out_leads))
    if own:
        kernel = functools.partial(feed_own_kernel, *counts, 2 * n // UNIT)
        in_specs = [own_spec, row_spec, row_spec, own_spec, once((1, d))]
        out_shape = (
            pltpu.HBM((n, d), bf16),
            pltpu.HBM((n, d), bf16),
            pltpu.HBM((n, d), bf16),
            pltpu.HBM((d, n), bf16),
            jax.ShapeDtypeStruct((d // 2, n), f32),
            jax.ShapeDtypeStruct((1, LANES), f32),
        )
        out_specs = [row_spec, row_spec, row_spec, full_spec, half_spec, once((1, LANES))]
        scratch.append(pltpu.VMEM((1, d), f32))
    else:
        kernel = functools.partial(feed_other_kernel, *counts)
        in_specs = [row_spec, row_spec, row_spec, full_spec]
        out_shape = (
            jax.ShapeDtypeStruct((n, d), bf16),
            jax.ShapeDtypeStruct((d // 2, n), bf16),
            jax.ShapeDtypeStruct((d // 2, n), bf16),
        )
        out_specs = [row_spec, half_spec, half_spec]
    return pl.pallas_call(
        kernel,
        out_shape=out_shape + block_shapes,
        grid_spec=pltpu.PrefetchScalarGridSpec(
            num_scalar_prefetch=1,
            grid=(steps,),
            in_specs=in_specs + any_specs(sources),
            out_specs=out_specs + block_specs,
            scratch_shapes=scratch + [pltpu.SemaphoreType.DMA((len(table),))],
        ),
        compiler_params=params(FEED_VMEM),
        cost_estimate=cost(2 * n * d * width * 3, 10 * n * d, n * width // 3),
        name="feed_forward",
    )(scalars, *[x if own and at == 2 else keep_in_hbm(x) for at, x in enumerate((*inputs, *sources))])


def mid_kernel(
    tables, counts, rows, units, s_ref, x_ref, a_ref, b_ref, g_ref, h_ref, cot_ref, gain_ref, o0_ref, o1_ref, *refs
):
    sources = [refs[: counts[0]], refs[counts[0] : sum(counts)]]
    gm_ref, do0_ref, do1_ref, dwo_ref, gain_out, buf, total, sem = refs[sum(counts) :]
    i = pl.program_id(0)

    @pl.when(i == 0)
    def _():
        for at in range(2):
            load_blocks(
                tables[at], sources[at], buf.at[pl.ds(at, 1)], s_ref[WIDE], rows, sem.at[at], buf.shape[2]
            )
        total[...] = jnp.zeros_like(total)

    _, middle, scale = mid_norm(x_ref, a_ref, b_ref)
    hat = middle * scale
    back = g_ref[...].astype(f32) + h_ref[...].astype(f32)
    tile, half_rows = x_ref.shape[0], x_ref.shape[0] * pl.num_programs(0)
    live = live_rows(s_ref, s_ref[X_HALF] * half_rows + i * tile, tile, units)
    cot = jnp.where(live, cot_ref[...].astype(f32), 0.0)
    total[...] += jnp.sum(back * hat, axis=0, keepdims=True)
    scaled = back * gain_ref[...]
    mean = jnp.mean(scaled * hat, axis=1, keepdims=True)
    grad_mid = cot + scale * (scaled - hat * mean)
    grad = grad_mid.astype(bf16)
    grad_t = grad_mid.T
    gm_ref[...] = grad_t
    grad_t = grad_t.astype(bf16)
    for at, (o_ref, do_ref) in enumerate(((o0_ref, do0_ref), (o1_ref, do1_ref))):
        do_ref[...] = mm(grad, buf[at]).astype(bf16)
        part = mm(grad_t, o_ref[...])

        @pl.when(i == 0)
        def _():
            dwo_ref[at] = part

        @pl.when(i > 0)
        def _():
            dwo_ref[at] += part

    @pl.when(i == pl.num_programs(0) - 1)
    def _():
        gain_out[...] = total[...]


def mid_backward(scalars, patches, a, b, g, h, cot, gain, o, own, other, rows, tile=512):
    n, d = a.shape
    lanes = o[0].shape[1]
    steps = n // tile
    own_spec = pl.BlockSpec((tile, d), lambda i, s: (s[X_HALF] * steps + i, 0))
    row_spec = pl.BlockSpec((tile, d), lambda i, s: (i, 0))
    head_spec = pl.BlockSpec((tile, lanes), lambda i, s: (i, 0))
    return pl.pallas_call(
        functools.partial(
            mid_kernel, (own[0], other[0]), (len(own[1]), len(other[1])), rows, 2 * n // UNIT
        ),
        out_shape=(
            pltpu.HBM((d, n), f32),
            pltpu.HBM((n, lanes), bf16),
            jax.ShapeDtypeStruct((n, lanes), bf16),
            jax.ShapeDtypeStruct((2, d, lanes), f32),
            jax.ShapeDtypeStruct((1, d), f32),
        ),
        grid_spec=pltpu.PrefetchScalarGridSpec(
            num_scalar_prefetch=1,
            grid=(steps,),
            in_specs=[own_spec, row_spec, row_spec, row_spec, row_spec, own_spec]
            + [once((1, d)), head_spec, head_spec]
            + any_specs(own[1])
            + any_specs(other[1]),
            out_specs=[
                pl.BlockSpec((d, tile), lambda i, s: (0, i)),
                head_spec,
                head_spec,
                once((2, d, lanes)),
                once((1, d)),
            ],
            scratch_shapes=[
                pltpu.VMEM((2, d, lanes), bf16),
                pltpu.VMEM((1, d), f32),
                pltpu.SemaphoreType.DMA((2, len(own[0]))),
            ],
        ),
        compiler_params=params(MID_VMEM),
        cost_estimate=cost(8 * n * d * lanes, 16 * n * d),
        name="mid_backward",
    )(scalars, *[keep_in_hbm(t) for t in (patches, a, b)], g, h, keep_in_hbm(cot), gain, *o, *[keep_in_hbm(t) for t in (*own[1], *other[1])])


def head_back_kernel(
    in_table, n_src, table, n_out, rows, share, chunk, s_ref, q_ref, k_ref, v_ref, do_ref, o_ref, aux_ref, dwo_ref, gain_ref, normed_ref, *refs
):
    sources = refs[:n_src]
    dq_out, dk_out, dv_out, gain_out = refs[n_src : n_src + 4]
    targets = refs[n_src + 4 : n_src + 4 + n_out]
    normed, dq_buf, dk_buf, dv_buf, pack, weights, sem, load_sem = refs[n_src + 4 + n_out :]
    heads = head_list(share)
    lane, first, second = lane_halves()
    in_first = lane < HEAD_DIM
    n, n_q = dk_buf.shape[0], dq_buf.shape[0]
    units = n // UNIT
    load = pltpu.make_async_copy(normed_ref, normed, sem.at[0])
    load.start()
    loads = start_all(block_copies(in_table, sources, weights, s_ref[WIDE], rows, load_sem))
    minus = [
        -((lane >= 64) & (lane < 67)).astype(f32).astype(bf16),
        -(lane < 3).astype(f32).astype(bf16),
    ]
    masks = [key_mask(s_ref, u, lane, units).astype(bf16) for u in range(units)]
    for pair in range(q_ref.shape[1] // LANES):
        members = [side for p, side in heads if p == pair]
        lanes = slice(pair * LANES, (pair + 1) * LANES)
        q, aux, do = q_ref[:, lanes], aux_ref[:, lanes], do_ref[:, lanes]
        product = do.astype(f32) * o_ref[:, lanes].astype(f32)
        features = jnp.zeros(q.shape, f32)
        for side in members:
            inside = ~in_first if side else in_first
            row_sum = jnp.sum(jnp.where(inside, product, 0.0), axis=1, keepdims=True)
            for j, value in enumerate(split3(row_sum)):
                features = jnp.where(lane == (j if side else 64 + j), value, features)
        features = features.astype(bf16)
        sides = [(second, first) if side else (first, second) for side in members]
        q_own = [q * own for own, _ in sides]
        do_own = [do * own for own, _ in sides]
        queries = [part + aux * rest for part, (_, rest) in zip(q_own, sides)]
        grads = [part + features * rest for part, (_, rest) in zip(do_own, sides)]
        q_own, do_own = jnp.concatenate(q_own, axis=0), jnp.concatenate(do_own, axis=0)
        dq = None
        for c in range(0, n, chunk):
            k, v = k_ref[c : c + chunk, lanes], v_ref[c : c + chunk, lanes]
            mask = masks[c // UNIT]
            probs, backs, k_own = [], [], []
            for j, side in enumerate(members):
                own, rest = sides[j]
                k_own.append(k * own)
                p = jnp.exp(mm(k_own[j] + mask * rest, queries[j], NT))
                backs.append((p * mm(v * own + minus[side], grads[j], NT)).astype(bf16))
                probs.append(p.astype(bf16))
            part = mm(jnp.concatenate(k_own, axis=0).T, jnp.concatenate(backs, axis=0))
            dq = part if dq is None else dq + part
            dv_buf[c : c + chunk, lanes] = mm(jnp.concatenate(probs, axis=1), do_own).astype(bf16)
            dk_buf[c : c + chunk, lanes] = mm(jnp.concatenate(backs, axis=1), q_own).astype(bf16)
        dq_buf[:, lanes] = dq.T.astype(bf16)
    copies = start_all(
        [
            pltpu.make_async_copy(source, to, sem.at[1 + at])
            for at, (source, to) in enumerate(((dq_buf, dq_out), (dk_buf, dk_out), (dv_buf, dv_out)))
        ]
    )
    load.wait()
    pack[0, :, 0:share] = dwo_ref[0, :, 0:share]
    mine = normed[block_rows(s_ref[X_HALF], n_q, UNIT), :]
    pack[0, :, share : 2 * share] = mm(mine, dq_buf[...], TN)[:, 0:share]
    both = mm(normed[...], jnp.concatenate([dk_buf[...], dv_buf[...]], axis=1), TN)
    pack[0, :, 2 * share : 3 * share] = both[:, 0:share]
    pack[0, :, 3 * share : 4 * share] = both[:, dk_buf.shape[1] : dk_buf.shape[1] + share]
    store_blocks(table, pack, targets, s_ref[WIDE], rows)
    wait_all(loads)
    product = weights[0, :, share : 4 * share].astype(f32) * pack[0, :, share : 4 * share]
    row_sum = jnp.sum(product, axis=1, keepdims=True)
    gain_out[...] = jnp.broadcast_to(row_sum, (row_sum.shape[0], LANES)).T[:1, :] / gain_ref[...]
    wait_all(copies)


def head_backward(
    scalars, q, k, v, do, o, aux, dwo, which, gain, normed, weights, out, rows, share, chunk=512
):
    n, d = normed.shape
    n_q, lanes = q.shape
    out_table, out_leads = out
    shapes = [(n_q, lanes), (n, lanes), (n, lanes)]
    blocks = [(lead, rows, 4 * share) for lead in out_leads]
    q_spec, k_spec = once((n_q, lanes)), once((n, lanes))
    any_spec = pl.BlockSpec(memory_space=pl.ANY)
    return pl.pallas_call(
        functools.partial(
            head_back_kernel, weights[0], len(weights[1]), out_table, len(blocks), rows, share, chunk
        ),
        out_shape=tuple(jax.ShapeDtypeStruct(shape, bf16) for shape in shapes)
        + (jax.ShapeDtypeStruct((1, d), f32),)
        + tuple(jax.ShapeDtypeStruct(shape, bf16) for shape in blocks),
        grid_spec=pltpu.PrefetchScalarGridSpec(
            num_scalar_prefetch=1,
            grid=(1,),
            in_specs=[q_spec, k_spec, k_spec, q_spec, q_spec, q_spec]
            + [
                pl.BlockSpec((1, d, lanes), lambda i, s: (which, 0, 0), pipeline_mode=pl.Buffered(1)),
                once((1, d)),
                any_spec,
            ]
            + any_specs(weights[1]),
            out_specs=[any_spec] * 3 + [once((1, d))] + [once(block) for block in blocks],
            scratch_shapes=[pltpu.VMEM((n, d), bf16)]
            + [pltpu.VMEM(shape, bf16) for shape in shapes]
            + [
                pltpu.VMEM((1, d, 4 * share), f32),
                pltpu.VMEM((1, d, 4 * share), bf16),
                pltpu.SemaphoreType.DMA((4,)),
                pltpu.SemaphoreType.DMA((len(weights[0]),)),
            ],
        ),
        compiler_params=params(BACK_VMEM),
        cost_estimate=cost(20 * n * n * share, 8 * n * d, n * n * share // 128),
        name="head_backward",
    )(scalars, *[keep_in_hbm(t) for t in (q, k, v)], do, o, keep_in_hbm(aux), dwo, gain, *[keep_in_hbm(t) for t in (normed, *weights[1])])


def last_kernel(tables, counts, rows, share, s_ref, x_ref, gain_ref, gm_ref, *refs):
    grads = refs[:6]
    refs = refs[6:]
    sources = [refs[: counts[0]], refs[counts[0] : sum(counts)]]
    keep_ref, send_ref, buf, weights, gain, sem = refs[sum(counts) :]
    i = pl.program_id(0)
    half = pl.num_programs(0) // 2
    d = x_ref.shape[1]

    @pl.when(i == 0)
    def _():
        for at in range(2):
            load_blocks(tables[at], sources[at], buf.at[pl.ds(at, 1)], s_ref[WIDE], rows, sem.at[at])
        for at in range(2):
            for j in range(3):
                weights[3 * at + j] = padded(
                    buf[at, :, (j + 1) * share : (j + 2) * share], weights.shape[2]
                )
        gain[...] = jnp.broadcast_to(gain_ref[...], (LANES, d)).T[:, :1]

    mine = i // half == s_ref[X_HALF]
    x = x_ref[...].T.astype(f32)
    scale = lax.rsqrt(jnp.mean(x * x, axis=0, keepdims=True) + epsilon)
    hat = x * scale
    back = None
    for at in range(2):
        for j in range(3):
            value = grads[3 * at + j][...]
            if j == 0:
                value = jnp.where(mine, value.astype(f32), 0.0).astype(bf16)
            part = mm(weights[3 * at + j], value, NT)
            back = part if back is None else back + part
    scaled = back * gain[...]
    mean = jnp.mean(scaled * hat, axis=0, keepdims=True)
    grad = scale * (scaled - hat * mean) + jnp.where(mine, 0.5, 0.0) * gm_ref[...]
    store_quarters(s_ref[NARROW], grad, keep_ref, send_ref)


def last_backward(scalars, patches, gain, gm_t, grads, own, other, rows, share, tile=512):
    n, d = patches.shape
    width = own[1][0].shape[-1]
    lanes = grads[0].shape[1]
    steps = n // tile
    half = steps // 2
    key_spec = pl.BlockSpec((tile, lanes), lambda i, s: (i, 0))
    own_spec = pl.BlockSpec((tile, lanes), lambda i, s: (own_tile(i, s, half), 0))
    half_spec = pl.BlockSpec((d // 2, tile), lambda i, s: (0, i))
    return pl.pallas_call(
        functools.partial(last_kernel, (own[0], other[0]), (len(own[1]), len(other[1])), rows, share),
        out_shape=(
            jax.ShapeDtypeStruct((d // 2, n), bf16),
            jax.ShapeDtypeStruct((d // 2, n), bf16),
        ),
        grid_spec=pltpu.PrefetchScalarGridSpec(
            num_scalar_prefetch=1,
            grid=(steps,),
            in_specs=[
                pl.BlockSpec((tile, d), lambda i, s: (i, 0)),
                once((1, d)),
                pl.BlockSpec((d, tile), lambda i, s: (0, own_tile(i, s, half))),
            ]
            + [own_spec, key_spec, key_spec] * 2
            + any_specs(own[1])
            + any_specs(other[1]),
            out_specs=[half_spec, half_spec],
            scratch_shapes=[
                pltpu.VMEM((2, d, width), bf16),
                pltpu.VMEM((6, d, lanes), bf16),
                pltpu.VMEM((d, 1), f32),
                pltpu.SemaphoreType.DMA((2, len(own[0]))),
            ],
        ),
        compiler_params=params(LAST_VMEM),
        cost_estimate=cost(2 * n * d * lanes * 5, 10 * n * d),
        name="last_backward",
    )(scalars, patches, gain, gm_t, *grads, *[keep_in_hbm(t) for t in (*own[1], *other[1])])


def swap_core(value):
    return lax.ppermute(value, "narrow", [(i, i ^ 1) for i in range(4)])


def swap_x(value):
    return lax.ppermute(value, "narrow", [(i, i ^ 2) for i in range(4)])


def swap_wide(value, offset):
    n = lax.axis_size("wide")
    return lax.ppermute(value, "wide", [(i, i ^ offset) for i in range(n)])


def after(value, *others):
    return lax.optimization_barrier((value,) + others)[0]


def small_slice():
    return lax.axis_size("wide") == 8


def along_z(first, second, half, flip):
    return [(first, 0, half, flip)] + [(second, z - 1, half, 2 * z + flip) for z in (1, 2, 3)]


OWN_TABLE = along_z(0, 1, 0, 0) + along_z(2, 3, 0, 1)
OTHER_TABLE = along_z(0, 1, 0, 0) + along_z(2, 3, 0, 1)
CORNER = ((2, 0, 1), (3, 0, 3), (3, 1, 5), (4, 0, 7))
FF_TABLE = along_z(0, 1, 0, 0) + [(src, lead, 0, offset) for src, lead, offset in CORNER]
FLAT_TABLE = [(0, r, 0, r) for r in range(8)]
COLUMN_TABLE = [(0, z, 0, 2 * z) for z in range(4)] + [(1, z, 0, 2 * z + 1) for z in range(4)]
FF_COLUMN_TABLE = (
    [(0, z, 0, 2 * z) for z in range(4)]
    + [(1, z, 0, 2 * z + 1) for z in range(2)]
    + [(2, z, 0, 2 * z + 5) for z in range(2)]
)
ACROSS_TABLE = (
    [(0, z, 0, 2 * z) for z in range(2)]
    + [(1, z, 0, 2 * z + 4) for z in range(2)]
    + [(2, z, 0, 2 * z + 1) for z in range(2)]
    + [(3, z, 0, 2 * z + 5) for z in range(2)]
)
WHOLE_TABLE = [(0, 0, 0, 0)]


def gather_whole(shard):
    full = lax.all_gather(shard, "wide", axis=0, tiled=True)[None]
    return full, swap_x(full)


def total(*terms):
    return functools.reduce(jnp.add, [t.astype(f32) for t in terms])


def reduce_whole(part):
    return lax.psum_scatter(part, "wide", scatter_dimension=0, tiled=True).astype(f32)


def body(
    patches,
    norm_gain_attn,
    norm_gain_mlp,
    w_query,
    w_key,
    w_value,
    w_out,
    w_gate,
    w_up,
    w_down,
    cotangent,
    item_slots,
    valid_counts,
):
    rows, d = patches.shape
    share = w_query.shape[1]
    ff = w_gate.shape[1]
    half_rows = rows // 2
    quarter = d // 4
    small = small_slice()
    narrow = lax.axis_index("narrow")
    wide = lax.axis_index("wide")
    x_half = narrow // 2
    scalars = jnp.concatenate(
        [jnp.stack([x_half, wide if small else 0 * wide, narrow]), item_slots, valid_counts]
    ).astype(jnp.int32)
    gain_in, gain_mid = norm_gain_attn[None, :], norm_gain_mlp[None, :]

    def own_units(counts):
        units = half_rows // UNIT
        mine = lax.dynamic_slice_in_dim(counts, x_half * units, units)
        return (mine[:, None] + jnp.zeros((1, UNIT), jnp.int32)).reshape(1, half_rows)

    position = x_half * half_rows + jnp.arange(half_rows, dtype=jnp.int32)[None, :]
    live_own = (position & (own_units(item_slots) - 1)) < own_units(valid_counts)
    live_count = 0.5 * jnp.sum(live_own.astype(f32))

    head_shard = jnp.concatenate([w_out.T, w_query, w_key, w_value], axis=1)[None]
    ff_shard = jnp.concatenate([w_gate, w_up, w_down.T], axis=1)[None]
    if small:
        block = head_shard.shape[1]
        first = [swap_wide(head_shard, 2 * z) for z in (1, 2, 3)]
        first += [swap_wide(head_shard, 1), swap_x(head_shard)]
        ff_early = after(ff_shard, head_shard)
        first += [swap_wide(ff_early, 1), swap_x(ff_early), swap_x(first[3])]
        z1, z2, z4, y0, x0, ff_y0, ff_x0, corner = lax.optimization_barrier(first)
        z3 = jnp.concatenate([z1, z2, z4])
        y3, x3 = swap_wide(z3, 1), swap_x(z3)
        own = (OWN_TABLE, [head_shard, z3, y0, y3])
        other = (OTHER_TABLE, [x0, x3, corner, swap_x(y3)])
        ff_late = after(ff_shard, z3)
        ff_z = [swap_wide(ff_late, 2 * z) for z in (1, 2, 3)]
        early = (y3,)
        own_out = (COLUMN_TABLE, (4, 4))
        other_out = (FLAT_TABLE, (8,))
        ff_out = (FF_COLUMN_TABLE, (4, 2, 2))
        across_out = (ACROSS_TABLE, (2, 2, 2, 2))
    else:
        block = d
        own, other = [(WHOLE_TABLE, [full]) for full in gather_whole(head_shard[0])]
        ff_own_weights, ff_other_weights = [(WHOLE_TABLE, [full]) for full in gather_whole(ff_shard[0])]
        own_out = other_out = ff_out = across_out = (WHOLE_TABLE, (1,))
        early = ()

    values = after(patches, scalars, gain_in, gain_mid, live_own, live_count, *early)
    normed, q0, k0, v0, o0, aux0 = head_forward(scalars, values, gain_in, [own], block, share, True)
    normed = after(normed, o0)
    if small:
        *ff_z, normed = lax.optimization_barrier((*ff_z, normed))
        ff_z3 = jnp.concatenate(ff_z)
        ff_z3, normed = lax.optimization_barrier((ff_z3, normed))
        ff_y3, ff_x3 = swap_wide(ff_z3, 1), swap_x(ff_z3)
        ff_own_weights = (OWN_TABLE, [ff_shard, ff_z3, ff_y0, ff_y3])
    q1, k1, v1, o1, aux1, attn_part = head_forward(
        scalars, normed, gain_in, [other, own], block, share, False, before=o0
    )
    if small:
        ff_y3, ff_x3, ff_x0, attn_part = lax.optimization_barrier((ff_y3, ff_x3, ff_x0, attn_part))
        ff_own_weights[1][3] = ff_y3
        corner = [swap_wide(ff_x0, 1), swap_x(ff_y3[:2]), swap_wide(ff_x3[2:], 1)]
        ff_other_weights = (FF_TABLE, [ff_x0, ff_x3, *corner])
    attn_other = swap_core(attn_part)
    normed_mid, grad_mlp, back_own, mlp_own, mid_keep, attn_square, *ff_own_grads = feed_forward(
        scalars, (values, attn_part, attn_other, cotangent, gain_mid), ff_own_weights, block, ff_out, True
    )
    back_part, mlp_keep, mlp_send, *ff_other_grads = feed_forward(
        scalars, (normed_mid, grad_mlp, back_own, mlp_own), ff_other_weights, block, across_out, False
    )
    back_other = swap_core(back_part)
    if small:
        column, to_y, early_y = ff_own_grads
        early_x, to_x, corner_x, corner_y = ff_other_grads
        got_early_y = swap_wide(early_y, 1)
        got_x, got_y = swap_x(corner_x), swap_wide(corner_y, 1)
        got_early_x = swap_x(after(early_x, back_other))
    gm_t, do0, do1, dwo, gain_mid_sum = mid_backward(
        scalars, values, attn_part, attn_other, back_part, back_other, cotangent, gain_mid,
        (o0, o1), own, other, block,
    )
    if small:
        got_x, got_y, to_x, to_y = lax.optimization_barrier((got_x, got_y, to_x, to_y, do1))[:4]
        to_y, to_x = total(to_y, got_x).astype(bf16), total(to_x, got_y).astype(bf16)
        got_y, got_x = swap_wide(to_y, 1), swap_x(to_x)
        do1 = after(do1, to_y, to_x)
    *grads1, gain1, head1 = head_backward(
        scalars, q1, k1, v1, do1, o1, aux1, dwo, 1, gain_in, normed, other, other_out, block, share
    )

    mlp = total(mlp_keep, after(swap_core(after(mlp_send, do1)), head1))
    layer = jnp.where(live_own, mid_keep + mlp, 0.0)
    layer16 = layer.astype(bf16)
    mlp_square = jnp.sum(jnp.where(live_own, mlp * mlp, 0.0))
    layer_square = jnp.sum(layer * layer)
    stats = jnp.stack([mlp_square, layer_square, live_count])[None]
    stats = jnp.concatenate(
        [0.5 * gain_mid_sum, 0.5 * attn_square[:, :1], jnp.pad(stats, ((0, 0), (0, LANES - 4)))],
        axis=1,
    )

    head1_other = swap_x(head1)
    layer_mine, layer_sent = layer16[:quarter], layer16[quarter:]
    do0, stats, layer_mine, layer_sent = lax.optimization_barrier(
        (do0, stats, layer_mine, layer_sent, head1)
    )[:4]
    layer_got = swap_x(layer_sent)
    if small:
        got_x, got_y, got_early_x, got_early_y = lax.optimization_barrier(
            (got_x, got_y, got_early_x, got_early_y, head1)
        )[:4]
        column = total(
            column, jnp.concatenate([got_y, got_early_y]), jnp.concatenate([got_early_x, got_x])
        )
        sent = [column[z].astype(bf16) for z in (1, 2, 3)]
        do0 = after(do0, *sent)
        back = [swap_wide(sent[z - 1], 2 * z) for z in (1, 2, 3)]
    *grads0, gain0, head0, head0_y = head_backward(
        scalars, q0, k0, v0, do0, o0, aux0, dwo, 0, gain_in, normed, own, own_out, block, share
    ) + (() if small else (None,))
    dq0, head1_other = lax.optimization_barrier((grads0[0], head1_other))
    if small:
        head_y = total(head0_y, head1_other[1::2]).astype(bf16)
        dq0, head_y, *back = lax.optimization_barrier((dq0, head_y, *back))
        head_y = swap_wide(head_y, 1)
    sums = jnp.concatenate([gain0 + gain1, stats], axis=1)
    if small:
        sums = sums + swap_core(sums)
        dq0, sums = lax.optimization_barrier((dq0, sums))
        sums_x = swap_x(sums)
    grad_keep, grad_send = last_backward(
        scalars, values, gain_in, gm_t, [dq0, *grads0[1:], *grads1], own, other, block, share
    )

    if small:
        grad_keep, grad_send, sums_x, head_y, layer_got = lax.optimization_barrier(
            (grad_keep, grad_send, sums_x, head_y, layer_got)
        )
        sums = sums + sums_x
        ff_own = total(column[0], *back)
    output = jnp.where(
        x_half == 0,
        jnp.concatenate([layer_mine, layer_got], axis=1),
        jnp.concatenate([layer_got, layer_mine], axis=1),
    )
    grad_got = swap_core(grad_send)
    grad_sent = total(grad_keep[quarter:], grad_got[quarter:]).astype(bf16)
    if small:
        sums = sums + swap_wide(sums, 1)
        head_column = total(head0, head1_other[::2], head_y)
        head_sent = [head_column[z].astype(bf16) for z in (1, 2, 3)]
        grad_sent, sums, *head_sent, output, ff_own = lax.optimization_barrier(
            (grad_sent, sums, *head_sent, output, ff_own)
        )
        grad_other = swap_x(grad_sent)
        head_got = [swap_wide(head_sent[z - 1], 2 * z) for z in (1, 2, 3)]
        sums_got = [swap_wide(sums, 2 * z) for z in (1, 2, 3)]
        grad_other, *got = lax.optimization_barrier((grad_other, *head_got, *sums_got))
        head_own = total(head_column[0], *got[:3])
        sums = total(sums, *got[3:])
    else:
        both = total(ff_own_grads[0][0], swap_x(ff_other_grads[0][0])).astype(bf16)
        ff_own = reduce_whole(both)
        head_own = reduce_whole(total(head0[0], head1_other[0]).astype(bf16))
        grad_other = swap_x(grad_sent)
        sums = lax.psum(sums, ("wide", "narrow"))
    grad_patches = total(grad_keep[:quarter], grad_got[:quarter], grad_other)
    sums = sums[0]
    total_in, total_mid, totals = sums[:d], sums[d : 2 * d], sums[2 * d : 2 * d + 4]
    rms_values = jnp.sqrt(totals[:3] / (totals[3] * d))
    return (
        output.T,
        grad_patches.T,
        total_in,
        total_mid,
        head_own[:, share : 2 * share],
        head_own[:, 2 * share : 3 * share],
        head_own[:, 3 * share :],
        head_own[:, :share].T,
        ff_own[:, :ff],
        ff_own[:, ff : 2 * ff],
        ff_own[:, 2 * ff :].T,
        rms_values,
    )


def solution(mesh):
    return jax.shard_map(
        body,
        mesh=mesh,
        in_specs=(
            P("wide", None),
            P(),
            P(),
            P("wide", "narrow"),
            P("wide", "narrow"),
            P("wide", "narrow"),
            P("narrow", "wide"),
            P("wide", "narrow"),
            P("wide", "narrow"),
            P("narrow", "wide"),
            P("wide", None),
            P("wide"),
            P("wide"),
        ),
        out_specs=(
            P("wide", "narrow"),
            P("wide", "narrow"),
            P(),
            P(),
            P("wide", "narrow"),
            P("wide", "narrow"),
            P("wide", "narrow"),
            P("narrow", "wide"),
            P("wide", "narrow"),
            P("wide", "narrow"),
            P("narrow", "wide"),
            P(),
        ),
        check_vma=False,
    )
```

```python
import functools

import jax
import jax.numpy as jnp
from jax import lax
from jax.experimental import pallas as pl
from jax.experimental.pallas import tpu as pltpu
from jax.sharding import PartitionSpec as P

f32 = jnp.float32
bf16 = jnp.bfloat16
HEAD_DIM = 64
UNIT = 512
LANES = 128
epsilon = 1e-06
BIG = 1e30
GELU_C = 0.7978845608028654
GELU_A = 0.044715
HEAD_VMEM, FEED_VMEM, MID_VMEM, BACK_VMEM, LAST_VMEM = 24, 40, 26, 36, 26

NT = (((1,), (1,)), ((), ()))
NN = (((1,), (0,)), ((), ()))
TN = (((0,), (0,)), ((), ()))


def mm(a, b, dims=NN):
    return lax.dot_general(a, b, dims, preferred_element_type=f32)


def split3(v):
    high = v.astype(bf16)
    rest = v - high.astype(f32)
    middle = rest.astype(bf16)
    low = (rest - middle.astype(f32)).astype(bf16)
    return high.astype(f32), middle.astype(f32), low.astype(f32)


def lane_halves():
    lane = lax.broadcasted_iota(jnp.int32, (1, LANES), 1)
    first = (lane < HEAD_DIM).astype(f32)
    return lane, first.astype(bf16), (1.0 - first).astype(bf16)


def block_rows(index, rows, step):
    return pl.ds(pl.multiple_of(index * rows, step), rows)


def block_copies(table, sources, target, wide_index, rows, sem, columns=None):
    step = 16 if rows % 16 == 0 else 8
    copies = []
    for k, (src, lead, half, offset) in enumerate(table):
        source = sources[src].at[lead]
        if columns is not None:
            source = source.at[:, pl.ds(0, columns)]
        copies.append(
            pltpu.make_async_copy(
                source, target.at[half, block_rows(wide_index ^ offset, rows, step), :], sem.at[k]
            )
        )
    return copies


def start_all(copies):
    for copy in copies:
        copy.start()
    return copies


def wait_all(copies):
    for copy in copies:
        copy.wait()


def load_blocks(*args):
    wait_all(start_all(block_copies(*args)))


def store_blocks(table, acc, targets, wide_index, rows):
    for src, lead, half, offset in table:
        targets[src][lead] = acc[half, block_rows(wide_index ^ offset, rows, 8), :].astype(bf16)


def padded(weights, width):
    return jnp.concatenate(
        [weights, jnp.zeros((weights.shape[0], width - weights.shape[1]), weights.dtype)], axis=1
    )


X_HALF, WIDE, NARROW, ITEMS = 0, 1, 2, 3


def unit_item(s_ref, unit, units):
    start = (unit * UNIT) & -s_ref[ITEMS + unit]
    return start, s_ref[ITEMS + units + unit]


def live_rows(s_ref, first, tile, units):
    start, valid = unit_item(s_ref, first // UNIT, units)
    return first - start + lax.broadcasted_iota(jnp.int32, (tile, 1), 0) < valid


def query_mask(s_ref, first, lane, units):
    start, _ = unit_item(s_ref, first // UNIT, units)
    column = lane & (HEAD_DIM - 1)
    named = (column < units) & (column != start // UNIT)
    return jnp.where(named | (column == units), 1.0, 0.0)


def key_mask(s_ref, unit, lane, units):
    start, valid = unit_item(s_ref, unit, units)
    column = lane & (HEAD_DIM - 1)
    row = unit * UNIT - start + lax.broadcasted_iota(jnp.int32, (UNIT, 1), 0)
    fixed = jnp.where(column == start // UNIT, -BIG, 0.0)
    fixed = jnp.where((column > units) & (column < units + 4), -1.0, fixed)
    return jnp.where((column == units) & (row >= valid), -BIG, fixed)


def any_specs(arrays):
    return [pl.BlockSpec(memory_space=pltpu.HBM)] * len(arrays)


def own_tile(i, s, half):
    return jnp.clip(i - s[0] * half, 0, half - 1)


def keep_in_hbm(value):
    return pltpu.with_memory_space_constraint(value, pltpu.HBM)


def params(mebibytes):
    return pltpu.CompilerParams(vmem_limit_bytes=mebibytes << 20)


def cost(flops, moved, exps=0):
    return pl.CostEstimate(flops=flops, bytes_accessed=moved, transcendentals=exps)


def once(shape):
    return pl.BlockSpec(shape, lambda *_: (0,) * len(shape), pipeline_mode=pl.Buffered(1))


def head_list(share):
    return [(h // 2, h % 2) for h in range(share // HEAD_DIM)]


def head_lanes(share):
    return -(-share // LANES) * LANES


def head_kernel(
    tables, counts, rows, share, first_shard, sub, chunk, s_ref, x_ref, gain_ref, *refs
):
    heads = head_list(share)
    lane, first, second = lane_halves()
    final = len(tables) == 2
    if final:
        before_ref, refs = refs[0], refs[1:]
    sources = [refs[: counts[0]], refs[counts[0] : sum(counts)]]
    refs = refs[sum(counts) :]
    if first_shard:
        normed_out, refs = refs[0], refs[1:]
    q_out, k_out, v_out, o_ref, aux_ref = refs[:5]
    refs = refs[5:]
    if final:
        part_ref, refs = refs[0], refs[1:]
    buf, weights, values_in, normed, qs, ks, vs, keys, values, sem, in_sem, out_sem = refs[:12]
    n, d = normed.shape
    n_q = qs.shape[0]
    units = n // UNIT
    loads = start_all(block_copies(tables[0], sources[0], buf, s_ref[WIDE], rows, sem.at[0]))
    target = values_in if first_shard else normed
    unit_rows = [slice(u * UNIT, (u + 1) * UNIT) for u in range(units)]
    inputs = start_all(
        [
            pltpu.make_async_copy(x_ref.at[here, :], target.at[here, :], in_sem.at[u])
            for u, here in enumerate(unit_rows)
        ]
    )
    if final:
        other = start_all(
            block_copies(tables[1], sources[1], refs[12], s_ref[WIDE], rows, sem.at[1], refs[12].shape[2])
        )
    wait_all(loads)
    for at in range(3):
        weights[at] = padded(buf[0, :, (at + 1) * share : (at + 2) * share], weights.shape[2])
    outputs = []

    def send(source, to):
        copy = pltpu.make_async_copy(source, to, out_sem.at[len(outputs)])
        copy.start()
        outputs.append(copy)

    ones = [(lane == 64).astype(f32).astype(bf16), (lane == 0).astype(f32).astype(bf16)]
    for u, here in enumerate(unit_rows):
        inputs[u].wait()
        if first_shard:
            x = values_in[here, :].astype(f32)
            scale = lax.rsqrt(jnp.mean(x * x, axis=1, keepdims=True) + epsilon)
            normed[here, :] = (x * scale * gain_ref[...]).astype(bf16)
            send(normed.at[here, :], normed_out.at[here, :])
        rows_in = normed[here, :]
        k = mm(rows_in, weights[1]).astype(bf16)
        v = mm(rows_in, weights[2]).astype(bf16)
        ks[here, :] = k
        vs[here, :] = v
        mask = key_mask(s_ref, u, lane, units).astype(bf16)
        for at, (pair, side) in enumerate(heads):
            lanes = slice(pair * LANES, (pair + 1) * LANES)
            own, rest = (second, first) if side else (first, second)
            keys[at, here, :] = k[:, lanes] * own + mask * rest
            values[at, here, :] = v[:, lanes] * own + ones[side]
    send(ks, k_out)
    send(vs, v_out)
    qs[...] = mm(normed[block_rows(s_ref[X_HALF], n_q, UNIT), :], weights[0]).astype(bf16)
    send(qs, q_out)

    jobs = [(r, at) for r in range(0, n_q, sub) for at in range(len(heads))]
    marks = {
        r: query_mask(s_ref, s_ref[X_HALF] * n_q + r, lane, units) for r in range(0, n_q, sub)
    }

    def scores(job):
        r, at = job
        pair, side = heads[at]
        own, rest = (second, first) if side else (first, second)
        query = qs[r : r + sub, pair * LANES : (pair + 1) * LANES] * own + marks[r].astype(bf16) * rest
        return [lambda c=c: mm(query, keys[at, c : c + chunk, :], NT) for c in range(0, n, chunk)]

    outs, sums = {}, {}
    current = [f() for f in scores(jobs[0])]
    for j, (r, at) in enumerate(jobs):
        ahead = scores(jobs[j + 1]) if j + 1 < len(jobs) else []
        following = []
        top = functools.reduce(jnp.maximum, [jnp.max(s, axis=1, keepdims=True) for s in current])
        mixed = None
        for i, s in enumerate(current):
            if ahead:
                following.append(ahead[i]())
            part = mm(jnp.exp(s - top).astype(bf16), values[at, i * chunk : (i + 1) * chunk, :])
            mixed = part if mixed is None else mixed + part
        pair, side = heads[at]
        row_sum = mixed[:, 0:1] if side else mixed[:, HEAD_DIM : HEAD_DIM + 1]
        outs[side] = mixed / row_sum
        sums[side] = top + jnp.log(row_sum)
        current = following
        if side == 0 and (pair, 1) in heads:
            continue
        here, lanes = slice(r, r + sub), slice(pair * LANES, (pair + 1) * LANES)
        features = jnp.broadcast_to(marks[r], (sub, LANES))
        for which, value in sums.items():
            for i, piece in enumerate(split3(value)):
                features = jnp.where(lane == (units + 1 if which else 64 + units + 1) + i, piece, features)
        aux_ref[here, lanes] = features.astype(bf16)
        right = outs[1] if 1 in outs else 0.0
        o_ref[here, lanes] = jnp.where(lane < HEAD_DIM, outs[0], right).astype(bf16)
        outs, sums = {}, {}
    if final:
        wait_all(other)
        lanes = o_ref.shape[1]
        part = mm(before_ref[...], refs[12][0], NT) + mm(o_ref[...], buf[0, :, :lanes], NT)
        part_ref[...] = part.astype(bf16)
    wait_all(outputs)


def head_forward(scalars, values, gain, weights, rows, share, first_shard, before=None, sub=256, chunk=512):
    n, d = values.shape
    lanes = head_lanes(share)
    heads = share // HEAD_DIM
    tables, sources = [weights[0][0]], [weights[0][1]]
    args = [scalars, values, gain]
    in_specs = [pl.BlockSpec(memory_space=pl.ANY), once((1, d))]
    width = sources[0][0].shape[-1]
    q_shape, k_shape = (n // 2, lanes), (n, lanes)
    shapes = [q_shape, k_shape, k_shape, q_shape, q_shape]
    if first_shard:
        shapes = [(n, d)] + shapes
    out_specs = [pl.BlockSpec(memory_space=pltpu.HBM)] * (len(shapes) - 2) + [once(q_shape)] * 2
    scratch = [
        pltpu.VMEM((1, d, width), bf16),
        pltpu.VMEM((3, d, lanes), bf16),
        pltpu.VMEM((n, d) if first_shard else (16, LANES), bf16),
        pltpu.VMEM((n, d), bf16),
        pltpu.VMEM(q_shape, bf16),
        pltpu.VMEM(k_shape, bf16),
        pltpu.VMEM(k_shape, bf16),
        pltpu.VMEM((heads, n, LANES), bf16),
        pltpu.VMEM((heads, n, LANES), bf16),
        pltpu.SemaphoreType.DMA((2, len(tables[0]))),
        pltpu.SemaphoreType.DMA((n // UNIT,)),
        pltpu.SemaphoreType.DMA((n // UNIT + 3,)),
    ]
    if before is not None:
        tables.append(weights[1][0])
        sources.append(weights[1][1])
        args.append(before)
        in_specs.append(once(before.shape))
        shapes.append((n // 2, d))
        out_specs.append(once((n // 2, d)))
        scratch.append(pltpu.VMEM((1, d, lanes), bf16))
    counts = tuple(len(part) for part in sources)
    for part in sources:
        args += [keep_in_hbm(t) for t in part]
        in_specs += any_specs(part)
    return pl.pallas_call(
        functools.partial(head_kernel, tables, counts, rows, share, first_shard, sub, chunk),
        out_shape=tuple(jax.ShapeDtypeStruct(shape, bf16) for shape in shapes),
        grid_spec=pltpu.PrefetchScalarGridSpec(
            num_scalar_prefetch=1,
            grid=(1,),
            in_specs=in_specs,
            out_specs=out_specs,
            scratch_shapes=scratch,
        ),
        compiler_params=params(HEAD_VMEM),
        cost_estimate=cost(20 * n * n * share // 2, 8 * n * d, n * n * heads),
        name="head_forward",
    )(*args)


def mid_norm(x_ref, a_ref, b_ref):
    attn = a_ref[...].astype(f32) + b_ref[...].astype(f32)
    middle = x_ref[...].astype(f32) + attn
    scale = lax.rsqrt(jnp.mean(middle * middle, axis=1, keepdims=True) + epsilon)
    return attn, middle, scale


def store_quarters(narrow_index, value, keep_ref, send_ref):
    quarter = value.shape[0] // 4
    for block in range(4):
        at = narrow_index ^ block
        here = block_rows(at // 2, quarter, 16)
        piece = value[block * quarter : (block + 1) * quarter, :]

        @pl.when(at % 2 == 0)
        def _():
            keep_ref[here, :] = piece.astype(keep_ref.dtype)

        if send_ref is not None:

            @pl.when(at % 2 == 1)
            def _():
                send_ref[here, :] = piece.astype(send_ref.dtype)


def feed_half(normed, grad, buf, acc, first):
    ff = buf.shape[2] // 3
    w_gate, w_up, w_down = [buf[0, :, at * ff : (at + 1) * ff] for at in range(3)]
    gate = mm(normed, w_gate)
    up = mm(normed, w_up)
    back_hidden = mm(grad, w_down)
    square = gate * gate
    cdf = 0.5 + 0.5 * jnp.tanh(gate * (GELU_C + GELU_C * GELU_A * square))
    act = gate * cdf
    slope = cdf + act * (1.0 - cdf) * (2.0 * GELU_C + 6.0 * GELU_C * GELU_A * square)
    hidden = (act * up).astype(bf16)
    grad_gate = (back_hidden * up * slope).astype(bf16)
    grad_up = (back_hidden * act).astype(bf16)
    normed_t, grad_t = normed.T, grad.T
    for at, (left, right) in enumerate(((normed_t, grad_gate), (normed_t, grad_up), (grad_t, hidden))):
        lanes = slice(at * ff, (at + 1) * ff)
        part = mm(left, right)

        @pl.when(first)
        def _():
            acc[0, :, lanes] = part

        @pl.when(jnp.logical_not(first))
        def _():
            acc[0, :, lanes] += part

    back = mm(grad_gate, w_gate, NT) + mm(grad_up, w_up, NT)
    return back, mm(w_down, hidden, NT)


def feed_own_kernel(
    table, n_src, rows, out_table, n_out, units, s_ref, x_ref, a_ref, b_ref, cot_ref, gain_ref, *refs
):
    sources = refs[:n_src]
    normed_ref, grad_ref, back_ref, mlp_ref, mid_ref, stat_ref = refs[n_src : n_src + 6]
    targets = refs[n_src + 6 : n_src + 6 + n_out]
    buf, acc, stat, sem = refs[n_src + 6 + n_out :]
    i = pl.program_id(0)
    copies = block_copies(table, sources, buf, s_ref[WIDE], rows, sem)

    @pl.when(i == 0)
    def _():
        start_all(copies)
        stat[...] = jnp.zeros_like(stat)

    attn, middle, scale = mid_norm(x_ref, a_ref, b_ref)
    tile, half_rows = x_ref.shape[0], x_ref.shape[0] * pl.num_programs(0)
    live = live_rows(s_ref, s_ref[X_HALF] * half_rows + i * tile, tile, units)
    stat[...] += jnp.sum(jnp.where(live, attn * attn, 0.0), axis=0, keepdims=True)
    normed = (middle * scale * gain_ref[...]).astype(bf16)
    grad = jnp.where(live, cot_ref[...].astype(f32), 0.0).astype(bf16)
    normed_ref[...] = normed
    grad_ref[...] = grad
    store_quarters(s_ref[NARROW], middle.T, mid_ref, None)

    @pl.when(i == 0)
    def _():
        wait_all(copies)

    back, out = feed_half(normed, grad, buf, acc, i == 0)
    back_ref[...] = back.astype(bf16)
    mlp_ref[...] = out.astype(bf16)

    @pl.when(i == pl.num_programs(0) - 1)
    def _():
        stat_ref[...] = jnp.full(stat_ref.shape, jnp.sum(stat[...]))
        store_blocks(out_table, acc, targets, s_ref[WIDE], rows)


def feed_other_kernel(table, n_src, rows, out_table, n_out, s_ref, normed_ref, grad_ref, before_ref, mlp_ref, *refs):
    sources = refs[:n_src]
    back_ref, keep_ref, send_ref = refs[n_src : n_src + 3]
    targets = refs[n_src + 3 : n_src + 3 + n_out]
    buf, acc, sem = refs[n_src + 3 + n_out :]
    i = pl.program_id(0)

    @pl.when(i == 0)
    def _():
        load_blocks(table, sources, buf, s_ref[WIDE], rows, sem)

    back, out = feed_half(normed_ref[...], grad_ref[...], buf, acc, i == 0)
    back_ref[...] = (before_ref[...].astype(f32) + back).astype(bf16)
    store_quarters(s_ref[NARROW], mlp_ref[...].astype(f32) + out, keep_ref, send_ref)

    @pl.when(i == pl.num_programs(0) - 1)
    def _():
        store_blocks(out_table, acc, targets, s_ref[WIDE], rows)


def feed_forward(scalars, inputs, weights, rows, out, own, tile=512):
    table, sources = weights
    out_table, out_leads = out
    n, d = inputs[1].shape
    width = sources[0].shape[-1]
    steps = n // tile
    own_spec = pl.BlockSpec((tile, d), lambda i, s: (s[X_HALF] * steps + i, 0))
    row_spec = pl.BlockSpec((tile, d), lambda i, s: (i, 0))
    full_spec = pl.BlockSpec((d, tile), lambda i, s: (0, i))
    half_spec = pl.BlockSpec((d // 2, tile), lambda i, s: (0, i))
    block_specs = [once((lead, rows, width)) for lead in out_leads]
    block_shapes = tuple(jax.ShapeDtypeStruct((lead, rows, width), bf16) for lead in out_leads)
    scratch = [pltpu.VMEM((1, d, width), bf16), pltpu.VMEM((1, d, width), f32)]
    counts = (table, len(sources), rows, out_table, len(out_leads))
    if own:
        kernel = functools.partial(feed_own_kernel, *counts, 2 * n // UNIT)
        in_specs = [own_spec, row_spec, row_spec, own_spec, once((1, d))]
        out_shape = (
            pltpu.HBM((n, d), bf16),
            pltpu.HBM((n, d), bf16),
            pltpu.HBM((n, d), bf16),
            pltpu.HBM((d, n), bf16),
            jax.ShapeDtypeStruct((d // 2, n), f32),
            jax.ShapeDtypeStruct((1, LANES), f32),
        )
        out_specs = [row_spec, row_spec, row_spec, full_spec, half_spec, once((1, LANES))]
        scratch.append(pltpu.VMEM((1, d), f32))
    else:
        kernel = functools.partial(feed_other_kernel, *counts)
        in_specs = [row_spec, row_spec, row_spec, full_spec]
        out_shape = (
            jax.ShapeDtypeStruct((n, d), bf16),
            jax.ShapeDtypeStruct((d // 2, n), bf16),
            jax.ShapeDtypeStruct((d // 2, n), bf16),
        )
        out_specs = [row_spec, half_spec, half_spec]
    return pl.pallas_call(
        kernel,
        out_shape=out_shape + block_shapes,
        grid_spec=pltpu.PrefetchScalarGridSpec(
            num_scalar_prefetch=1,
            grid=(steps,),
            in_specs=in_specs + any_specs(sources),
            out_specs=out_specs + block_specs,
            scratch_shapes=scratch + [pltpu.SemaphoreType.DMA((len(table),))],
        ),
        compiler_params=params(FEED_VMEM),
        cost_estimate=cost(2 * n * d * width * 3, 10 * n * d, n * width // 3),
        name="feed_forward",
    )(scalars, *[x if own and at == 2 else keep_in_hbm(x) for at, x in enumerate((*inputs, *sources))])


def mid_kernel(
    tables, counts, rows, units, s_ref, x_ref, a_ref, b_ref, g_ref, h_ref, cot_ref, gain_ref, o0_ref, o1_ref, *refs
):
    sources = [refs[: counts[0]], refs[counts[0] : sum(counts)]]
    gm_ref, do0_ref, do1_ref, dwo_ref, gain_out, buf, total, sem = refs[sum(counts) :]
    i = pl.program_id(0)

    @pl.when(i == 0)
    def _():
        for at in range(2):
            load_blocks(
                tables[at], sources[at], buf.at[pl.ds(at, 1)], s_ref[WIDE], rows, sem.at[at], buf.shape[2]
            )
        total[...] = jnp.zeros_like(total)

    _, middle, scale = mid_norm(x_ref, a_ref, b_ref)
    hat = middle * scale
    back = g_ref[...].astype(f32) + h_ref[...].astype(f32)
    tile, half_rows = x_ref.shape[0], x_ref.shape[0] * pl.num_programs(0)
    live = live_rows(s_ref, s_ref[X_HALF] * half_rows + i * tile, tile, units)
    cot = jnp.where(live, cot_ref[...].astype(f32), 0.0)
    total[...] += jnp.sum(back * hat, axis=0, keepdims=True)
    scaled = back * gain_ref[...]
    mean = jnp.mean(scaled * hat, axis=1, keepdims=True)
    grad_mid = cot + scale * (scaled - hat * mean)
    grad = grad_mid.astype(bf16)
    grad_t = grad_mid.T
    gm_ref[...] = grad_t
    grad_t = grad_t.astype(bf16)
    for at, (o_ref, do_ref) in enumerate(((o0_ref, do0_ref), (o1_ref, do1_ref))):
        do_ref[...] = mm(grad, buf[at]).astype(bf16)
        part = mm(grad_t, o_ref[...])

        @pl.when(i == 0)
        def _():
            dwo_ref[at] = part

        @pl.when(i > 0)
        def _():
            dwo_ref[at] += part

    @pl.when(i == pl.num_programs(0) - 1)
    def _():
        gain_out[...] = total[...]


def mid_backward(scalars, patches, a, b, g, h, cot, gain, o, own, other, rows, tile=512):
    n, d = a.shape
    lanes = o[0].shape[1]
    steps = n // tile
    own_spec = pl.BlockSpec((tile, d), lambda i, s: (s[X_HALF] * steps + i, 0))
    row_spec = pl.BlockSpec((tile, d), lambda i, s: (i, 0))
    head_spec = pl.BlockSpec((tile, lanes), lambda i, s: (i, 0))
    return pl.pallas_call(
        functools.partial(
            mid_kernel, (own[0], other[0]), (len(own[1]), len(other[1])), rows, 2 * n // UNIT
        ),
        out_shape=(
            pltpu.HBM((d, n), f32),
            pltpu.HBM((n, lanes), bf16),
            jax.ShapeDtypeStruct((n, lanes), bf16),
            jax.ShapeDtypeStruct((2, d, lanes), f32),
            jax.ShapeDtypeStruct((1, d), f32),
        ),
        grid_spec=pltpu.PrefetchScalarGridSpec(
            num_scalar_prefetch=1,
            grid=(steps,),
            in_specs=[own_spec, row_spec, row_spec, row_spec, row_spec, own_spec]
            + [once((1, d)), head_spec, head_spec]
            + any_specs(own[1])
            + any_specs(other[1]),
            out_specs=[
                pl.BlockSpec((d, tile), lambda i, s: (0, i)),
                head_spec,
                head_spec,
                once((2, d, lanes)),
                once((1, d)),
            ],
            scratch_shapes=[
                pltpu.VMEM((2, d, lanes), bf16),
                pltpu.VMEM((1, d), f32),
                pltpu.SemaphoreType.DMA((2, len(own[0]))),
            ],
        ),
        compiler_params=params(MID_VMEM),
        cost_estimate=cost(8 * n * d * lanes, 16 * n * d),
        name="mid_backward",
    )(scalars, *[keep_in_hbm(t) for t in (patches, a, b)], g, h, keep_in_hbm(cot), gain, *o, *[keep_in_hbm(t) for t in (*own[1], *other[1])])


def head_back_kernel(
    in_table, n_src, table, n_out, rows, share, chunk, s_ref, q_ref, k_ref, v_ref, do_ref, o_ref, aux_ref, dwo_ref, gain_ref, normed_ref, *refs
):
    sources = refs[:n_src]
    dq_out, dk_out, dv_out, gain_out = refs[n_src : n_src + 4]
    targets = refs[n_src + 4 : n_src + 4 + n_out]
    normed, dq_buf, dk_buf, dv_buf, pack, weights, sem, load_sem = refs[n_src + 4 + n_out :]
    heads = head_list(share)
    lane, first, second = lane_halves()
    in_first = lane < HEAD_DIM
    n, n_q = dk_buf.shape[0], dq_buf.shape[0]
    units = n // UNIT
    load = pltpu.make_async_copy(normed_ref, normed, sem.at[0])
    load.start()
    loads = start_all(block_copies(in_table, sources, weights, s_ref[WIDE], rows, load_sem))
    minus = [
        -((lane >= 64) & (lane < 67)).astype(f32).astype(bf16),
        -(lane < 3).astype(f32).astype(bf16),
    ]
    masks = [key_mask(s_ref, u, lane, units).astype(bf16) for u in range(units)]
    for pair in range(q_ref.shape[1] // LANES):
        members = [side for p, side in heads if p == pair]
        lanes = slice(pair * LANES, (pair + 1) * LANES)
        q, aux, do = q_ref[:, lanes], aux_ref[:, lanes], do_ref[:, lanes]
        product = do.astype(f32) * o_ref[:, lanes].astype(f32)
        features = jnp.zeros(q.shape, f32)
        for side in members:
            inside = ~in_first if side else in_first
            row_sum = jnp.sum(jnp.where(inside, product, 0.0), axis=1, keepdims=True)
            for j, value in enumerate(split3(row_sum)):
                features = jnp.where(lane == (j if side else 64 + j), value, features)
        features = features.astype(bf16)
        sides = [(second, first) if side else (first, second) for side in members]
        q_own = [q * own for own, _ in sides]
        do_own = [do * own for own, _ in sides]
        queries = [part + aux * rest for part, (_, rest) in zip(q_own, sides)]
        grads = [part + features * rest for part, (_, rest) in zip(do_own, sides)]
        q_own, do_own = jnp.concatenate(q_own, axis=0), jnp.concatenate(do_own, axis=0)
        dq = None
        for c in range(0, n, chunk):
            k, v = k_ref[c : c + chunk, lanes], v_ref[c : c + chunk, lanes]
            mask = masks[c // UNIT]
            probs, backs, k_own = [], [], []
            for j, side in enumerate(members):
                own, rest = sides[j]
                k_own.append(k * own)
                p = jnp.exp(mm(k_own[j] + mask * rest, queries[j], NT))
                backs.append((p * mm(v * own + minus[side], grads[j], NT)).astype(bf16))
                probs.append(p.astype(bf16))
            part = mm(jnp.concatenate(k_own, axis=0).T, jnp.concatenate(backs, axis=0))
            dq = part if dq is None else dq + part
            dv_buf[c : c + chunk, lanes] = mm(jnp.concatenate(probs, axis=1), do_own).astype(bf16)
            dk_buf[c : c + chunk, lanes] = mm(jnp.concatenate(backs, axis=1), q_own).astype(bf16)
        dq_buf[:, lanes] = dq.T.astype(bf16)
    copies = start_all(
        [
            pltpu.make_async_copy(source, to, sem.at[1 + at])
            for at, (source, to) in enumerate(((dq_buf, dq_out), (dk_buf, dk_out), (dv_buf, dv_out)))
        ]
    )
    load.wait()
    pack[0, :, 0:share] = dwo_ref[0, :, 0:share]
    mine = normed[block_rows(s_ref[X_HALF], n_q, UNIT), :]
    pack[0, :, share : 2 * share] = mm(mine, dq_buf[...], TN)[:, 0:share]
    both = mm(normed[...], jnp.concatenate([dk_buf[...], dv_buf[...]], axis=1), TN)
    pack[0, :, 2 * share : 3 * share] = both[:, 0:share]
    pack[0, :, 3 * share : 4 * share] = both[:, dk_buf.shape[1] : dk_buf.shape[1] + share]
    store_blocks(table, pack, targets, s_ref[WIDE], rows)
    wait_all(loads)
    product = weights[0, :, share : 4 * share].astype(f32) * pack[0, :, share : 4 * share]
    row_sum = jnp.sum(product, axis=1, keepdims=True)
    gain_out[...] = jnp.broadcast_to(row_sum, (row_sum.shape[0], LANES)).T[:1, :] / gain_ref[...]
    wait_all(copies)


def head_backward(
    scalars, q, k, v, do, o, aux, dwo, which, gain, normed, weights, out, rows, share, chunk=512
):
    n, d = normed.shape
    n_q, lanes = q.shape
    out_table, out_leads = out
    shapes = [(n_q, lanes), (n, lanes), (n, lanes)]
    blocks = [(lead, rows, 4 * share) for lead in out_leads]
    q_spec, k_spec = once((n_q, lanes)), once((n, lanes))
    any_spec = pl.BlockSpec(memory_space=pl.ANY)
    return pl.pallas_call(
        functools.partial(
            head_back_kernel, weights[0], len(weights[1]), out_table, len(blocks), rows, share, chunk
        ),
        out_shape=tuple(jax.ShapeDtypeStruct(shape, bf16) for shape in shapes)
        + (jax.ShapeDtypeStruct((1, d), f32),)
        + tuple(jax.ShapeDtypeStruct(shape, bf16) for shape in blocks),
        grid_spec=pltpu.PrefetchScalarGridSpec(
            num_scalar_prefetch=1,
            grid=(1,),
            in_specs=[q_spec, k_spec, k_spec, q_spec, q_spec, q_spec]
            + [
                pl.BlockSpec((1, d, lanes), lambda i, s: (which, 0, 0), pipeline_mode=pl.Buffered(1)),
                once((1, d)),
                any_spec,
            ]
            + any_specs(weights[1]),
            out_specs=[any_spec] * 3 + [once((1, d))] + [once(block) for block in blocks],
            scratch_shapes=[pltpu.VMEM((n, d), bf16)]
            + [pltpu.VMEM(shape, bf16) for shape in shapes]
            + [
                pltpu.VMEM((1, d, 4 * share), f32),
                pltpu.VMEM((1, d, 4 * share), bf16),
                pltpu.SemaphoreType.DMA((4,)),
                pltpu.SemaphoreType.DMA((len(weights[0]),)),
            ],
        ),
        compiler_params=params(BACK_VMEM),
        cost_estimate=cost(20 * n * n * share, 8 * n * d, n * n * share // 128),
        name="head_backward",
    )(scalars, *[keep_in_hbm(t) for t in (q, k, v)], do, o, keep_in_hbm(aux), dwo, gain, *[keep_in_hbm(t) for t in (normed, *weights[1])])


def last_kernel(tables, counts, rows, share, s_ref, x_ref, gain_ref, gm_ref, *refs):
    grads = refs[:6]
    refs = refs[6:]
    sources = [refs[: counts[0]], refs[counts[0] : sum(counts)]]
    keep_ref, send_ref, buf, weights, gain, sem = refs[sum(counts) :]
    i = pl.program_id(0)
    half = pl.num_programs(0) // 2
    d = x_ref.shape[1]

    @pl.when(i == 0)
    def _():
        for at in range(2):
            load_blocks(tables[at], sources[at], buf.at[pl.ds(at, 1)], s_ref[WIDE], rows, sem.at[at])
        for at in range(2):
            for j in range(3):
                weights[3 * at + j] = padded(
                    buf[at, :, (j + 1) * share : (j + 2) * share], weights.shape[2]
                )
        gain[...] = jnp.broadcast_to(gain_ref[...], (LANES, d)).T[:, :1]

    mine = i // half == s_ref[X_HALF]
    x = x_ref[...].T.astype(f32)
    scale = lax.rsqrt(jnp.mean(x * x, axis=0, keepdims=True) + epsilon)
    hat = x * scale
    back = None
    for at in range(2):
        for j in range(3):
            value = grads[3 * at + j][...]
            if j == 0:
                value = jnp.where(mine, value.astype(f32), 0.0).astype(bf16)
            part = mm(weights[3 * at + j], value, NT)
            back = part if back is None else back + part
    scaled = back * gain[...]
    mean = jnp.mean(scaled * hat, axis=0, keepdims=True)
    grad = scale * (scaled - hat * mean) + jnp.where(mine, 0.5, 0.0) * gm_ref[...]
    store_quarters(s_ref[NARROW], grad, keep_ref, send_ref)


def last_backward(scalars, patches, gain, gm_t, grads, own, other, rows, share, tile=512):
    n, d = patches.shape
    width = own[1][0].shape[-1]
    lanes = grads[0].shape[1]
    steps = n // tile
    half = steps // 2
    key_spec = pl.BlockSpec((tile, lanes), lambda i, s: (i, 0))
    own_spec = pl.BlockSpec((tile, lanes), lambda i, s: (own_tile(i, s, half), 0))
    half_spec = pl.BlockSpec((d // 2, tile), lambda i, s: (0, i))
    return pl.pallas_call(
        functools.partial(last_kernel, (own[0], other[0]), (len(own[1]), len(other[1])), rows, share),
        out_shape=(
            jax.ShapeDtypeStruct((d // 2, n), bf16),
            jax.ShapeDtypeStruct((d // 2, n), bf16),
        ),
        grid_spec=pltpu.PrefetchScalarGridSpec(
            num_scalar_prefetch=1,
            grid=(steps,),
            in_specs=[
                pl.BlockSpec((tile, d), lambda i, s: (i, 0)),
                once((1, d)),
                pl.BlockSpec((d, tile), lambda i, s: (0, own_tile(i, s, half))),
            ]
            + [own_spec, key_spec, key_spec] * 2
            + any_specs(own[1])
            + any_specs(other[1]),
            out_specs=[half_spec, half_spec],
            scratch_shapes=[
                pltpu.VMEM((2, d, width), bf16),
                pltpu.VMEM((6, d, lanes), bf16),
                pltpu.VMEM((d, 1), f32),
                pltpu.SemaphoreType.DMA((2, len(own[0]))),
            ],
        ),
        compiler_params=params(LAST_VMEM),
        cost_estimate=cost(2 * n * d * lanes * 5, 10 * n * d),
        name="last_backward",
    )(scalars, patches, gain, gm_t, *grads, *[keep_in_hbm(t) for t in (*own[1], *other[1])])


def swap_core(value):
    return lax.ppermute(value, "narrow", [(i, i ^ 1) for i in range(4)])


def swap_x(value):
    return lax.ppermute(value, "narrow", [(i, i ^ 2) for i in range(4)])


def swap_wide(value, offset):
    n = lax.axis_size("wide")
    return lax.ppermute(value, "wide", [(i, i ^ offset) for i in range(n)])


def after(value, *others):
    return lax.optimization_barrier((value,) + others)[0]


def small_slice():
    return lax.axis_size("wide") == 8


def along_z(first, second, half, flip):
    return [(first, 0, half, flip)] + [(second, z - 1, half, 2 * z + flip) for z in (1, 2, 3)]


OWN_TABLE = along_z(0, 1, 0, 0) + along_z(2, 3, 0, 1)
OTHER_TABLE = along_z(0, 1, 0, 0) + along_z(2, 3, 0, 1)
CORNER = ((2, 0, 1), (3, 0, 3), (3, 1, 5), (4, 0, 7))
FF_TABLE = along_z(0, 1, 0, 0) + [(src, lead, 0, offset) for src, lead, offset in CORNER]
FLAT_TABLE = [(0, r, 0, r) for r in range(8)]
COLUMN_TABLE = [(0, z, 0, 2 * z) for z in range(4)] + [(1, z, 0, 2 * z + 1) for z in range(4)]
FF_COLUMN_TABLE = (
    [(0, z, 0, 2 * z) for z in range(4)]
    + [(1, z, 0, 2 * z + 1) for z in range(2)]
    + [(2, z, 0, 2 * z + 5) for z in range(2)]
)
ACROSS_TABLE = (
    [(0, z, 0, 2 * z) for z in range(2)]
    + [(1, z, 0, 2 * z + 4) for z in range(2)]
    + [(2, z, 0, 2 * z + 1) for z in range(2)]
    + [(3, z, 0, 2 * z + 5) for z in range(2)]
)
WHOLE_TABLE = [(0, 0, 0, 0)]


def gather_whole(shard):
    full = lax.all_gather(shard, "wide", axis=0, tiled=True)[None]
    return full, swap_x(full)


def total(*terms):
    return functools.reduce(jnp.add, [t.astype(f32) for t in terms])


def reduce_whole(part):
    return lax.psum_scatter(part, "wide", scatter_dimension=0, tiled=True).astype(f32)


def body(
    patches,
    norm_gain_attn,
    norm_gain_mlp,
    w_query,
    w_key,
    w_value,
    w_out,
    w_gate,
    w_up,
    w_down,
    cotangent,
    item_slots,
    valid_counts,
):
    rows, d = patches.shape
    share = w_query.shape[1]
    ff = w_gate.shape[1]
    half_rows = rows // 2
    quarter = d // 4
    small = small_slice()
    narrow = lax.axis_index("narrow")
    wide = lax.axis_index("wide")
    x_half = narrow // 2
    scalars = jnp.concatenate(
        [jnp.stack([x_half, wide if small else 0 * wide, narrow]), item_slots, valid_counts]
    ).astype(jnp.int32)
    gain_in, gain_mid = norm_gain_attn[None, :], norm_gain_mlp[None, :]

    def own_units(counts):
        units = half_rows // UNIT
        mine = lax.dynamic_slice_in_dim(counts, x_half * units, units)
        return (mine[:, None] + jnp.zeros((1, UNIT), jnp.int32)).reshape(1, half_rows)

    position = x_half * half_rows + jnp.arange(half_rows, dtype=jnp.int32)[None, :]
    live_own = (position & (own_units(item_slots) - 1)) < own_units(valid_counts)
    live_count = 0.5 * jnp.sum(live_own.astype(f32))

    head_shard = jnp.concatenate([w_out.T, w_query, w_key, w_value], axis=1)[None]
    ff_shard = jnp.concatenate([w_gate, w_up, w_down.T], axis=1)[None]
    if small:
        block = head_shard.shape[1]
        first = [swap_wide(head_shard, 2 * z) for z in (1, 2, 3)]
        first += [swap_wide(head_shard, 1), swap_x(head_shard)]
        ff_early = after(ff_shard, head_shard)
        first += [swap_wide(ff_early, 1), swap_x(ff_early), swap_x(first[3])]
        z1, z2, z4, y0, x0, ff_y0, ff_x0, corner = lax.optimization_barrier(first)
        z3 = jnp.concatenate([z1, z2, z4])
        y3, x3 = swap_wide(z3, 1), swap_x(z3)
        own = (OWN_TABLE, [head_shard, z3, y0, y3])
        other = (OTHER_TABLE, [x0, x3, corner, swap_x(y3)])
        ff_late = after(ff_shard, z3)
        ff_z = [swap_wide(ff_late, 2 * z) for z in (1, 2, 3)]
        early = (y3,)
        own_out = (COLUMN_TABLE, (4, 4))
        other_out = (FLAT_TABLE, (8,))
        ff_out = (FF_COLUMN_TABLE, (4, 2, 2))
        across_out = (ACROSS_TABLE, (2, 2, 2, 2))
    else:
        block = d
        own, other = [(WHOLE_TABLE, [full]) for full in gather_whole(head_shard[0])]
        ff_own_weights, ff_other_weights = [(WHOLE_TABLE, [full]) for full in gather_whole(ff_shard[0])]
        own_out = other_out = ff_out = across_out = (WHOLE_TABLE, (1,))
        early = ()

    values = after(patches, scalars, gain_in, gain_mid, live_own, live_count, *early)
    normed, q0, k0, v0, o0, aux0 = head_forward(scalars, values, gain_in, [own], block, share, True)
    normed = after(normed, o0)
    if small:
        *ff_z, normed = lax.optimization_barrier((*ff_z, normed))
        ff_z3 = jnp.concatenate(ff_z)
        ff_z3, normed = lax.optimization_barrier((ff_z3, normed))
        ff_y3, ff_x3 = swap_wide(ff_z3, 1), swap_x(ff_z3)
        ff_own_weights = (OWN_TABLE, [ff_shard, ff_z3, ff_y0, ff_y3])
    q1, k1, v1, o1, aux1, attn_part = head_forward(
        scalars, normed, gain_in, [other, own], block, share, False, before=o0
    )
    if small:
        ff_y3, ff_x3, ff_x0, attn_part = lax.optimization_barrier((ff_y3, ff_x3, ff_x0, attn_part))
        ff_own_weights[1][3] = ff_y3
        corner = [swap_wide(ff_x0, 1), swap_x(ff_y3[:2]), swap_wide(ff_x3[2:], 1)]
        ff_other_weights = (FF_TABLE, [ff_x0, ff_x3, *corner])
    attn_other = swap_core(attn_part)
    normed_mid, grad_mlp, back_own, mlp_own, mid_keep, attn_square, *ff_own_grads = feed_forward(
        scalars, (values, attn_part, attn_other, cotangent, gain_mid), ff_own_weights, block, ff_out, True
    )
    back_part, mlp_keep, mlp_send, *ff_other_grads = feed_forward(
        scalars, (normed_mid, grad_mlp, back_own, mlp_own), ff_other_weights, block, across_out, False
    )
    back_other = swap_core(back_part)
    if small:
        column, to_y, early_y = ff_own_grads
        early_x, to_x, corner_x, corner_y = ff_other_grads
        got_early_y = swap_wide(early_y, 1)
        got_x, got_y = swap_x(corner_x), swap_wide(corner_y, 1)
        got_early_x = swap_x(after(early_x, back_other))
    gm_t, do0, do1, dwo, gain_mid_sum = mid_backward(
        scalars, values, attn_part, attn_other, back_part, back_other, cotangent, gain_mid,
        (o0, o1), own, other, block,
    )
    if small:
        got_x, got_y, to_x, to_y = lax.optimization_barrier((got_x, got_y, to_x, to_y, do1))[:4]
        to_y, to_x = total(to_y, got_x).astype(bf16), total(to_x, got_y).astype(bf16)
        got_y, got_x = swap_wide(to_y, 1), swap_x(to_x)
        do1 = after(do1, to_y, to_x)
    *grads1, gain1, head1 = head_backward(
        scalars, q1, k1, v1, do1, o1, aux1, dwo, 1, gain_in, normed, other, other_out, block, share
    )

    mlp = total(mlp_keep, after(swap_core(after(mlp_send, do1)), head1))
    layer = jnp.where(live_own, mid_keep + mlp, 0.0)
    layer16 = layer.astype(bf16)
    mlp_square = jnp.sum(jnp.where(live_own, mlp * mlp, 0.0))
    layer_square = jnp.sum(layer * layer)
    stats = jnp.stack([mlp_square, layer_square, live_count])[None]
    stats = jnp.concatenate(
        [0.5 * gain_mid_sum, 0.5 * attn_square[:, :1], jnp.pad(stats, ((0, 0), (0, LANES - 4)))],
        axis=1,
    )

    head1_other = swap_x(head1)
    layer_mine, layer_sent = layer16[:quarter], layer16[quarter:]
    do0, stats, layer_mine, layer_sent = lax.optimization_barrier(
        (do0, stats, layer_mine, layer_sent, head1)
    )[:4]
    layer_got = swap_x(layer_sent)
    if small:
        got_x, got_y, got_early_x, got_early_y = lax.optimization_barrier(
            (got_x, got_y, got_early_x, got_early_y, head1)
        )[:4]
        column = total(
            column, jnp.concatenate([got_y, got_early_y]), jnp.concatenate([got_early_x, got_x])
        )
        sent = [column[z].astype(bf16) for z in (1, 2, 3)]
        do0 = after(do0, *sent)
        back = [swap_wide(sent[z - 1], 2 * z) for z in (1, 2, 3)]
    *grads0, gain0, head0, head0_y = head_backward(
        scalars, q0, k0, v0, do0, o0, aux0, dwo, 0, gain_in, normed, own, own_out, block, share
    ) + (() if small else (None,))
    dq0, head1_other = lax.optimization_barrier((grads0[0], head1_other))
    if small:
        head_y = total(head0_y, head1_other[1::2]).astype(bf16)
        dq0, head_y, *back = lax.optimization_barrier((dq0, head_y, *back))
        head_y = swap_wide(head_y, 1)
    sums = jnp.concatenate([gain0 + gain1, stats], axis=1)
    if small:
        sums = sums + swap_core(sums)
        dq0, sums = lax.optimization_barrier((dq0, sums))
        sums_x = swap_x(sums)
    grad_keep, grad_send = last_backward(
        scalars, values, gain_in, gm_t, [dq0, *grads0[1:], *grads1], own, other, block, share
    )

    if small:
        grad_keep, grad_send, sums_x, head_y, layer_got = lax.optimization_barrier(
            (grad_keep, grad_send, sums_x, head_y, layer_got)
        )
        sums = sums + sums_x
        ff_own = total(column[0], *back)
    output = jnp.where(
        x_half == 0,
        jnp.concatenate([layer_mine, layer_got], axis=1),
        jnp.concatenate([layer_got, layer_mine], axis=1),
    )
    grad_got = swap_core(grad_send)
    grad_sent = total(grad_keep[quarter:], grad_got[quarter:]).astype(bf16)
    if small:
        sums = sums + swap_wide(sums, 1)
        head_column = total(head0, head1_other[::2], head_y)
        head_sent = [head_column[z].astype(bf16) for z in (1, 2, 3)]
        grad_sent, sums, *head_sent, output, ff_own = lax.optimization_barrier(
            (grad_sent, sums, *head_sent, output, ff_own)
        )
        grad_other = swap_x(grad_sent)
        head_got = [swap_wide(head_sent[z - 1], 2 * z) for z in (1, 2, 3)]
        sums_got = [swap_wide(sums, 2 * z) for z in (1, 2, 3)]
        grad_other, *got = lax.optimization_barrier((grad_other, *head_got, *sums_got))
        head_own = total(head_column[0], *got[:3])
        sums = total(sums, *got[3:])
    else:
        both = total(ff_own_grads[0][0], swap_x(ff_other_grads[0][0])).astype(bf16)
        ff_own = reduce_whole(both)
        head_own = reduce_whole(total(head0[0], head1_other[0]).astype(bf16))
        grad_other = swap_x(grad_sent)
        sums = lax.psum(sums, ("wide", "narrow"))
    grad_patches = total(grad_keep[:quarter], grad_got[:quarter], grad_other)
    sums = sums[0]
    total_in, total_mid, totals = sums[:d], sums[d : 2 * d], sums[2 * d : 2 * d + 4]
    rms_values = jnp.sqrt(totals[:3] / (totals[3] * d))
    return (
        output.T,
        grad_patches.T,
        total_in,
        total_mid,
        head_own[:, share : 2 * share],
        head_own[:, 2 * share : 3 * share],
        head_own[:, 3 * share :],
        head_own[:, :share].T,
        ff_own[:, :ff],
        ff_own[:, ff : 2 * ff],
        ff_own[:, 2 * ff :].T,
        rms_values,
    )


def solution(mesh):
    return jax.shard_map(
        body,
        mesh=mesh,
        in_specs=(
            P("wide", None),
            P(),
            P(),
            P("wide", "narrow"),
            P("wide", "narrow"),
            P("wide", "narrow"),
            P("narrow", "wide"),
            P("wide", "narrow"),
            P("wide", "narrow"),
            P("narrow", "wide"),
            P("wide", None),
            P("wide"),
            P("wide"),
        ),
        out_specs=(
            P("wide", "narrow"),
            P("wide", "narrow"),
            P(),
            P(),
            P("wide", "narrow"),
            P("wide", "narrow"),
            P("wide", "narrow"),
            P("narrow", "wide"),
            P("wide", "narrow"),
            P("wide", "narrow"),
            P("narrow", "wide"),
            P(),
        ),
        check_vma=False,
    )
```
